32 devices in a mesh: dp: 16 (over z, y, x), rep: 2 (over core).
Axes of the slice: x: 2, y: 2, z: 4, core: 2. Of those that a mesh axis runs over, the one named last changes fastest.
Arguments:
- hidden_old: bfloat16 [8192, 6144], P(('dp', 'rep')), may hold values from -400 to 400
- cotangent: bfloat16 [8192, 128], P(('dp', 'rep')), may hold values from -0.15625 to 0.15625
- gain_old: float32 [6144], replicated, may hold values from 0.1 to 1.9
- old_bounds: int32 [17], replicated, may hold values from 0 to 6144, as said below
- new_bounds: int32 [17], replicated, may hold values from 0 to 8192, as said below
- source_map: int32 [8192], replicated, may hold values from 0 to 6143, as said below
- weight_old: bfloat16 [8192, 128], P('dp'), may hold values from -0.078125 to 0.078125
- moment_first: float32 [8192, 128], P('dp'), may hold values from -6 to 6
- moment_second: float32 [8192, 128], P('dp'), may hold values from 0.25 to 4
Outputs:
- projected: bfloat16 [8192, 128], P(('dp', 'rep'))
- gain_grad: float32 [8192], replicated
- first_next: float32 [10240, 128], P('dp')
- second_next: float32 [10240, 128], P('dp')
- adam_step: float32 [10240, 128], P('dp')
The draws below stay inside these ranges and needn't reach their ends.
Inputs may be any that keep to these rules, and one draw needn't show every extreme that they name: old_bounds[0] = 0, old_bounds[16] = 6144; device p holds old units old_bounds[p] to old_bounds[p+1] - 1, between 256 and 512 of them, exactly 512 on some device. new_bounds[0] = 0, new_bounds[16] = 8192; device q holds new units new_bounds[q] to new_bounds[q+1] - 1, between 384 and 640 of them, exactly 640 on some device. `source_map`: the s-th new unit of a device (counted from its first) copies an old unit held by old device (s + c) mod 16, with an offset c of that new device; so at most 40 new units of one device copy units of one old device, and some pair of devices reaches 40.
All inputs are finite; a program needn't handle non-finite values.
Results may differ from the reference program's by a relative error of at most 0.0049.
Values may be sent and summed in bfloat16 or wider, within the bound.
No kernel may reach another device: no remote copies, remote signals or barrier semaphores. Data moves between devices by JAX's collectives and lax.ppermute only.
A program may use at most 64 MiB of HBM per device.

```python
import math
import jax
import jax.numpy as jnp
from jax import lax

D_OLD = 6144
D_NEW = 8192
HEAD = 128
TOK_DEV = 256
TOKENS = 8192
CAPO = 512
CAPN = 640
BOUNDS = 17
N_DP = 16


def counted_bounds(seed_key, mean_count, spread_max, devices):
    key_one, key_two = jax.random.split(seed_key)
    raised = jax.random.randint(key_one, (devices,), 0, spread_max + 1)
    chosen = jax.random.randint(key_two, (), 0, devices)
    indices = jnp.arange(devices, dtype=jnp.int32)
    raised = jnp.where(indices == chosen, spread_max, raised)
    raised = jnp.where(indices == (chosen + 1) % devices, 0, raised)
    counts = mean_count + raised - jnp.roll(raised, -1)
    return jnp.concatenate([jnp.zeros((1,), jnp.int32), jnp.cumsum(counts).astype(jnp.int32)])


def old_layout(key):
    devices = BOUNDS - 1
    return counted_bounds(jax.random.fold_in(key, 11), D_OLD // devices, D_OLD // devices // 3, devices)


def new_layout(key):
    devices = BOUNDS - 1
    return counted_bounds(jax.random.fold_in(key, 12), D_NEW // devices, D_NEW // devices // 4, devices)


def draw_old_bounds(key, part):
    return old_layout(key)


def draw_new_bounds(key, part):
    return new_layout(key)


def draw_source_map(key, part):
    devices = BOUNDS - 1
    old_edges = old_layout(key)
    new_edges = new_layout(key)
    positions = jnp.arange(D_NEW, dtype=jnp.int32)
    holder = jnp.sum((new_edges[None, 1:] <= positions[:, None]).astype(jnp.int32), axis=1)
    within = positions - new_edges[holder]
    offsets = jax.random.randint(jax.random.fold_in(key, 13), (devices,), 0, devices)
    source_dev = (within + offsets[holder]) % devices
    old_counts = old_edges[1:] - old_edges[:-1]
    picked = jax.random.randint(jax.random.fold_in(key, 14), (D_NEW,), 0, old_counts[source_dev])
    return (old_edges[source_dev] + picked).astype(jnp.int32)


def draw_hidden_old(key, part):
    key_one, key_two, key_three = jax.random.split(key, 3)
    base = jax.random.truncated_normal(key_one, -4.0, 4.0, (TOKENS, D_OLD), jnp.float32)
    top = jnp.log(10.0)
    row_scale = jnp.exp(jax.random.uniform(key_two, (TOKENS, 1), jnp.float32, 0.0, 1.0) * top)
    col_scale = jnp.exp(jax.random.uniform(key_three, (1, D_OLD), jnp.float32, 0.0, 1.0) * top)
    return (base * row_scale * col_scale).astype(jnp.bfloat16)


def block_scale(own_key, extent, shards, smallest, top_value):
    def one(axis_at, parts):
        steps = jax.random.uniform(jax.random.fold_in(jax.random.fold_in(own_key, 6), axis_at), (parts,), jnp.float32, smallest / len(shards), top_value / len(shards))
        return jnp.repeat(jnp.exp(steps), extent[axis_at] // parts).reshape((-1,) + (1,) * (len(extent) - axis_at - 1))

    gain = one(*shards[0])
    for cut in shards[1:]:
        gain = gain * one(*cut)
    return gain


def centred(rng, dims, deviation, most, cuts=(), kind=jnp.bfloat16):
    array = deviation * jax.random.normal(rng, dims, jnp.float32)
    if cuts:
        array = array * block_scale(rng, dims, cuts, -0.22, 0.18)
    return jnp.clip(array, -most, most).astype(kind)


def setup_inputs(seed: int = 0) -> dict:
    splits = jax.random.split(jax.random.key(seed), 10)
    hidden_old = draw_hidden_old(jax.random.fold_in(splits[9], 71), 0)
    cotangent = centred(splits[1], (TOKENS, HEAD), (TOKENS ** -0.5), 0.15625, ((0, 32),))
    gain_old = jnp.clip(1.0 + 0.18 * jax.random.normal(splits[2], (D_OLD,), jnp.float32), 0.1, 1.9)
    old_bounds = draw_old_bounds(jax.random.fold_in(splits[9], 71), 0)
    new_bounds = draw_new_bounds(jax.random.fold_in(splits[9], 71), 0)
    source_map = draw_source_map(jax.random.fold_in(splits[9], 71), 0)
    weight_old = centred(splits[6], (N_DP * CAPO, HEAD), D_OLD ** -0.5, 0.078125, ((0, 16),))
    moment_first = centred(splits[7], (N_DP * CAPO, HEAD), 1.0, 6.0, ((0, 16),), jnp.float32)
    moment_second = jnp.clip(jnp.exp(math.log(4.0) - 2.7725887 * jax.random.uniform(splits[8], (N_DP * CAPO, HEAD), jnp.float32) ** block_scale(splits[8], (N_DP * CAPO, HEAD), ((0, 16),), -0.2, 0.2)), 0.25, 4.0)
    return dict(hidden_old=hidden_old, cotangent=cotangent, gain_old=gain_old, old_bounds=old_bounds, new_bounds=new_bounds, source_map=source_map, weight_old=weight_old, moment_first=moment_first, moment_second=moment_second)


def dense_rows(padded, bounds, unit_count, capacity):
    unit_ids = jnp.arange(unit_count, dtype=jnp.int32)
    holder = lax.optimization_barrier(jnp.sum((bounds[None, 1:] <= unit_ids[:, None]).astype(jnp.int32), axis=1))
    return padded[holder * capacity + unit_ids - bounds[holder]]

def reference(hidden_old, cotangent, gain_old, old_bounds, new_bounds, source_map, weight_old, moment_first, moment_second):
    positions = jnp.arange(D_NEW, dtype=jnp.int32)
    first_use = jnp.full((D_OLD,), D_NEW, jnp.int32).at[source_map].min(positions)
    keep_mask = first_use[source_map] == positions
    weight_dense = dense_rows(weight_old, old_bounds, D_OLD, CAPO)
    weight_wide = jnp.where(keep_mask[:, None], weight_dense[source_map], jnp.zeros((), jnp.bfloat16))
    gain_wide = gain_old[source_map]
    token_blocks = hidden_old.reshape(TOKENS // TOK_DEV, TOK_DEV, D_OLD)
    cot_blocks = cotangent.reshape(TOKENS // TOK_DEV, TOK_DEV, HEAD)

    def token_block(totals, pieces):
        grad_sum, gain_sum = totals
        stream, cot_rows = pieces
        wide = stream[:, source_map].astype(jnp.float32)
        inv_rms = lax.rsqrt(lax.optimization_barrier(jnp.mean(wide * wide, axis=1)) + 1e-05)
        scaled = wide * inv_rms[:, None]
        normed = (scaled * gain_wide).astype(jnp.bfloat16)
        block_keys = jnp.dot(normed, weight_wide, preferred_element_type=jnp.float32).astype(jnp.bfloat16)
        grad_sum = grad_sum + jnp.dot(normed.T, cot_rows, preferred_element_type=jnp.float32)
        slopes = jnp.dot(cot_rows, weight_wide.T, preferred_element_type=jnp.float32)
        gain_sum = gain_sum + lax.optimization_barrier(jnp.sum(slopes * scaled, axis=0))
        return ((grad_sum, gain_sum), block_keys)
    starting = (jnp.zeros((D_NEW, HEAD), jnp.float32), jnp.zeros((D_NEW,), jnp.float32))
    (grad_wide, gain_grad), key_blocks = lax.scan(token_block, starting, (token_blocks, cot_blocks))
    projected = key_blocks.reshape(TOKENS, HEAD)
    first_wide = 0.9 * dense_rows(moment_first, old_bounds, D_OLD, CAPO)[source_map] + 0.1 * grad_wide
    second_wide = 0.95 * dense_rows(moment_second, old_bounds, D_OLD, CAPO)[source_map] + 0.05 * grad_wide * grad_wide
    holder = lax.optimization_barrier(jnp.sum((new_bounds[None, 1:] <= positions[:, None]).astype(jnp.int32), axis=1))
    slots = holder * CAPN + positions - new_bounds[holder]
    first_next = jnp.zeros((N_DP * CAPN, HEAD), jnp.float32).at[slots].set(first_wide)
    second_next = jnp.zeros((N_DP * CAPN, HEAD), jnp.float32).at[slots].set(second_wide)
    adam_step = first_next / (jnp.sqrt(second_next) + 1e-08)
    return (projected, gain_grad, first_next, second_next, adam_step)
```

```python
import jax
import jax.numpy as jnp
from jax import lax
from jax.experimental import pallas as pl
from jax.experimental.pallas import tpu as pltpu
from jax.sharding import PartitionSpec as P

D_OLD = 6144
D_NEW = 8192
LANES = 128
VMEM_LIMIT = 56 * 1024 * 1024
F32 = jnp.float32
BF16 = jnp.bfloat16

SMEM_SPEC = pl.BlockSpec(memory_space=pltpu.SMEM)
VMEM_SPEC = pl.BlockSpec(memory_space=pltpu.VMEM)


def dot(left, right, contract):
    return lax.dot_general(left, right, ((contract[:1], contract[1:]), ((), ())), preferred_element_type=F32)


def one_hot(rows, values):
    lanes = values.shape[1]
    match = lax.broadcasted_iota(jnp.int32, (rows, lanes), 0) == values
    return jnp.where(match, 1.0, 0.0).astype(BF16)


def split(value):
    high = value.astype(BF16)
    return high, (value - high.astype(F32)).astype(BF16)


def token_kernel(dp_count, rep_count, cap, ob, src, gain, hidden, cot, x_out, own, other, hist, grads):
    rep = lax.axis_index("rep")
    part = cap // rep_count
    tiles = D_OLD // LANES
    step = 1024
    total = jnp.zeros((tiles, LANES), F32)
    for at in range(0, D_NEW, step):
        units = src[:, at : at + step]
        total = total + dot(one_hot(tiles, units >> 7), one_hot(LANES, units & 127), (1, 1))
    hist[...] = total
    tokens = hidden.shape[0]
    squares = jnp.zeros((tokens, LANES), F32)
    for tile in range(tiles):
        stream = hidden[:, tile * LANES : (tile + 1) * LANES].astype(F32)
        squares = squares + stream * stream * hist[tile : tile + 1, :]
    inv_rms = lax.rsqrt(jnp.sum(squares, axis=1, keepdims=True) / D_NEW + 1e-05)
    for tile in range(tiles):
        at = tile * LANES
        stream = hidden[:, at : at + LANES].astype(F32)
        normed = (stream * inv_rms) * gain[tile : tile + 1, :]
        normed = jnp.where(hist[tile : tile + 1, :] > 0.5, normed, 0.0).astype(BF16)
        x_out[:, at : at + LANES] = normed
        grads[at : at + LANES, :] = dot(normed, cot[...], (0, 0))
    grads[D_OLD:, :] = jnp.zeros((cap, LANES), F32)
    for p in range(dp_count):
        first = ob[p]
        own[p] = grads[pl.ds(first + rep * part, part), :].astype(BF16)
        for away in range(1, rep_count):
            mate = (rep + away) % rep_count
            other[away - 1, p] = grads[pl.ds(first + mate * part, part), :].astype(BF16)


def project_kernel(dp_count, cap, ob, x, weights, out, dense):
    for p in range(dp_count):
        dense[pl.ds(ob[p], cap), :] = weights[p * cap : (p + 1) * cap, :].astype(F32)
    out[...] = dot(x[...], dense[0:D_OLD, :].astype(BF16), (1, 0)).astype(BF16)


def offset_of(src, ob, nb, q, dp_count):
    first = src[nb[q]]
    holder = jnp.int32(0)
    for p in range(1, dp_count):
        holder = holder + (ob[p] <= first).astype(jnp.int32)
    return holder


def pack_kernel(dp_count, cap, slots, table_rows, ob, nb, src, gain, grad, weight, first, second, out, rows, gains):
    me = lax.axis_index("dp")
    mine = ob[me]
    pairs = dp_count * slots
    groups = cap // LANES
    rows[...] = jnp.full(rows.shape, -1, jnp.int32)
    for q in range(dp_count):
        start = nb[q] + ((me - offset_of(src, ob, nb, q, dp_count)) & (dp_count - 1))
        end = nb[q + 1]
        for k in range(slots):
            unit = start + dp_count * k
            row = jnp.where(unit < end, src[jnp.minimum(unit, D_NEW - 1)] - mine, -1)
            rows[q * slots + k : q * slots + k + 1, :] = jnp.full((1, LANES), row, jnp.int32)
    lanes = lax.broadcasted_iota(jnp.int32, rows.shape, 1)
    chosen = jnp.concatenate(
        [jnp.where(rows[...] == lanes + g * LANES, 1.0, 0.0).astype(BF16) for g in range(groups)], axis=1
    )
    gains[0 : gain.shape[0], :] = gain[...]
    gains[gain.shape[0] :, :] = jnp.ones((gains.shape[0] - gain.shape[0], LANES), F32)
    gain_rows = gains[pl.ds(mine >> 7, groups + 1), :]
    shift = mine & 127
    rolled = pltpu.roll(gain_rows, (LANES - shift) & 127, 1)
    lane_row = lax.broadcasted_iota(jnp.int32, (groups, LANES), 1)
    own_gain = jnp.where(lane_row < LANES - shift, rolled[:groups], rolled[1:])
    own_row = jnp.concatenate([own_gain[g : g + 1] for g in range(groups)], axis=1)
    high, low = split(weight[...].astype(F32) * grad[...].astype(F32))
    ones = jnp.ones((8, LANES), BF16)
    column = (dot(ones, high, (1, 1)) + dot(ones, low, (1, 1))) / own_row
    high, low = split(column)
    same = dot(chosen, chosen, (1, 1))
    earlier = lax.broadcasted_iota(jnp.int32, same.shape, 0) < lax.broadcasted_iota(jnp.int32, same.shape, 1)
    repeated = jnp.max(jnp.where(earlier, same, 0.0), axis=0, keepdims=True)
    keep = repeated < 0.5
    high = jnp.where(keep, dot(high, chosen, (1, 1))[0:1], 0.0)
    low = jnp.where(keep, dot(low, chosen, (1, 1))[0:1], 0.0)
    table = [part[:, r * LANES : (r + 1) * LANES] for part in (high, low) for r in range(table_rows)]
    spare = out.shape[1] - 3 * slots - 2 * table_rows
    table = jnp.concatenate(table + [jnp.zeros((spare, LANES), F32)], axis=0).astype(BF16)
    picked = chosen[0:pairs]
    for at, value in enumerate((grad[...], first[...].astype(BF16), second[...].astype(BF16))):
        moved = dot(picked, value, (1, 0)).astype(BF16).reshape(dp_count, slots, LANES)
        out[:, at * slots : (at + 1) * slots, :] = moved
    for q in range(dp_count):
        out[q, 3 * slots :, :] = table


def finish_kernel(
    dp_count, slots, table_rows, ob, nb, src, units, moved, gain_grad, first, second, adam, grads, ones, twos, table
):
    me = lax.axis_index("dp")
    offset = offset_of(src, ob, nb, me, dp_count)
    for i in range(dp_count):
        p = (i + offset) & (dp_count - 1)
        strided = pl.ds(i, slots, stride=dp_count)
        grads[strided, :] = moved[p, 0:slots, :].astype(F32)
        ones[strided, :] = moved[p, slots : 2 * slots, :].astype(F32)
        twos[strided, :] = moved[p, 2 * slots : 3 * slots, :].astype(F32)
    cap = first.shape[0]
    live = lax.broadcasted_iota(jnp.int32, (cap, LANES), 0) < nb[me + 1] - nb[me]
    grad = grads[0:cap, :]
    first_next = jnp.where(live, 0.9 * ones[0:cap, :] + 0.1 * grad, 0.0)
    second_next = jnp.where(live, 0.95 * twos[0:cap, :] + 0.05 * grad * grad, 0.0)
    first[...] = first_next
    second[...] = second_next
    adam[...] = first_next / (jnp.sqrt(second_next) + 1e-08)
    at = 3 * slots
    for p in range(dp_count):
        here = p * table_rows
        table[here : here + table_rows, 0:LANES] = moved[p, at : at + table_rows, :].astype(F32)
        table[here : here + table_rows, LANES:] = moved[p, at + table_rows : at + 2 * table_rows, :].astype(F32)
    values = table[...].astype(BF16)
    step = 1024
    for start in range(0, D_NEW, step):
        source = units[:, start : start + step]
        position = start + lax.broadcasted_iota(jnp.int32, (1, step), 1)
        holder = jnp.zeros((1, step), jnp.int32)
        dest = jnp.zeros((1, step), jnp.int32)
        begin = jnp.zeros((1, step), jnp.int32)
        for p in range(1, dp_count):
            holder = holder + jnp.where(source >= ob[p], 1, 0)
            past = position >= nb[p]
            dest = jnp.where(past, p, dest)
            begin = jnp.where(past, nb[p], begin)
        rank = (position - begin) // dp_count
        slot = holder * (table_rows * LANES) + dest * slots + rank
        spread = dot(values, one_hot(values.shape[0], slot >> 7), (0, 0))
        mask = lax.broadcasted_iota(jnp.int32, (LANES, step), 0) == (slot & 127)
        value = jnp.where(mask, spread[:LANES] + spread[LANES:], 0.0)
        gain_grad[:, start : start + step] = jnp.sum(value, axis=0, keepdims=True)


def call(kernel, out_shape, specs, scratch, *args):
    return pl.pallas_call(
        kernel,
        out_shape=out_shape,
        in_specs=specs,
        out_specs=jax.tree.map(lambda _: VMEM_SPEC, out_shape),
        scratch_shapes=scratch,
        compiler_params=pltpu.CompilerParams(vmem_limit_bytes=VMEM_LIMIT),
    )(*args)


def on_device(
    hidden_old,
    cotangent,
    gain_old,
    old_bounds,
    new_bounds,
    source_map,
    weight_old,
    moment_first,
    moment_second,
):
    dp_count = lax.axis_size("dp")
    rep_count = lax.axis_size("rep")
    cap = weight_old.shape[0]
    mean = D_NEW // dp_count
    new_cap = mean + mean // 4
    slots = (new_cap + dp_count - 1) // dp_count
    table_rows = (dp_count * slots + LANES - 1) // LANES
    tokens = hidden_old.shape[0]
    part = cap // rep_count
    shape = jax.ShapeDtypeStruct

    units = source_map.reshape(1, D_NEW)
    gain = gain_old.reshape(D_OLD // LANES, LANES)
    weights = lax.all_gather(weight_old, "dp", axis=0, tiled=True)

    normed, own, other = call(
        lambda *refs: token_kernel(dp_count, rep_count, cap, *refs),
        (
            shape((tokens, D_OLD), BF16),
            shape((dp_count, part, LANES), BF16),
            shape((rep_count - 1, dp_count, part, LANES), BF16),
        ),
        [SMEM_SPEC] + [VMEM_SPEC] * 4,
        [pltpu.VMEM((D_OLD // LANES, LANES), F32), pltpu.VMEM((D_OLD + cap, LANES), F32)],
        old_bounds,
        units,
        gain,
        hidden_old,
        cotangent,
    )
    chip = own.astype(F32)
    for away in range(1, rep_count):
        ring = [(r, (r + away) % rep_count) for r in range(rep_count)]
        chip = chip + lax.ppermute(other[away - 1], "rep", ring).astype(F32)
    parts = lax.all_to_all(chip.astype(BF16), "dp", split_axis=0, concat_axis=0)
    grad_part = jnp.sum(parts.astype(F32), axis=0).astype(BF16)
    grad_own = lax.all_gather(grad_part, "rep", axis=0, tiled=True)

    message = 3 * slots + 2 * table_rows
    message = (message + 7) // 8 * 8
    packed = call(
        lambda *refs: pack_kernel(dp_count, cap, slots, table_rows, *refs),
        shape((dp_count, message, LANES), BF16),
        [SMEM_SPEC] * 3 + [VMEM_SPEC] * 5,
        [pltpu.VMEM((table_rows * LANES, LANES), jnp.int32), pltpu.VMEM((D_OLD // LANES + 8, LANES), F32)],
        old_bounds,
        new_bounds,
        source_map,
        gain,
        grad_own,
        weight_old,
        moment_first,
        moment_second,
    )
    moved = lax.all_to_all(packed, "dp", split_axis=0, concat_axis=0)
    rows = shape((new_cap, LANES), F32)
    gain_grad, first_next, second_next, adam_step = call(
        lambda *refs: finish_kernel(dp_count, slots, table_rows, *refs),
        (shape((1, D_NEW), F32), rows, rows, rows),
        [SMEM_SPEC] * 3 + [VMEM_SPEC] * 2,
        [pltpu.VMEM((dp_count * slots, LANES), F32)] * 3
        + [pltpu.VMEM((dp_count * table_rows, 2 * LANES), F32)],
        old_bounds,
        new_bounds,
        source_map,
        units,
        moved,
    )
    projected = call(
        lambda *refs: project_kernel(dp_count, cap, *refs),
        shape((tokens, LANES), BF16),
        [SMEM_SPEC] + [VMEM_SPEC] * 2,
        [pltpu.VMEM((D_OLD + cap, LANES), F32)],
        old_bounds,
        normed,
        weights,
    )
    return (projected, gain_grad.reshape(D_NEW), first_next, second_next, adam_step)


def solution(mesh):
    placed = (
        P(("dp", "rep"), None),
        P(("dp", "rep"), None),
        P(),
        P(),
        P(),
        P(),
        P("dp", None),
        P("dp", None),
        P("dp", None),
    )
    return jax.shard_map(
        on_device,
        mesh=mesh,
        in_specs=placed,
        out_specs=(P(("dp", "rep"), None), P(), P("dp", None), P("dp", None), P("dp", None)),
        check_vma=False,
    )
```

```python
import jax
import jax.numpy as jnp
from jax import lax
from jax.experimental import pallas as pl
from jax.experimental.pallas import tpu as pltpu
from jax.sharding import PartitionSpec as P

D_OLD = 6144
D_NEW = 8192
LANES = 128
VMEM_LIMIT = 56 * 1024 * 1024
F32 = jnp.float32
BF16 = jnp.bfloat16

SMEM_SPEC = pl.BlockSpec(memory_space=pltpu.SMEM)
VMEM_SPEC = pl.BlockSpec(memory_space=pltpu.VMEM)


def dot(left, right, contract):
    return lax.dot_general(left, right, ((contract[:1], contract[1:]), ((), ())), preferred_element_type=F32)


def one_hot(rows, values):
    lanes = values.shape[1]
    match = lax.broadcasted_iota(jnp.int32, (rows, lanes), 0) == values
    return jnp.where(match, 1.0, 0.0).astype(BF16)


def split(value):
    high = value.astype(BF16)
    return high, (value - high.astype(F32)).astype(BF16)


def token_kernel(rels, rep_count, cap, ob, src, gain, hidden, cot, x_out, *rest):
    *owns, other, hist, grads = rest
    me = lax.axis_index("dp")
    rep = lax.axis_index("rep")
    part = cap // rep_count
    tiles = D_OLD // LANES
    step = 1024
    total = jnp.zeros((tiles, LANES), F32)
    for at in range(0, D_NEW, step):
        units = src[:, at : at + step]
        total = total + dot(one_hot(tiles, units >> 7), one_hot(LANES, units & 127), (1, 1))
    hist[...] = total
    tokens = hidden.shape[0]
    squares = jnp.zeros((tokens, LANES), F32)
    for tile in range(tiles):
        stream = hidden[:, tile * LANES : (tile + 1) * LANES].astype(F32)
        squares = squares + stream * stream * hist[tile : tile + 1, :]
    inv_rms = lax.rsqrt(jnp.sum(squares, axis=1, keepdims=True) / D_NEW + 1e-05)
    for tile in range(tiles):
        at = tile * LANES
        stream = hidden[:, at : at + LANES].astype(F32)
        normed = (stream * inv_rms) * gain[tile : tile + 1, :]
        normed = jnp.where(hist[tile : tile + 1, :] > 0.5, normed, 0.0).astype(BF16)
        x_out[:, at : at + LANES] = normed
        grads[at : at + LANES, :] = dot(normed, cot[...], (0, 0))
    grads[D_OLD:, :] = jnp.zeros((cap, LANES), F32)
    dp_count = len(rels[0])
    half = dp_count // len(owns)
    for at in range(dp_count):
        first = ob[holder_at(rels, rep, me, at)]
        owns[at // half][at % half] = grads[pl.ds(first + rep * part, part), :]
        for away in range(1, rep_count):
            mate = (rep + away) % rep_count
            first = ob[holder_at(rels, mate, me, at)] if len(rels) > 1 else first
            other[away - 1, at] = grads[pl.ds(first + mate * part, part), :].astype(BF16)


def holder_at(rels, rep, me, at):
    if len(rels) == 1:
        return rels[0][at]
    return me ^ jnp.where(rep == 0, rels[0][at], rels[1][at])


def project_kernel(dp_count, orders, cap, ob, x, mine, mate, out, dense):
    me = lax.axis_index("dp")
    rep = lax.axis_index("rep")
    part = cap // 2
    for p in range(dp_count):
        away = me ^ p
        at = [sum(((away >> bit) & 1) << s for s, bit in enumerate(order)) for order in orders]
        first = ob[p]

        @pl.when(rep == 0)
        def _():
            dense[pl.ds(first, part), :] = mine[at[0]].astype(F32)
            dense[pl.ds(first + part, part), :] = mate[at[1]].astype(F32)

        @pl.when(rep != 0)
        def _():
            dense[pl.ds(first, part), :] = mate[at[0]].astype(F32)
            dense[pl.ds(first + part, part), :] = mine[at[1]].astype(F32)

    out[...] = dot(x[...], dense[0:D_OLD, :].astype(BF16), (1, 0)).astype(BF16)


def project_gathered_kernel(dp_count, cap, ob, x, weights, out, dense):
    for p in range(dp_count):
        dense[pl.ds(ob[p], cap), :] = weights[p * cap : (p + 1) * cap, :].astype(F32)
    out[...] = dot(x[...], dense[0:D_OLD, :].astype(BF16), (1, 0)).astype(BF16)


def offset_of(src, ob, nb, q, dp_count):
    first = src[nb[q]]
    holder = jnp.int32(0)
    for p in range(1, dp_count):
        holder = holder + (ob[p] <= first).astype(jnp.int32)
    return holder


def index_kernel(dp_count, cap, slots, table_rows, ob, nb, src, gain, units, chosen, keep, own_gain, places, rows, gains):
    me = lax.axis_index("dp")
    mine = ob[me]
    groups = cap // LANES
    rows[...] = jnp.full(rows.shape, -1, jnp.int32)
    for q in range(dp_count):
        start = nb[q] + ((me - offset_of(src, ob, nb, q, dp_count)) & (dp_count - 1))
        end = nb[q + 1]
        for k in range(slots):
            unit = start + dp_count * k
            row = jnp.where(unit < end, src[jnp.minimum(unit, D_NEW - 1)] - mine, -1)
            rows[q * slots + k : q * slots + k + 1, :] = jnp.full((1, LANES), row, jnp.int32)
    lanes = lax.broadcasted_iota(jnp.int32, rows.shape, 1)
    for g in range(groups):
        chosen[:, g * LANES : (g + 1) * LANES] = jnp.where(rows[...] == lanes + g * LANES, 1.0, 0.0).astype(BF16)
    gains[0 : gain.shape[0], :] = gain[...]
    gains[gain.shape[0] :, :] = jnp.ones((gains.shape[0] - gain.shape[0], LANES), F32)
    gain_rows = gains[pl.ds(mine >> 7, groups + 1), :]
    shift = mine & 127
    rolled = pltpu.roll(gain_rows, (LANES - shift) & 127, 1)
    lane_row = lax.broadcasted_iota(jnp.int32, (groups, LANES), 1)
    inverse = 1.0 / jnp.where(lane_row < LANES - shift, rolled[:groups], rolled[1:])
    for g in range(groups):
        own_gain[:, g * LANES : (g + 1) * LANES] = inverse[g : g + 1]
    same = dot(chosen[...], chosen[...], (1, 1))
    earlier = lax.broadcasted_iota(jnp.int32, same.shape, 0) < lax.broadcasted_iota(jnp.int32, same.shape, 1)
    repeated = jnp.max(jnp.where(earlier, same, 0.0), axis=0, keepdims=True)
    keep[...] = jnp.where(repeated < 0.5, 1.0, 0.0)
    step = 1024
    for first in range(0, D_NEW, step):
        source = units[:, first : first + step]
        position = first + lax.broadcasted_iota(jnp.int32, (1, step), 1)
        holder = jnp.zeros((1, step), jnp.int32)
        dest = jnp.zeros((1, step), jnp.int32)
        begin = jnp.zeros((1, step), jnp.int32)
        for p in range(1, dp_count):
            holder = holder + jnp.where(source >= ob[p], 1, 0)
            past = position >= nb[p]
            dest = jnp.where(past, p, dest)
            begin = jnp.where(past, nb[p], begin)
        rank = (position - begin) >> (dp_count.bit_length() - 1)
        places[:, first : first + step] = holder * (table_rows * LANES) + dest * slots + rank


def pack_kernel(dp_count, slots, table_rows, chosen, keep, own_gain, grad, weight, first, second, out):
    pairs = dp_count * slots
    high, low = split(weight[...].astype(F32) * grad[...])
    ones = jnp.ones((8, LANES), BF16)
    column = (dot(ones, high, (1, 1)) + dot(ones, low, (1, 1))) * own_gain[...]
    high, low = split(column)
    table = []
    for part in (high, low):
        part = dot(part, chosen[...], (1, 1))[0:1] * keep[...]
        table += [part[:, r * LANES : (r + 1) * LANES] for r in range(table_rows)]
    spare = out.shape[1] - 3 * slots - 2 * table_rows
    table = jnp.concatenate(table + [jnp.zeros((spare, LANES), F32)], axis=0).astype(BF16)
    picked = chosen[0:pairs]
    for at, value in enumerate((grad, first, second)):
        moved = dot(picked, value[...].astype(BF16), (1, 0)).astype(BF16).reshape(dp_count, slots, LANES)
        out[:, at * slots : (at + 1) * slots, :] = moved
    for q in range(dp_count):
        out[q, 3 * slots :, :] = table


def finish_kernel(
    dp_count, slots, table_rows, ob, nb, src, places, moved, gain_grad, first, second, adam, grads, ones, twos, table
):
    me = lax.axis_index("dp")
    offset = offset_of(src, ob, nb, me, dp_count)
    for i in range(dp_count):
        p = (i + offset) & (dp_count - 1)
        strided = pl.ds(i, slots, stride=dp_count)
        grads[strided, :] = moved[p, 0:slots, :].astype(F32)
        ones[strided, :] = moved[p, slots : 2 * slots, :].astype(F32)
        twos[strided, :] = moved[p, 2 * slots : 3 * slots, :].astype(F32)
    cap = first.shape[0]
    live = lax.broadcasted_iota(jnp.int32, (cap, LANES), 0) < nb[me + 1] - nb[me]
    grad = grads[0:cap, :]
    first_next = jnp.where(live, 0.9 * ones[0:cap, :] + 0.1 * grad, 0.0)
    second_next = jnp.where(live, 0.95 * twos[0:cap, :] + 0.05 * grad * grad, 0.0)
    first[...] = first_next
    second[...] = second_next
    adam[...] = first_next / (jnp.sqrt(second_next) + 1e-08)
    at = 3 * slots
    for p in range(dp_count):
        here = p * table_rows
        table[here : here + table_rows, 0:LANES] = moved[p, at : at + table_rows, :].astype(F32)
        table[here : here + table_rows, LANES:] = moved[p, at + table_rows : at + 2 * table_rows, :].astype(F32)
    values = table[...].astype(BF16)
    step = 1024
    for start in range(0, D_NEW, step):
        slot = places[:, start : start + step]
        spread = dot(values, one_hot(values.shape[0], slot >> 7), (0, 0))
        mask = lax.broadcasted_iota(jnp.int32, (LANES, step), 0) == (slot & 127)
        value = jnp.where(mask, spread[:LANES] + spread[LANES:], 0.0)
        gain_grad[:, start : start + step] = jnp.sum(value, axis=0, keepdims=True)


def call(kernel, out_shape, specs, scratch, *args):
    return pl.pallas_call(
        kernel,
        out_shape=out_shape,
        in_specs=specs,
        out_specs=jax.tree.map(lambda _: VMEM_SPEC, out_shape),
        scratch_shapes=scratch,
        compiler_params=pltpu.CompilerParams(vmem_limit_bytes=VMEM_LIMIT),
    )(*args)


def on_device(
    hidden_old,
    cotangent,
    gain_old,
    old_bounds,
    new_bounds,
    source_map,
    weight_old,
    moment_first,
    moment_second,
):
    dp_count = lax.axis_size("dp")
    rep_count = lax.axis_size("rep")
    cap = weight_old.shape[0]
    mean = D_NEW // dp_count
    new_cap = mean + mean // 4
    slots = (new_cap + dp_count - 1) // dp_count
    table_rows = (dp_count * slots + LANES - 1) // LANES
    tokens = hidden_old.shape[0]
    part = cap // rep_count
    shape = jax.ShapeDtypeStruct

    units = source_map.reshape(1, D_NEW)
    gain = gain_old.reshape(D_OLD // LANES, LANES)
    staged = rep_count == 2 and dp_count >= 4
    bits = dp_count.bit_length() - 1
    line = list(range(bits - 1))
    halving = [line + [bits - 1], line[::-1] + [bits - 1]]
    doubling = [[bits - 1] + line, [bits - 1] + line[::-1]]
    if staged:
        rels = [
            [sum(((at >> (bits - 1 - s)) & 1) << bit for s, bit in enumerate(order)) for at in range(dp_count)]
            for order in halving
        ]
        parts = 2
    else:
        rels = [list(range(dp_count))]
        parts = 1

    def across(value, orders, stage):
        pairs = [
            (dp * rep_count + rep, (dp ^ (1 << orders[rep][stage])) * rep_count + rep)
            for dp in range(dp_count)
            for rep in range(rep_count)
        ]
        return lax.ppermute(value, ("dp", "rep"), pairs)

    swap = [(0, 1), (1, 0)]
    if staged:
        gathered = lax.dynamic_slice_in_dim(weight_old, lax.axis_index("rep") * part, part)[None]
        gathered = jnp.concatenate([gathered, across(gathered, doubling, 0)])
    else:
        weights = lax.all_gather(weight_old, "dp", axis=0, tiled=True)

    normed, *owns, other = call(
        lambda *refs: token_kernel(rels, rep_count, cap, *refs),
        (
            shape((tokens, D_OLD), BF16),
            *[shape((dp_count // parts, part, LANES), F32)] * parts,
            shape((rep_count - 1, dp_count, part, LANES), BF16),
        ),
        [SMEM_SPEC] + [VMEM_SPEC] * 4,
        [pltpu.VMEM((D_OLD // LANES, LANES), F32), pltpu.VMEM((D_OLD + cap, LANES), F32)],
        old_bounds,
        units,
        gain,
        hidden_old,
        cotangent,
    )
    chosen, keep, own_gain, places = call(
        lambda *refs: index_kernel(dp_count, cap, slots, table_rows, *refs),
        (
            shape((table_rows * LANES, cap), BF16),
            shape((1, table_rows * LANES), F32),
            shape((1, cap), F32),
            shape((1, D_NEW), jnp.int32),
        ),
        [SMEM_SPEC] * 3 + [VMEM_SPEC] * 2,
        [pltpu.VMEM((table_rows * LANES, LANES), jnp.int32), pltpu.VMEM((D_OLD // LANES + 8, LANES), F32)],
        old_bounds,
        new_bounds,
        source_map,
        gain,
        units,
    )
    project_shape = shape((tokens, LANES), BF16)
    dense = [pltpu.VMEM((D_OLD + cap, LANES), F32)]
    if staged:
        from_mate = lax.ppermute(other[0], "rep", swap).astype(F32)
        half = dp_count // 2
        low, high = owns[0] + from_mate[:half], owns[1] + from_mate[half:]
        for stage in range(bits):
            kind = BF16 if stage < 2 else F32
            came = across(high.astype(kind), halving, stage).astype(F32)
            if stage < bits - 1:
                sent = across(gathered, doubling, stage + 1)
                gathered = jnp.concatenate([gathered, sent])
                half = half // 2
                low, high = low[:half] + came[:half], low[half:] + came[half:]
            else:
                grad_part = (low + came)[0]
        from_mate = lax.ppermute(gathered, "rep", swap)
        projected = call(
            lambda *refs: project_kernel(dp_count, doubling, cap, *refs),
            project_shape,
            [SMEM_SPEC] + [VMEM_SPEC] * 3,
            dense,
            old_bounds,
            normed,
            gathered,
            from_mate,
        )
    else:
        chip = owns[0]
        for away in range(1, rep_count):
            ring = [(r, (r + away) % rep_count) for r in range(rep_count)]
            chip = chip + lax.ppermute(other[away - 1], "rep", ring).astype(F32)
        blocks = lax.all_to_all(chip.astype(BF16), "dp", split_axis=0, concat_axis=0)
        grad_part = jnp.sum(blocks.astype(F32), axis=0)
        projected = call(
            lambda *refs: project_gathered_kernel(dp_count, cap, *refs),
            project_shape,
            [SMEM_SPEC] + [VMEM_SPEC] * 2,
            dense,
            old_bounds,
            normed,
            weights,
        )
    grad_own = lax.all_gather(grad_part, "rep", axis=0, tiled=True)

    message = 3 * slots + 2 * table_rows
    message = (message + 7) // 8 * 8
    packed = call(
        lambda *refs: pack_kernel(dp_count, slots, table_rows, *refs),
        shape((dp_count, message, LANES), BF16),
        [VMEM_SPEC] * 7,
        [],
        chosen,
        keep,
        own_gain,
        grad_own,
        weight_old,
        moment_first,
        moment_second,
    )
    moved = lax.all_to_all(packed, "dp", split_axis=0, concat_axis=0)
    rows = shape((new_cap, LANES), F32)
    gain_grad, first_next, second_next, adam_step = call(
        lambda *refs: finish_kernel(dp_count, slots, table_rows, *refs),
        (shape((1, D_NEW), F32), rows, rows, rows),
        [SMEM_SPEC] * 3 + [VMEM_SPEC] * 2,
        [pltpu.VMEM((dp_count * slots, LANES), F32)] * 3
        + [pltpu.VMEM((dp_count * table_rows, 2 * LANES), F32)],
        old_bounds,
        new_bounds,
        source_map,
        places,
        moved,
    )
    return (projected, gain_grad.reshape(D_NEW), first_next, second_next, adam_step)


def solution(mesh):
    placed = (
        P(("dp", "rep"), None),
        P(("dp", "rep"), None),
        P(),
        P(),
        P(),
        P(),
        P("dp", None),
        P("dp", None),
        P("dp", None),
    )
    return jax.shard_map(
        on_device,
        mesh=mesh,
        in_specs=placed,
        out_specs=(P(("dp", "rep"), None), P(), P("dp", None), P("dp", None), P("dp", None)),
        check_vma=False,
    )
```

```python
import jax
import jax.numpy as jnp
from jax import lax
from jax.experimental import pallas as pl
from jax.experimental.pallas import tpu as pltpu
from jax.sharding import PartitionSpec as P

D_OLD = 6144
D_NEW = 8192
LANES = 128
BYTES_PER_US = 3_000_000
VMEM_LIMIT = 56 * 1024 * 1024
F32 = jnp.float32
BF16 = jnp.bfloat16

SMEM_SPEC = pl.BlockSpec(memory_space=pltpu.SMEM)
VMEM_SPEC = pl.BlockSpec(memory_space=pltpu.VMEM)


def dot(left, right, contract):
    return lax.dot_general(left, right, ((contract[:1], contract[1:]), ((), ())), preferred_element_type=F32)


def one_hot(rows, values):
    lanes = values.shape[1]
    match = lax.broadcasted_iota(jnp.int32, (rows, lanes), 0) == values
    return jnp.where(match, 1.0, 0.0).astype(BF16)


def split(value):
    high = value.astype(BF16)
    return high, (value - high.astype(F32)).astype(BF16)


def statistics_kernel(src, hidden, hist, inv_rms):
    tiles = D_OLD // LANES
    step = 1024
    total = jnp.zeros((tiles, LANES), F32)
    for at in range(0, D_NEW, step):
        units = src[:, at : at + step]
        total = total + dot(one_hot(tiles, units >> 7), one_hot(LANES, units & 127), (1, 1))
    hist[...] = total
    tokens = hidden.shape[0]
    squares = jnp.zeros((tokens, LANES), F32)
    for tile in range(tiles):
        stream = hidden[:, tile * LANES : (tile + 1) * LANES].astype(F32)
        squares = squares + stream * stream * hist[tile : tile + 1, :]
    mean = jnp.sum(squares, axis=1, keepdims=True) / D_NEW
    inv_rms[...] = jnp.broadcast_to(lax.rsqrt(mean + 1e-05), (tokens, LANES))


def token_kernel(rels, rep_count, cap, ob, hist, inv_rms, gain, hidden, cot, x_out, *rest):
    *blocks, grads = rest
    owns, others = blocks[: len(blocks) // 2], blocks[len(blocks) // 2 :]
    me = lax.axis_index("dp")
    rep = lax.axis_index("rep")
    part = cap // rep_count
    for tile in range(D_OLD // LANES):
        at = tile * LANES
        stream = hidden[:, at : at + LANES].astype(F32)
        normed = (stream * inv_rms[...]) * gain[tile : tile + 1, :]
        normed = jnp.where(hist[tile : tile + 1, :] > 0.5, normed, 0.0).astype(BF16)
        x_out[:, at : at + LANES] = normed
        grads[at : at + LANES, :] = dot(normed, cot[...], (0, 0))
    grads[D_OLD:, :] = jnp.zeros((cap, LANES), F32)
    dp_count = len(rels[0])
    half = dp_count // len(owns)
    for at in range(dp_count):
        first = ob[holder_at(rels, rep, me, at)]
        owns[at // half][at % half] = grads[pl.ds(first + rep * part, part), :]
        for away in range(1, rep_count):
            mate = (rep + away) % rep_count
            first = ob[holder_at(rels, mate, me, at)] if len(rels) > 1 else first
            others[at // half][away - 1, at % half] = grads[pl.ds(first + mate * part, part), :].astype(BF16)


def holder_at(rels, rep, me, at):
    if len(rels) == 1:
        return rels[0][at]
    return me ^ jnp.where(rep == 0, rels[0][at], rels[1][at])


def project_kernel(dp_count, orders, cap, ob, x, *rest):
    *pieces, out, dense, blocks, sems = rest
    me = lax.axis_index("dp")
    rep = lax.axis_index("rep")
    part = cap // 2
    half = dp_count // 2
    copies = []
    for at, piece in enumerate(pieces):
        side = rep if at < 2 else 1 - rep
        place = blocks.at[side, pl.ds((at % 2) * half, half)]
        copies.append(pltpu.make_async_copy(piece, place, sems.at[at]))
    for copy in copies:
        copy.start()
    for copy in copies:
        copy.wait()
    for p in range(dp_count):
        away = me ^ p
        for side, order in enumerate(orders):
            at = sum(((away >> bit) & 1) << s for s, bit in enumerate(order))
            dense[pl.ds(ob[p] + side * part, part), :] = blocks[side, at].astype(F32)
    out[...] = dot(x[...], dense[0:D_OLD, :].astype(BF16), (1, 0)).astype(BF16)


def project_gathered_kernel(dp_count, cap, ob, x, weights, out, dense):
    for p in range(dp_count):
        dense[pl.ds(ob[p], cap), :] = weights[p * cap : (p + 1) * cap, :].astype(F32)
    out[...] = dot(x[...], dense[0:D_OLD, :].astype(BF16), (1, 0)).astype(BF16)


def offset_of(src, ob, nb, q, dp_count):
    first = src[nb[q]]
    holder = jnp.int32(0)
    for p in range(1, dp_count):
        holder = holder + (ob[p] <= first).astype(jnp.int32)
    return holder


def index_kernel(dp_count, cap, slots, table_rows, ob, nb, src, gain, units, chosen, keep, own_gain, places, rows, gains):
    me = lax.axis_index("dp")
    mine = ob[me]
    groups = cap // LANES
    rows[...] = jnp.full(rows.shape, -1, jnp.int32)
    for q in range(dp_count):
        start = nb[q] + ((me - offset_of(src, ob, nb, q, dp_count)) & (dp_count - 1))
        end = nb[q + 1]
        for k in range(slots):
            unit = start + dp_count * k
            row = jnp.where(unit < end, src[jnp.minimum(unit, D_NEW - 1)] - mine, -1)
            rows[q * slots + k : q * slots + k + 1, :] = jnp.full((1, LANES), row, jnp.int32)
    lanes = lax.broadcasted_iota(jnp.int32, rows.shape, 1)
    for g in range(groups):
        chosen[:, g * LANES : (g + 1) * LANES] = jnp.where(rows[...] == lanes + g * LANES, 1.0, 0.0).astype(BF16)
    gains[0 : gain.shape[0], :] = gain[...]
    gains[gain.shape[0] :, :] = jnp.ones((gains.shape[0] - gain.shape[0], LANES), F32)
    gain_rows = gains[pl.ds(mine >> 7, groups + 1), :]
    shift = mine & 127
    rolled = pltpu.roll(gain_rows, (LANES - shift) & 127, 1)
    lane_row = lax.broadcasted_iota(jnp.int32, (groups, LANES), 1)
    inverse = 1.0 / jnp.where(lane_row < LANES - shift, rolled[:groups], rolled[1:])
    for g in range(groups):
        own_gain[:, g * LANES : (g + 1) * LANES] = inverse[g : g + 1]
    same = dot(chosen[...], chosen[...], (1, 1))
    earlier = lax.broadcasted_iota(jnp.int32, same.shape, 0) < lax.broadcasted_iota(jnp.int32, same.shape, 1)
    repeated = jnp.max(jnp.where(earlier, same, 0.0), axis=0, keepdims=True)
    keep[...] = jnp.where(repeated < 0.5, 1.0, 0.0)
    step = 1024
    for first in range(0, D_NEW, step):
        source = units[:, first : first + step]
        position = first + lax.broadcasted_iota(jnp.int32, (1, step), 1)
        holder = jnp.zeros((1, step), jnp.int32)
        dest = jnp.zeros((1, step), jnp.int32)
        begin = jnp.zeros((1, step), jnp.int32)
        for p in range(1, dp_count):
            holder = holder + jnp.where(source >= ob[p], 1, 0)
            past = position >= nb[p]
            dest = jnp.where(past, p, dest)
            begin = jnp.where(past, nb[p], begin)
        rank = (position - begin) >> (dp_count.bit_length() - 1)
        places[:, first : first + step] = holder * (table_rows * LANES) + dest * slots + rank


def pack_kernel(dp_count, slots, table_rows, chosen, keep, own_gain, mine, *rest):
    *mate, weight, first, second, out = rest
    pairs = dp_count * slots
    grad = mine[...]
    if mate:
        grad, other = mine[0], mate[0][0]
        own_first = lax.axis_index("rep") == 0
        grad = jnp.concatenate([jnp.where(own_first, grad, other), jnp.where(own_first, other, grad)], axis=0)
    high, low = split(weight[...].astype(F32) * grad)
    ones = jnp.ones((8, LANES), BF16)
    column = (dot(ones, high, (1, 1)) + dot(ones, low, (1, 1))) * own_gain[...]
    high, low = split(column)
    table = []
    for part in (high, low):
        part = dot(part, chosen[...], (1, 1))[0:1] * keep[...]
        table += [part[:, r * LANES : (r + 1) * LANES] for r in range(table_rows)]
    spare = out.shape[1] - 2 * slots - 2 * table_rows
    table = jnp.concatenate(table + [jnp.zeros((spare, LANES), F32)], axis=0).astype(BF16)
    picked = chosen[0:pairs]
    updated = (0.9 * first[...] + 0.1 * grad, 0.95 * second[...] + 0.05 * grad * grad)
    for at, value in enumerate(updated):
        moved = dot(picked, value.astype(BF16), (1, 0)).astype(BF16).reshape(dp_count, slots, LANES)
        out[:, at * slots : (at + 1) * slots, :] = moved
    for q in range(dp_count):
        out[q, 2 * slots :, :] = table


def finish_kernel(
    dp_count, slots, table_rows, ob, nb, src, places, moved, gain_grad, first, second, adam, ones, twos, table
):
    me = lax.axis_index("dp")
    offset = offset_of(src, ob, nb, me, dp_count)
    for i in range(dp_count):
        p = (i + offset) & (dp_count - 1)
        strided = pl.ds(i, slots, stride=dp_count)
        ones[strided, :] = moved[p, 0:slots, :].astype(F32)
        twos[strided, :] = moved[p, slots : 2 * slots, :].astype(F32)
    cap = first.shape[0]
    live = lax.broadcasted_iota(jnp.int32, (cap, LANES), 0) < nb[me + 1] - nb[me]
    first_next = jnp.where(live, ones[0:cap, :], 0.0)
    second_next = jnp.where(live, twos[0:cap, :], 0.0)
    first[...] = first_next
    second[...] = second_next
    adam[...] = first_next / (jnp.sqrt(second_next) + 1e-08)
    at = 2 * slots
    for p in range(dp_count):
        here = p * table_rows
        table[here : here + table_rows, 0:LANES] = moved[p, at : at + table_rows, :].astype(F32)
        table[here : here + table_rows, LANES:] = moved[p, at + table_rows : at + 2 * table_rows, :].astype(F32)
    values = table[...].astype(BF16)
    step = 1024
    for start in range(0, D_NEW, step):
        slot = places[:, start : start + step]
        spread = dot(values, one_hot(values.shape[0], slot >> 7), (0, 0))
        mask = lax.broadcasted_iota(jnp.int32, (LANES, step), 0) == (slot & 127)
        value = jnp.where(mask, spread[:LANES] + spread[LANES:], 0.0)
        gain_grad[:, start : start + step] = jnp.sum(value, axis=0, keepdims=True)


def call(kernel, micros, out_shape, specs, scratch, *args):
    return pl.pallas_call(
        kernel,
        out_shape=out_shape,
        in_specs=specs,
        out_specs=jax.tree.map(lambda _: VMEM_SPEC, out_shape),
        scratch_shapes=scratch,
        cost_estimate=pl.CostEstimate(flops=0, transcendentals=0, bytes_accessed=micros * BYTES_PER_US),
        compiler_params=pltpu.CompilerParams(vmem_limit_bytes=VMEM_LIMIT),
    )(*args)


def on_device(
    hidden_old,
    cotangent,
    gain_old,
    old_bounds,
    new_bounds,
    source_map,
    weight_old,
    moment_first,
    moment_second,
):
    dp_count = lax.axis_size("dp")
    rep_count = lax.axis_size("rep")
    cap = weight_old.shape[0]
    mean = D_NEW // dp_count
    new_cap = mean + mean // 4
    slots = (new_cap + dp_count - 1) // dp_count
    table_rows = (dp_count * slots + LANES - 1) // LANES
    tokens = hidden_old.shape[0]
    part = cap // rep_count
    shape = jax.ShapeDtypeStruct

    units = source_map.reshape(1, D_NEW)
    gain = gain_old.reshape(D_OLD // LANES, LANES)
    staged = rep_count == 2 and dp_count >= 4
    bits = dp_count.bit_length() - 1
    line = list(range(bits - 1))
    halving = [line + [bits - 1], line[::-1] + [bits - 1]]
    doubling = [[bits - 1] + line, [bits - 1] + line[::-1]]
    if staged:
        rels = [
            [sum(((at >> (bits - 1 - s)) & 1) << bit for s, bit in enumerate(order)) for at in range(dp_count)]
            for order in halving
        ]
        parts = 2
    else:
        rels = [list(range(dp_count))]
        parts = 1

    def across(value, orders, stage):
        pairs = [
            (dp * rep_count + rep, (dp ^ (1 << orders[rep][stage])) * rep_count + rep)
            for dp in range(dp_count)
            for rep in range(rep_count)
        ]
        return lax.ppermute(value, ("dp", "rep"), pairs)

    swap = [(0, 1), (1, 0)]
    if staged:
        gathered = lax.dynamic_slice_in_dim(weight_old, lax.axis_index("rep") * part, part)[None]
    else:
        weights = lax.all_gather(weight_old, "dp", axis=0, tiled=True)

    tiles = D_OLD // LANES
    hist, inv_rms = call(
        statistics_kernel,
        4,
        (shape((tiles, LANES), F32), shape((tokens, LANES), F32)),
        [VMEM_SPEC] * 2,
        [],
        units,
        hidden_old,
    )
    if staged:
        hist, sent = lax.optimization_barrier((hist, across(gathered, doubling, 0)))
        gathered = jnp.concatenate([gathered, sent])
        sent = across(gathered, doubling, 1)
    normed, *blocks = call(
        lambda *refs: token_kernel(rels, rep_count, cap, *refs),
        5,
        (
            shape((tokens, D_OLD), BF16),
            *[shape((dp_count // parts, part, LANES), F32)] * parts,
            *[shape((rep_count - 1, dp_count // parts, part, LANES), BF16)] * parts,
        ),
        [SMEM_SPEC] + [VMEM_SPEC] * 5,
        [pltpu.VMEM((D_OLD + cap, LANES), F32)],
        old_bounds,
        hist,
        inv_rms,
        gain,
        hidden_old,
        cotangent,
    )
    owns, others = blocks[:parts], blocks[parts:]
    chosen, keep, own_gain, places = call(
        lambda *refs: index_kernel(dp_count, cap, slots, table_rows, *refs),
        5,
        (
            shape((table_rows * LANES, cap), BF16),
            shape((1, table_rows * LANES), F32),
            shape((1, cap), F32),
            shape((1, D_NEW), jnp.int32),
        ),
        [SMEM_SPEC] * 3 + [VMEM_SPEC] * 2,
        [pltpu.VMEM((table_rows * LANES, LANES), jnp.int32), pltpu.VMEM((D_OLD // LANES + 8, LANES), F32)],
        old_bounds,
        new_bounds,
        source_map,
        gain,
        units,
    )
    project_shape = shape((tokens, LANES), BF16)
    dense = [pltpu.VMEM((D_OLD + cap, LANES), F32)]
    if staged:
        half = dp_count // 2
        high = owns[1] + lax.ppermute(others[1][0], "rep", swap).astype(F32)
        low = owns[0] + lax.ppermute(others[0][0], "rep", swap).astype(F32)
        high, sent = lax.optimization_barrier((high.astype(BF16), sent))
        for stage in range(bits - 1):
            came = across(high, halving, stage)
            if stage < bits - 2:
                gathered = jnp.concatenate([gathered, sent])
                sent = across(gathered, doubling, stage + 2)
                came, sent, chosen = lax.optimization_barrier((came, sent, chosen))
            came = came.astype(F32)
            half = half // 2
            low, high = low[:half] + came[:half], low[half:] + came[half:]
            if stage < 1:
                high = high.astype(BF16)
        grad_part = low + across(high, halving, bits - 1).astype(F32)
        grads = [grad_part, lax.ppermute(grad_part, "rep", swap)]
        pieces = [gathered, sent]
        pieces += [lax.ppermute(piece, "rep", swap) for piece in pieces]
        projected = call(
            lambda *refs: project_kernel(dp_count, doubling, cap, *refs),
            5,
            project_shape,
            [SMEM_SPEC, VMEM_SPEC] + [pl.BlockSpec(memory_space=pl.ANY)] * 4,
            dense + [pltpu.VMEM((2, dp_count, part, LANES), BF16), pltpu.SemaphoreType.DMA((4,))],
            old_bounds,
            normed,
            *pieces,
        )
    else:
        chip = owns[0]
        for away in range(1, rep_count):
            ring = [(r, (r + away) % rep_count) for r in range(rep_count)]
            chip = chip + lax.ppermute(others[0][away - 1], "rep", ring).astype(F32)
        blocks = lax.all_to_all(chip.astype(BF16), "dp", split_axis=0, concat_axis=0)
        grad_part = jnp.sum(blocks.astype(F32), axis=0)
        grads = [lax.all_gather(grad_part, "rep", axis=0, tiled=True)]
        projected = call(
            lambda *refs: project_gathered_kernel(dp_count, cap, *refs),
            5,
            project_shape,
            [SMEM_SPEC] + [VMEM_SPEC] * 2,
            dense,
            old_bounds,
            normed,
            weights,
        )
    message = 2 * slots + 2 * table_rows
    message = (message + 7) // 8 * 8
    packed = call(
        lambda *refs: pack_kernel(dp_count, slots, table_rows, *refs),
        3,
        shape((dp_count, message, LANES), BF16),
        [VMEM_SPEC] * (6 + len(grads)),
        [],
        chosen,
        keep,
        own_gain,
        *grads,
        weight_old,
        moment_first,
        moment_second,
    )
    moved = lax.all_to_all(packed, "dp", split_axis=0, concat_axis=0)
    rows = shape((new_cap, LANES), F32)
    gain_grad, first_next, second_next, adam_step = call(
        lambda *refs: finish_kernel(dp_count, slots, table_rows, *refs),
        4,
        (shape((1, D_NEW), F32), rows, rows, rows),
        [SMEM_SPEC] * 3 + [VMEM_SPEC] * 2,
        [pltpu.VMEM((dp_count * slots, LANES), F32)] * 2
        + [pltpu.VMEM((dp_count * table_rows, 2 * LANES), F32)],
        old_bounds,
        new_bounds,
        source_map,
        places,
        moved,
    )
    return (projected, gain_grad.reshape(D_NEW), first_next, second_next, adam_step)


def solution(mesh):
    placed = (
        P(("dp", "rep"), None),
        P(("dp", "rep"), None),
        P(),
        P(),
        P(),
        P(),
        P("dp", None),
        P("dp", None),
        P("dp", None),
    )
    return jax.shard_map(
        on_device,
        mesh=mesh,
        in_specs=placed,
        out_specs=(P(("dp", "rep"), None), P(), P("dp", None), P("dp", None), P("dp", None)),
        check_vma=False,
    )
```

```python
import jax
import jax.numpy as jnp
from jax import lax
from jax.experimental import pallas as pl
from jax.experimental.pallas import tpu as pltpu
from jax.sharding import PartitionSpec as P

D_OLD = 6144
D_NEW = 8192
LANES = 128
BYTES_PER_US = 3_000_000
VMEM_LIMIT = 56 * 1024 * 1024
F32 = jnp.float32
BF16 = jnp.bfloat16

SMEM_SPEC = pl.BlockSpec(memory_space=pltpu.SMEM)
VMEM_SPEC = pl.BlockSpec(memory_space=pltpu.VMEM)


def dot(left, right, contract):
    return lax.dot_general(left, right, ((contract[:1], contract[1:]), ((), ())), preferred_element_type=F32)


def one_hot(rows, values):
    lanes = values.shape[1]
    match = lax.broadcasted_iota(jnp.int32, (rows, lanes), 0) == values
    return jnp.where(match, 1.0, 0.0).astype(BF16)


def split(value):
    high = value.astype(BF16)
    return high, (value - high.astype(F32)).astype(BF16)


def normed_tile(tile, hidden, inv_rms, gain, hist):
    stream = hidden[:, tile * LANES : (tile + 1) * LANES].astype(F32)
    normed = (stream * inv_rms) * gain[tile : tile + 1, :]
    return jnp.where(hist[tile : tile + 1, :] > 0.5, normed, 0.0).astype(BF16)


def lower_half(rows):
    return lax.broadcasted_iota(jnp.int32, (rows, LANES), 1) < LANES // 2


def token_kernel(rels, rep_count, cap, ob, src, gain, hidden_hbm, cot, hist, inv_out, *rest):
    *blocks, hidden, own_grads, other_grads, sem = rest
    owns, others = blocks[: len(blocks) // 2], blocks[len(blocks) // 2 :]
    copy = pltpu.make_async_copy(hidden_hbm, hidden, sem)
    copy.start()
    me = lax.axis_index("dp")
    rep = lax.axis_index("rep")
    tiles = D_OLD // LANES
    tokens = hidden.shape[0]
    step = 1024
    total = jnp.zeros((tiles, LANES), F32)
    for at in range(0, D_NEW, step):
        units = src[:, at : at + step]
        total = total + dot(one_hot(tiles, units >> 7), one_hot(LANES, units & 127), (1, 1))
    hist[...] = total
    copy.wait()
    squares = jnp.zeros((tokens, LANES), F32)
    for tile in range(tiles):
        stream = hidden[:, tile * LANES : (tile + 1) * LANES].astype(F32)
        squares = squares + stream * stream * hist[tile : tile + 1, :]
    inv_rms = lax.rsqrt(jnp.sum(squares, axis=1, keepdims=True) / D_NEW + 1e-05)
    inv_out[...] = jnp.broadcast_to(inv_rms, (tokens, LANES))
    staged = len(rels) > 1
    columns = cot[...]
    if staged:
        lower = lower_half(tokens)
        columns = columns.astype(F32)
        turned = pltpu.roll(columns, LANES // 2, 1)
        left, right = jnp.where(lower, columns, turned), jnp.where(lower, turned, columns)
        sides = [jnp.where(rep == 0, left, right), jnp.where(rep == 0, right, left)]
        columns = jnp.concatenate(sides, axis=1).astype(BF16)
    for tile in range(tiles):
        at = tile * LANES
        result = dot(normed_tile(tile, hidden, inv_rms, gain, hist), columns, (0, 0))
        own_grads[at : at + LANES, :] = result[:, :LANES]
        if staged:
            other_grads[at : at + LANES, :] = result[:, LANES:]
    own_grads[D_OLD:, :] = jnp.zeros((cap, LANES), F32)
    other_grads[D_OLD:, :] = jnp.zeros((cap, LANES), F32)
    dp_count = len(rels[0])
    half = dp_count // len(owns)
    part = cap // rep_count
    for at in range(dp_count):
        if staged:
            first = ob[holder_at(rels, rep, me, at)]
            owns[at // half][at % half] = packed_rows(own_grads, first, part)
            first = ob[holder_at(rels, 1 - rep, me, at)]
            others[at // half][0, at % half] = packed_rows(other_grads, first, part).astype(BF16)
        else:
            first = ob[at]
            owns[0][at] = own_grads[pl.ds(first + rep * part, part), :]
            for away in range(1, rep_count):
                mate = (rep + away) % rep_count
                others[0][away - 1, at] = own_grads[pl.ds(first + mate * part, part), :].astype(BF16)


def packed_rows(grads, first, part):
    return jnp.where(lower_half(part), grads[pl.ds(first, part), :], grads[pl.ds(first + part, part), :])


def holder_at(rels, rep, me, at):
    return me ^ jnp.where(rep == 0, rels[0][at], rels[1][at])


def fill_normed(x, hidden, inv_rms, gain, hist):
    for tile in range(D_OLD // LANES):
        x[:, tile * LANES : (tile + 1) * LANES] = normed_tile(tile, hidden, inv_rms[...], gain, hist)


def project_kernel(dp_count, orders, cap, ob, hidden, inv_rms, gain, hist, *rest):
    *pieces, out, dense, x, blocks, sems = rest
    me = lax.axis_index("dp")
    rep = lax.axis_index("rep")
    part = cap // 2
    half = dp_count // 2
    copies = []
    for at, piece in enumerate(pieces):
        side = rep if at < 2 else 1 - rep
        place = blocks.at[side, pl.ds((at % 2) * half, half)]
        copies.append(pltpu.make_async_copy(piece, place, sems.at[at]))
    for copy in copies:
        copy.start()
    fill_normed(x, hidden, inv_rms, gain, hist)
    for copy in copies:
        copy.wait()
    for p in range(dp_count):
        away = me ^ p
        for side, order in enumerate(orders):
            at = sum(((away >> bit) & 1) << s for s, bit in enumerate(order))
            dense[pl.ds(ob[p] + side * part, part), :] = blocks[side, at].astype(F32)
    out[...] = dot(x[...], dense[0:D_OLD, :].astype(BF16), (1, 0)).astype(BF16)


def project_gathered_kernel(dp_count, cap, ob, hidden, inv_rms, gain, hist, weights, out, dense, x):
    fill_normed(x, hidden, inv_rms, gain, hist)
    for p in range(dp_count):
        dense[pl.ds(ob[p], cap), :] = weights[p * cap : (p + 1) * cap, :].astype(F32)
    out[...] = dot(x[...], dense[0:D_OLD, :].astype(BF16), (1, 0)).astype(BF16)


def offset_of(src, ob, nb, q, dp_count):
    first = src[nb[q]]
    holder = jnp.int32(0)
    for p in range(1, dp_count):
        holder = holder + (ob[p] <= first).astype(jnp.int32)
    return holder


def index_kernel(dp_count, cap, slots, table_rows, ob, nb, src, gain, units, chosen, keep, own_gain, places, rows, gains):
    me = lax.axis_index("dp")
    mine = ob[me]
    groups = cap // LANES
    rows[...] = jnp.full(rows.shape, -1, jnp.int32)
    for q in range(dp_count):
        start = nb[q] + ((me - offset_of(src, ob, nb, q, dp_count)) & (dp_count - 1))
        end = nb[q + 1]
        for k in range(slots):
            unit = start + dp_count * k
            row = jnp.where(unit < end, src[jnp.minimum(unit, D_NEW - 1)] - mine, -1)
            rows[q * slots + k : q * slots + k + 1, :] = jnp.full((1, LANES), row, jnp.int32)
    lanes = lax.broadcasted_iota(jnp.int32, rows.shape, 1)
    for g in range(groups):
        chosen[:, g * LANES : (g + 1) * LANES] = jnp.where(rows[...] == lanes + g * LANES, 1.0, 0.0).astype(BF16)
    gains[0 : gain.shape[0], :] = gain[...]
    gains[gain.shape[0] :, :] = jnp.ones((gains.shape[0] - gain.shape[0], LANES), F32)
    gain_rows = gains[pl.ds(mine >> 7, groups + 1), :]
    shift = mine & 127
    rolled = pltpu.roll(gain_rows, (LANES - shift) & 127, 1)
    lane_row = lax.broadcasted_iota(jnp.int32, (groups, LANES), 1)
    inverse = 1.0 / jnp.where(lane_row < LANES - shift, rolled[:groups], rolled[1:])
    for g in range(groups):
        own_gain[:, g * LANES : (g + 1) * LANES] = inverse[g : g + 1]
    same = dot(chosen[...], chosen[...], (1, 1))
    earlier = lax.broadcasted_iota(jnp.int32, same.shape, 0) < lax.broadcasted_iota(jnp.int32, same.shape, 1)
    repeated = jnp.max(jnp.where(earlier, same, 0.0), axis=0, keepdims=True)
    keep[...] = jnp.where(repeated < 0.5, 1.0, 0.0)
    step = 1024
    for first in range(0, D_NEW, step):
        source = units[:, first : first + step]
        position = first + lax.broadcasted_iota(jnp.int32, (1, step), 1)
        holder = jnp.zeros((1, step), jnp.int32)
        dest = jnp.zeros((1, step), jnp.int32)
        begin = jnp.zeros((1, step), jnp.int32)
        for p in range(1, dp_count):
            holder = holder + jnp.where(source >= ob[p], 1, 0)
            past = position >= nb[p]
            dest = jnp.where(past, p, dest)
            begin = jnp.where(past, nb[p], begin)
        rank = (position - begin) >> (dp_count.bit_length() - 1)
        places[:, first : first + step] = holder * (table_rows * LANES) + dest * slots + rank


def pack_kernel(dp_count, slots, table_rows, staged, chosen, keep, own_gain, reduced, weight_in, first_in, second_in, out):
    pairs = dp_count * slots
    rows = weight_in.shape[0]
    weight, first, second = weight_in[...].astype(F32), first_in[...], second_in[...]
    if staged:
        turn = LANES // 2
        lower = lower_half(rows)
        grad = reduced[0]
        grad = jnp.concatenate([grad, pltpu.roll(grad, turn, 1)], axis=0)
        left = lax.axis_index("rep") == 0
        weight, first, second = [
            jnp.where(left, value, pltpu.roll(value, turn, 1)) for value in (weight, first, second)
        ]
        product = jnp.where(lower, weight * grad, 0.0)
    else:
        grad = reduced[...]
        product = weight * grad
    high, low = split(product)
    ones = jnp.ones((8, LANES), BF16)
    column = (dot(ones, high, (1, 1)) + dot(ones, low, (1, 1))) * own_gain[...]
    high, low = split(column)
    table = []
    for part in (high, low):
        part = dot(part, chosen[...], (1, 1))[0:1] * keep[...]
        table += [part[:, r * LANES : (r + 1) * LANES] for r in range(table_rows)]
    updated = [0.9 * first + 0.1 * grad, 0.95 * second + 0.05 * grad * grad]
    if staged:
        updated = [jnp.where(lower, updated[0], pltpu.roll(updated[1], turn, 1))]
    filled = len(updated) * slots
    spare = out.shape[1] - filled - 2 * table_rows
    table = jnp.concatenate(table + [jnp.zeros((spare, LANES), F32)], axis=0).astype(BF16)
    picked = chosen[0:pairs]
    for at, value in enumerate(updated):
        moved = dot(picked, value.astype(BF16), (1, 0)).astype(BF16).reshape(dp_count, slots, LANES)
        out[:, at * slots : (at + 1) * slots, :] = moved
    for q in range(dp_count):
        out[q, filled:, :] = table


def finish_kernel(dp_count, slots, table_rows, staged, ob, nb, src, places, *rest):
    arrived, rest = (rest[:2], rest[2:]) if staged else (rest[:1], rest[1:])
    gain_grad, first, second, adam, ones, twos, table = rest
    me = lax.axis_index("dp")
    offset = offset_of(src, ob, nb, me, dp_count)
    groups = 1 if staged else 2
    pages = [(moved, 0) for moved in arrived] if staged else [(arrived[0], 0), (arrived[0], slots)]
    for i in range(dp_count):
        p = (i + offset) & (dp_count - 1)
        strided = pl.ds(i, slots, stride=dp_count)
        for (moved, at), rows in zip(pages, (ones, twos)):
            rows[strided, :] = moved[p, at : at + slots, :].astype(F32)
    cap = first.shape[0]
    live = lax.broadcasted_iota(jnp.int32, (cap, LANES), 0) < nb[me + 1] - nb[me]
    one, two = ones[0:cap, :], twos[0:cap, :]
    if staged:
        left = lax.axis_index("rep") == 0
        lower = lower_half(cap)
        one, two = jnp.where(left, one, two), jnp.where(left, two, one)
        turn = LANES // 2
        one, two = (
            jnp.where(lower, one, pltpu.roll(two, turn, 1)),
            jnp.where(lower, pltpu.roll(one, turn, 1), two),
        )
    first_next = jnp.where(live, one, 0.0)
    second_next = jnp.where(live, two, 0.0)
    first[...] = first_next
    second[...] = second_next
    adam[...] = first_next / (jnp.sqrt(second_next) + 1e-08)
    at = groups * slots
    for p in range(dp_count):
        here = p * table_rows
        terms = [
            moved[p, at + r : at + r + table_rows, :].astype(F32) for moved in arrived for r in (0, table_rows)
        ]
        table[here : here + table_rows, :] = sum(terms[1:], terms[0])
    high, low = split(table[...])
    values = jnp.concatenate([high, low], axis=1)
    step = 1024
    for start in range(0, D_NEW, step):
        slot = places[:, start : start + step]
        spread = dot(values, one_hot(values.shape[0], slot >> 7), (0, 0))
        mask = lax.broadcasted_iota(jnp.int32, (LANES, step), 0) == (slot & 127)
        value = jnp.where(mask, spread[:LANES] + spread[LANES:], 0.0)
        gain_grad[:, start : start + step] = jnp.sum(value, axis=0, keepdims=True)


def call(kernel, micros, out_shape, specs, scratch, *args):
    return pl.pallas_call(
        kernel,
        out_shape=out_shape,
        in_specs=specs,
        out_specs=jax.tree.map(lambda _: VMEM_SPEC, out_shape),
        scratch_shapes=scratch,
        cost_estimate=pl.CostEstimate(flops=0, transcendentals=0, bytes_accessed=micros * BYTES_PER_US),
        compiler_params=pltpu.CompilerParams(vmem_limit_bytes=VMEM_LIMIT),
    )(*args)


def on_device(
    hidden_old,
    cotangent,
    gain_old,
    old_bounds,
    new_bounds,
    source_map,
    weight_old,
    moment_first,
    moment_second,
):
    dp_count = lax.axis_size("dp")
    rep_count = lax.axis_size("rep")
    cap = weight_old.shape[0]
    mean = D_NEW // dp_count
    new_cap = mean + mean // 4
    slots = (new_cap + dp_count - 1) // dp_count
    table_rows = (dp_count * slots + LANES - 1) // LANES
    tokens = hidden_old.shape[0]
    part = cap // rep_count
    shape = jax.ShapeDtypeStruct

    units = source_map.reshape(1, D_NEW)
    gain = gain_old.reshape(D_OLD // LANES, LANES)
    staged = rep_count == 2 and dp_count >= 4
    bits = dp_count.bit_length() - 1
    line = list(range(bits - 1))
    halving = [line + [bits - 1], line[::-1] + [bits - 1]]
    doubling = [[bits - 1] + line, [bits - 1] + line[::-1]]
    if staged:
        rels = [
            [sum(((at >> (bits - 1 - s)) & 1) << bit for s, bit in enumerate(order)) for at in range(dp_count)]
            for order in halving
        ]
        parts = 2
    else:
        rels = [list(range(dp_count))]
        parts = 1

    def across(value, orders, stage):
        pairs = [
            (dp * rep_count + rep, (dp ^ (1 << orders[rep][stage])) * rep_count + rep)
            for dp in range(dp_count)
            for rep in range(rep_count)
        ]
        return lax.ppermute(value, ("dp", "rep"), pairs)

    swap = [(0, 1), (1, 0)]
    any_spec = pl.BlockSpec(memory_space=pl.ANY)
    if staged:
        gathered = lax.dynamic_slice_in_dim(weight_old, lax.axis_index("rep") * part, part)[None]
        sent = across(gathered, doubling, 0)
    else:
        weights = lax.all_gather(weight_old, "dp", axis=0, tiled=True)

    tiles = D_OLD // LANES
    hist, inv_rms, *blocks = call(
        lambda *refs: token_kernel(rels, rep_count, cap, *refs),
        8,
        (
            shape((tiles, LANES), F32),
            shape((tokens, LANES), F32),
            *[shape((dp_count // parts, part, LANES), F32)] * parts,
            *[shape((rep_count - 1, dp_count // parts, part, LANES), BF16)] * parts,
        ),
        [SMEM_SPEC] + [VMEM_SPEC] * 2 + [any_spec] + [VMEM_SPEC],
        [
            pltpu.VMEM((tokens, D_OLD), BF16),
            pltpu.VMEM((D_OLD + cap, LANES), F32),
            pltpu.VMEM((D_OLD + cap, LANES), F32),
            pltpu.SemaphoreType.DMA(()),
        ],
        old_bounds,
        units,
        gain,
        hidden_old,
        cotangent,
    )
    owns, others = blocks[:parts], blocks[parts:]
    def indices(units):
        return call(
            lambda *refs: index_kernel(dp_count, cap, slots, table_rows, *refs),
            5,
            (
                shape((table_rows * LANES, cap), BF16),
                shape((1, table_rows * LANES), F32),
                shape((1, cap), F32),
                shape((1, D_NEW), jnp.int32),
            ),
            [SMEM_SPEC] * 3 + [VMEM_SPEC] * 2,
            [pltpu.VMEM((table_rows * LANES, LANES), jnp.int32), pltpu.VMEM((D_OLD // LANES + 8, LANES), F32)],
            old_bounds,
            new_bounds,
            source_map,
            gain,
            units,
        )

    project_shape = shape((tokens, LANES), BF16)
    dense = [pltpu.VMEM((D_OLD + cap, LANES), F32), pltpu.VMEM((tokens, D_OLD), BF16)]
    if staged:
        half = dp_count // 2
        send, sent = lax.optimization_barrier((others[1][0], sent))
        gathered = jnp.concatenate([gathered, sent])
        sent = across(gathered, doubling, 1)
        high = (owns[1] + lax.ppermute(send, "rep", swap).astype(F32)).astype(BF16)
        low = owns[0] + lax.ppermute(others[0][0], "rep", swap).astype(F32)
        high, sent = lax.optimization_barrier((high, sent))
        for stage in range(bits - 1):
            came = across(high, halving, stage)
            if stage < bits - 2:
                gathered = jnp.concatenate([gathered, sent])
                sent = across(gathered, doubling, stage + 2)
                came, sent = lax.optimization_barrier((came, sent))
            if stage == 1:
                came, chosen = lax.optimization_barrier((came, chosen))
            came = came.astype(F32)
            half = half // 2
            low, high = low[:half] + came[:half], (low[half:] + came[half:]).astype(BF16)
            if stage == 0:
                high, late_units = lax.optimization_barrier((high, units))
                chosen, keep, own_gain, places = indices(late_units)
        came = across(high, halving, bits - 1)
        pieces = [gathered, sent]
        pieces += [lax.ppermute(piece, "rep", swap) for piece in pieces]
        came, *pieces = lax.optimization_barrier((came, *pieces))
        grad_own = low + came.astype(F32)
        projected = call(
            lambda *refs: project_kernel(dp_count, doubling, cap, *refs),
            6,
            project_shape,
            [SMEM_SPEC] + [VMEM_SPEC] * 4 + [any_spec] * 4,
            dense + [pltpu.VMEM((2, dp_count, part, LANES), BF16), pltpu.SemaphoreType.DMA((4,))],
            old_bounds,
            hidden_old,
            inv_rms,
            gain,
            hist,
            *pieces,
        )
    else:
        chip = owns[0]
        for away in range(1, rep_count):
            ring = [(r, (r + away) % rep_count) for r in range(rep_count)]
            chip = chip + lax.ppermute(others[0][away - 1], "rep", ring).astype(F32)
        blocks = lax.all_to_all(chip.astype(BF16), "dp", split_axis=0, concat_axis=0)
        grad_part = jnp.sum(blocks.astype(F32), axis=0)
        grad_own = lax.all_gather(grad_part, "rep", axis=0, tiled=True)
        chosen, keep, own_gain, places = indices(units)
        projected = call(
            lambda *refs: project_gathered_kernel(dp_count, cap, *refs),
            6,
            project_shape,
            [SMEM_SPEC] + [VMEM_SPEC] * 5,
            dense,
            old_bounds,
            hidden_old,
            inv_rms,
            gain,
            hist,
            weights,
        )

    message = (1 if staged else 2) * slots + 2 * table_rows
    message = (message + 7) // 8 * 8
    packed = call(
        lambda *refs: pack_kernel(dp_count, slots, table_rows, staged, *refs),
        3,
        shape((dp_count, message, LANES), BF16),
        [VMEM_SPEC] * 7,
        [],
        chosen,
        keep,
        own_gain,
        grad_own,
        weight_old,
        moment_first,
        moment_second,
    )
    moved = [lax.all_to_all(packed, "dp", split_axis=0, concat_axis=0)]
    if staged:
        arrived, projected = lax.optimization_barrier((moved[0], projected))
        moved = [arrived, lax.ppermute(arrived, "rep", swap)]
    rows = shape((new_cap, LANES), F32)
    gain_grad, first_next, second_next, adam_step = call(
        lambda *refs: finish_kernel(dp_count, slots, table_rows, staged, *refs),
        4,
        (shape((1, D_NEW), F32), rows, rows, rows),
        [SMEM_SPEC] * 3 + [VMEM_SPEC] * (1 + len(moved)),
        [pltpu.VMEM((dp_count * slots, LANES), F32)] * 2
        + [pltpu.VMEM((dp_count * table_rows, LANES), F32)],
        old_bounds,
        new_bounds,
        source_map,
        places,
        *moved,
    )
    return (projected, gain_grad.reshape(D_NEW), first_next, second_next, adam_step)


def solution(mesh):
    placed = (
        P(("dp", "rep"), None),
        P(("dp", "rep"), None),
        P(),
        P(),
        P(),
        P(),
        P("dp", None),
        P("dp", None),
        P("dp", None),
    )
    return jax.shard_map(
        on_device,
        mesh=mesh,
        in_specs=placed,
        out_specs=(P(("dp", "rep"), None), P(), P("dp", None), P("dp", None), P("dp", None)),
        check_vma=False,
    )
```

```python
import jax
import jax.numpy as jnp
from jax import lax
from jax.experimental import pallas as pl
from jax.experimental.pallas import tpu as pltpu
from jax.sharding import PartitionSpec as P

D_OLD = 6144
D_NEW = 8192
LANES = 128
BYTES_PER_US = 3_000_000
VMEM_LIMIT = 56 * 1024 * 1024
F32 = jnp.float32
BF16 = jnp.bfloat16

SMEM_SPEC = pl.BlockSpec(memory_space=pltpu.SMEM)
VMEM_SPEC = pl.BlockSpec(memory_space=pltpu.VMEM)


def dot(left, right, contract):
    return lax.dot_general(left, right, ((contract[:1], contract[1:]), ((), ())), preferred_element_type=F32)


def one_hot(rows, values):
    lanes = values.shape[1]
    match = lax.broadcasted_iota(jnp.int32, (rows, lanes), 0) == values
    return jnp.where(match, 1.0, 0.0).astype(BF16)


def split(value):
    high = value.astype(BF16)
    return high, (value - high.astype(F32)).astype(BF16)


def normed_tile(tile, hidden, inv_rms, gain, hist):
    stream = hidden[:, tile * LANES : (tile + 1) * LANES].astype(F32)
    normed = (stream * inv_rms) * gain[tile : tile + 1, :]
    return jnp.where(hist[tile : tile + 1, :] > 0.5, normed, 0.0).astype(BF16)


def lower_half(rows):
    return lax.broadcasted_iota(jnp.int32, (rows, LANES), 1) < LANES // 2


def token_kernel(rels, rep_count, cap, ob, src, gain, hidden_hbm, cot, hist, inv_out, *rest):
    *blocks, hidden, own_grads, other_grads, sem = rest
    owns, others = blocks[: len(blocks) // 2], blocks[len(blocks) // 2 :]
    copy = pltpu.make_async_copy(hidden_hbm, hidden, sem)
    copy.start()
    me = lax.axis_index("dp")
    rep = lax.axis_index("rep")
    tiles = D_OLD // LANES
    tokens = hidden.shape[0]
    step = 1024
    total = jnp.zeros((tiles, LANES), F32)
    for at in range(0, D_NEW, step):
        units = src[:, at : at + step]
        total = total + dot(one_hot(tiles, units >> 7), one_hot(LANES, units & 127), (1, 1))
    hist[...] = total
    copy.wait()
    squares = jnp.zeros((tokens, LANES), F32)
    for tile in range(tiles):
        stream = hidden[:, tile * LANES : (tile + 1) * LANES].astype(F32)
        squares = squares + stream * stream * hist[tile : tile + 1, :]
    inv_rms = lax.rsqrt(jnp.sum(squares, axis=1, keepdims=True) / D_NEW + 1e-05)
    inv_out[...] = jnp.broadcast_to(inv_rms, (tokens, LANES))
    staged = len(rels) > 1
    columns = cot[...]
    if staged:
        lower = lower_half(tokens)
        columns = columns.astype(F32)
        turned = pltpu.roll(columns, LANES // 2, 1)
        left, right = jnp.where(lower, columns, turned), jnp.where(lower, turned, columns)
        sides = [jnp.where(rep == 0, left, right), jnp.where(rep == 0, right, left)]
        columns = jnp.concatenate(sides, axis=1).astype(BF16)
    for tile in range(tiles):
        at = tile * LANES
        result = dot(normed_tile(tile, hidden, inv_rms, gain, hist), columns, (0, 0))
        own_grads[at : at + LANES, :] = result[:, :LANES]
        if staged:
            other_grads[at : at + LANES, :] = result[:, LANES:]
    own_grads[D_OLD:, :] = jnp.zeros((cap, LANES), F32)
    other_grads[D_OLD:, :] = jnp.zeros((cap, LANES), F32)
    dp_count = len(rels[0])
    half = dp_count // len(owns)
    part = cap // rep_count
    for at in range(dp_count):
        if staged:
            first = ob[holder_at(rels, rep, me, at)]
            owns[at // half][at % half] = packed_rows(own_grads, first, part)
            first = ob[holder_at(rels, 1 - rep, me, at)]
            others[at // half][0, at % half] = packed_rows(other_grads, first, part).astype(BF16)
        else:
            first = ob[at]
            owns[0][at] = own_grads[pl.ds(first + rep * part, part), :]
            for away in range(1, rep_count):
                mate = (rep + away) % rep_count
                others[0][away - 1, at] = own_grads[pl.ds(first + mate * part, part), :].astype(BF16)


def packed_rows(grads, first, part):
    return jnp.where(lower_half(part), grads[pl.ds(first, part), :], grads[pl.ds(first + part, part), :])


def holder_at(rels, rep, me, at):
    return me ^ jnp.where(rep == 0, rels[0][at], rels[1][at])


def fill_normed(x, hidden, inv_rms, gain, hist):
    for tile in range(D_OLD // LANES):
        x[:, tile * LANES : (tile + 1) * LANES] = normed_tile(tile, hidden, inv_rms[...], gain, hist)


def project_kernel(dp_count, orders, cap, ob, hidden, inv_rms, gain, hist, *rest):
    *pieces, out, dense, x, blocks, sems = rest
    me = lax.axis_index("dp")
    rep = lax.axis_index("rep")
    part = cap // 2
    half = dp_count // 2
    copies = []
    for at, piece in enumerate(pieces):
        side = rep if at < 2 else 1 - rep
        place = blocks.at[side, pl.ds((at % 2) * half, half)]
        copies.append(pltpu.make_async_copy(piece, place, sems.at[at]))
    for copy in copies:
        copy.start()
    fill_normed(x, hidden, inv_rms, gain, hist)
    for copy in copies:
        copy.wait()
    for p in range(dp_count):
        away = me ^ p
        for side, order in enumerate(orders):
            at = sum(((away >> bit) & 1) << s for s, bit in enumerate(order))
            dense[pl.ds(ob[p] + side * part, part), :] = blocks[side, at].astype(F32)
    out[...] = dot(x[...], dense[0:D_OLD, :].astype(BF16), (1, 0)).astype(BF16)


def project_gathered_kernel(dp_count, cap, ob, hidden, inv_rms, gain, hist, weights, out, dense, x):
    fill_normed(x, hidden, inv_rms, gain, hist)
    for p in range(dp_count):
        dense[pl.ds(ob[p], cap), :] = weights[p * cap : (p + 1) * cap, :].astype(F32)
    out[...] = dot(x[...], dense[0:D_OLD, :].astype(BF16), (1, 0)).astype(BF16)


def offset_of(src, ob, nb, q, dp_count):
    first = src[nb[q]]
    holder = jnp.int32(0)
    for p in range(1, dp_count):
        holder = holder + (ob[p] <= first).astype(jnp.int32)
    return holder


def index_kernel(dp_count, cap, slots, table_rows, ob, nb, src, gain, units, chosen, keep, own_gain, places, offset, rows, gains):
    me = lax.axis_index("dp")
    mine = ob[me]
    groups = cap // LANES
    offset[0] = offset_of(src, ob, nb, me, dp_count)
    rows[...] = jnp.full(rows.shape, -1, jnp.int32)
    for q in range(dp_count):
        start = nb[q] + ((me - offset_of(src, ob, nb, q, dp_count)) & (dp_count - 1))
        end = nb[q + 1]
        for k in range(slots):
            unit = start + dp_count * k
            row = jnp.where(unit < end, src[jnp.minimum(unit, D_NEW - 1)] - mine, -1)
            rows[q * slots + k : q * slots + k + 1, :] = jnp.full((1, LANES), row, jnp.int32)
    lanes = lax.broadcasted_iota(jnp.int32, rows.shape, 1)
    for g in range(groups):
        chosen[:, g * LANES : (g + 1) * LANES] = jnp.where(rows[...] == lanes + g * LANES, 1.0, 0.0).astype(BF16)
    gains[0 : gain.shape[0], :] = gain[...]
    gains[gain.shape[0] :, :] = jnp.ones((gains.shape[0] - gain.shape[0], LANES), F32)
    gain_rows = gains[pl.ds(mine >> 7, groups + 1), :]
    shift = mine & 127
    rolled = pltpu.roll(gain_rows, (LANES - shift) & 127, 1)
    lane_row = lax.broadcasted_iota(jnp.int32, (groups, LANES), 1)
    inverse = 1.0 / jnp.where(lane_row < LANES - shift, rolled[:groups], rolled[1:])
    for g in range(groups):
        own_gain[:, g * LANES : (g + 1) * LANES] = inverse[g : g + 1]
    same = dot(chosen[...], chosen[...], (1, 1))
    earlier = lax.broadcasted_iota(jnp.int32, same.shape, 0) < lax.broadcasted_iota(jnp.int32, same.shape, 1)
    repeated = jnp.max(jnp.where(earlier, same, 0.0), axis=0, keepdims=True)
    keep[...] = jnp.where(repeated < 0.5, 1.0, 0.0)
    step = 1024
    for first in range(0, D_NEW, step):
        source = units[:, first : first + step]
        position = first + lax.broadcasted_iota(jnp.int32, (1, step), 1)
        holder = jnp.zeros((1, step), jnp.int32)
        dest = jnp.zeros((1, step), jnp.int32)
        begin = jnp.zeros((1, step), jnp.int32)
        for p in range(1, dp_count):
            holder = holder + jnp.where(source >= ob[p], 1, 0)
            past = position >= nb[p]
            dest = jnp.where(past, p, dest)
            begin = jnp.where(past, nb[p], begin)
        rank = (position - begin) >> (dp_count.bit_length() - 1)
        places[:, first : first + step] = holder * (table_rows * LANES) + dest * slots + rank


def pack_kernel(dp_count, slots, table_rows, staged, chosen, keep, own_gain, *rest):
    *reduced, weight_in, first_in, second_in, out = rest
    pairs = dp_count * slots
    rows = weight_in.shape[0]
    weight, first, second = weight_in[...].astype(F32), first_in[...], second_in[...]
    if staged:
        turn = LANES // 2
        lower = lower_half(rows)
        grad = reduced[0][0] + reduced[1][0].astype(F32)
        grad = jnp.concatenate([grad, pltpu.roll(grad, turn, 1)], axis=0)
        left = lax.axis_index("rep") == 0
        weight, first, second = [
            jnp.where(left, value, pltpu.roll(value, turn, 1)) for value in (weight, first, second)
        ]
        product = jnp.where(lower, weight * grad, 0.0)
    else:
        grad = reduced[0][...]
        product = weight * grad
    high, low = split(product)
    ones = jnp.ones((8, LANES), BF16)
    column = (dot(ones, high, (1, 1)) + dot(ones, low, (1, 1))) * own_gain[...]
    picked = dot(jnp.concatenate(split(column), axis=0), chosen[...], (1, 1))
    table = []
    for part in (picked[0:1], picked[8:9]):
        part = part * keep[...]
        table += [part[:, r * LANES : (r + 1) * LANES] for r in range(table_rows)]
    updated = [0.9 * first + 0.1 * grad, 0.95 * second + 0.05 * grad * grad]
    if staged:
        updated = [jnp.where(lower, updated[0], pltpu.roll(updated[1], turn, 1))]
    filled = len(updated) * slots
    spare = out.shape[1] - filled - 2 * table_rows
    table = jnp.concatenate(table + [jnp.zeros((spare, LANES), F32)], axis=0).astype(BF16)
    picked = chosen[0:pairs]
    for at, value in enumerate(updated):
        moved = dot(picked, value.astype(BF16), (1, 0)).astype(BF16).reshape(dp_count, slots, LANES)
        out[:, at * slots : (at + 1) * slots, :] = moved
    for q in range(dp_count):
        out[q, filled:, :] = table


def finish_kernel(dp_count, slots, table_rows, staged, nb, offset_in, places, *rest):
    arrived, rest = (rest[:2], rest[2:]) if staged else (rest[:1], rest[1:])
    gain_grad, first, second, adam, ones, twos, table = rest
    me = lax.axis_index("dp")
    offset = offset_in[0]
    groups = 1 if staged else 2
    pages = [(moved, 0) for moved in arrived] if staged else [(arrived[0], 0), (arrived[0], slots)]
    for i in range(dp_count):
        p = (i + offset) & (dp_count - 1)
        strided = pl.ds(i, slots, stride=dp_count)
        for (moved, at), rows in zip(pages, (ones, twos)):
            rows[strided, :] = moved[p, at : at + slots, :].astype(F32)
    cap = first.shape[0]
    live = lax.broadcasted_iota(jnp.int32, (cap, LANES), 0) < nb[me + 1] - nb[me]
    one, two = ones[0:cap, :], twos[0:cap, :]
    if staged:
        left = lax.axis_index("rep") == 0
        lower = lower_half(cap)
        one, two = jnp.where(left, one, two), jnp.where(left, two, one)
        turn = LANES // 2
        one, two = (
            jnp.where(lower, one, pltpu.roll(two, turn, 1)),
            jnp.where(lower, pltpu.roll(one, turn, 1), two),
        )
    first_next = jnp.where(live, one, 0.0)
    second_next = jnp.where(live, two, 0.0)
    first[...] = first_next
    second[...] = second_next
    adam[...] = first_next / (jnp.sqrt(second_next) + 1e-08)
    at = groups * slots
    for p in range(dp_count):
        here = p * table_rows
        terms = [
            moved[p, at + r : at + r + table_rows, :].astype(F32) for moved in arrived for r in (0, table_rows)
        ]
        table[here : here + table_rows, :] = sum(terms[1:], terms[0])
    high, low = split(table[...])
    values = jnp.concatenate([high.astype(F32).T, low.astype(F32).T], axis=0).astype(BF16)
    step = 1024
    for start in range(0, D_NEW, step):
        slot = places[:, start : start + step]
        spread = dot(values, one_hot(values.shape[1], slot >> 7), (1, 0))
        mask = lax.broadcasted_iota(jnp.int32, (LANES, step), 0) == (slot & 127)
        value = jnp.where(mask, spread[:LANES] + spread[LANES:], 0.0)
        gain_grad[:, start : start + step] = jnp.sum(value, axis=0, keepdims=True)


def resident(value):
    return pltpu.with_memory_space_constraint(value, pltpu.VMEM)


def call(kernel, micros, out_shape, specs, scratch, *args):
    scalars = jax.ShapeDtypeStruct((1,), jnp.int32)
    out_specs = jax.tree.map(lambda out: SMEM_SPEC if out == scalars else VMEM_SPEC, out_shape)
    return pl.pallas_call(
        kernel,
        out_shape=out_shape,
        in_specs=specs,
        out_specs=out_specs,
        scratch_shapes=scratch,
        cost_estimate=pl.CostEstimate(flops=0, transcendentals=0, bytes_accessed=micros * BYTES_PER_US),
        compiler_params=pltpu.CompilerParams(vmem_limit_bytes=VMEM_LIMIT),
    )(*args)


def on_device(
    hidden_old,
    cotangent,
    gain_old,
    old_bounds,
    new_bounds,
    source_map,
    weight_old,
    moment_first,
    moment_second,
):
    dp_count = lax.axis_size("dp")
    rep_count = lax.axis_size("rep")
    cap = weight_old.shape[0]
    mean = D_NEW // dp_count
    new_cap = mean + mean // 4
    slots = (new_cap + dp_count - 1) // dp_count
    table_rows = (dp_count * slots + LANES - 1) // LANES
    tokens = hidden_old.shape[0]
    part = cap // rep_count
    shape = jax.ShapeDtypeStruct

    units = source_map.reshape(1, D_NEW)
    gain = gain_old.reshape(D_OLD // LANES, LANES)
    staged = rep_count == 2 and dp_count >= 4
    bits = dp_count.bit_length() - 1
    line = list(range(bits - 1))
    halving = [line + [bits - 1], line[::-1] + [bits - 1]]
    doubling = [[bits - 1] + line, [bits - 1] + line[::-1]]
    if staged:
        rels = [
            [sum(((at >> (bits - 1 - s)) & 1) << bit for s, bit in enumerate(order)) for at in range(dp_count)]
            for order in halving
        ]
        parts = 2
    else:
        rels = [list(range(dp_count))]
        parts = 1

    def across(value, orders, stage):
        pairs = [
            (dp * rep_count + rep, (dp ^ (1 << orders[rep][stage])) * rep_count + rep)
            for dp in range(dp_count)
            for rep in range(rep_count)
        ]
        return lax.ppermute(value, ("dp", "rep"), pairs)

    swap = [(0, 1), (1, 0)]
    any_spec = pl.BlockSpec(memory_space=pl.ANY)
    if staged:
        gathered = lax.dynamic_slice_in_dim(weight_old, lax.axis_index("rep") * part, part)[None]
        sent = across(gathered, doubling, 0)
    else:
        weights = lax.all_gather(weight_old, "dp", axis=0, tiled=True)

    tiles = D_OLD // LANES
    hist, inv_rms, *blocks = call(
        lambda *refs: token_kernel(rels, rep_count, cap, *refs),
        8,
        (
            shape((tiles, LANES), F32),
            shape((tokens, LANES), F32),
            *[pltpu.VMEM((dp_count // parts, part, LANES), F32)] * parts,
            *[pltpu.VMEM((rep_count - 1, dp_count // parts, part, LANES), BF16)] * parts,
        ),
        [SMEM_SPEC] + [VMEM_SPEC] * 2 + [any_spec] + [VMEM_SPEC],
        [
            pltpu.VMEM((tokens, D_OLD), BF16),
            pltpu.VMEM((D_OLD + cap, LANES), F32),
            pltpu.VMEM((D_OLD + cap, LANES), F32),
            pltpu.SemaphoreType.DMA(()),
        ],
        old_bounds,
        units,
        gain,
        hidden_old,
        cotangent,
    )
    owns, others = blocks[:parts], blocks[parts:]
    def indices(units):
        return call(
            lambda *refs: index_kernel(dp_count, cap, slots, table_rows, *refs),
            5,
            (
                pltpu.VMEM((table_rows * LANES, cap), BF16),
                pltpu.VMEM((1, table_rows * LANES), F32),
                pltpu.VMEM((1, cap), F32),
                pltpu.VMEM((1, D_NEW), jnp.int32),
                shape((1,), jnp.int32),
            ),
            [SMEM_SPEC] * 3 + [VMEM_SPEC] * 2,
            [pltpu.VMEM((table_rows * LANES, LANES), jnp.int32), pltpu.VMEM((D_OLD // LANES + 8, LANES), F32)],
            old_bounds,
            new_bounds,
            source_map,
            gain,
            units,
        )

    project_shape = shape((tokens, LANES), BF16)
    dense = [pltpu.VMEM((D_OLD + cap, LANES), F32), pltpu.VMEM((tokens, D_OLD), BF16)]
    if staged:
        half = dp_count // 2
        send, sent = lax.optimization_barrier((others[1][0], sent))
        gathered = jnp.concatenate([gathered, sent])
        sent = across(gathered, doubling, 1)
        high = (owns[1] + lax.ppermute(send, "rep", swap).astype(F32)).astype(BF16)
        low = owns[0] + lax.ppermute(others[0][0], "rep", swap).astype(F32)
        high, sent = lax.optimization_barrier((high, sent))
        for stage in range(bits - 1):
            came = across(high, halving, stage)
            if stage < bits - 2:
                gathered = jnp.concatenate([gathered, sent])
                sent = across(gathered, doubling, stage + 2)
                came, sent = lax.optimization_barrier((came, sent))
            if stage == 1:
                came, chosen = lax.optimization_barrier((came, chosen))
            came = came.astype(F32)
            half = half // 2
            low, high = low[:half] + came[:half], (low[half:] + came[half:]).astype(BF16)
            if stage == 0:
                high, late_units = lax.optimization_barrier((high, units))
                chosen, keep, own_gain, places, offset = indices(late_units)
        came = across(high, halving, bits - 1)
        pieces = [gathered, sent]
        pieces += [lax.ppermute(piece, "rep", swap) for piece in pieces]
        came, *pieces = lax.optimization_barrier((came, *pieces))
        reduced = [resident(low), resident(came)]
        projected = call(
            lambda *refs: project_kernel(dp_count, doubling, cap, *refs),
            6,
            project_shape,
            [SMEM_SPEC] + [VMEM_SPEC] * 4 + [any_spec] * 4,
            dense + [pltpu.VMEM((2, dp_count, part, LANES), BF16), pltpu.SemaphoreType.DMA((4,))],
            old_bounds,
            hidden_old,
            inv_rms,
            gain,
            hist,
            *pieces,
        )
    else:
        chip = owns[0]
        for away in range(1, rep_count):
            ring = [(r, (r + away) % rep_count) for r in range(rep_count)]
            chip = chip + lax.ppermute(others[0][away - 1], "rep", ring).astype(F32)
        blocks = lax.all_to_all(chip.astype(BF16), "dp", split_axis=0, concat_axis=0)
        grad_part = jnp.sum(blocks.astype(F32), axis=0)
        reduced = [lax.all_gather(grad_part, "rep", axis=0, tiled=True)]
        chosen, keep, own_gain, places, offset = indices(units)
        projected = call(
            lambda *refs: project_gathered_kernel(dp_count, cap, *refs),
            6,
            project_shape,
            [SMEM_SPEC] + [VMEM_SPEC] * 5,
            dense,
            old_bounds,
            hidden_old,
            inv_rms,
            gain,
            hist,
            weights,
        )

    message = (1 if staged else 2) * slots + 2 * table_rows
    message = (message + 7) // 8 * 8
    packed = call(
        lambda *refs: pack_kernel(dp_count, slots, table_rows, staged, *refs),
        3,
        pltpu.VMEM((dp_count, message, LANES), BF16),
        [VMEM_SPEC] * (6 + len(reduced)),
        [],
        *[resident(value) for value in (chosen, keep, own_gain)],
        *reduced,
        *[resident(value) for value in (weight_old, moment_first, moment_second)],
    )
    moved = [lax.all_to_all(packed, "dp", split_axis=0, concat_axis=0)]
    if staged:
        arrived, projected = lax.optimization_barrier((moved[0], projected))
        moved = [arrived, lax.ppermute(arrived, "rep", swap)]
        moved = [resident(value) for value in moved]
    rows = shape((new_cap, LANES), F32)
    gain_grad, first_next, second_next, adam_step = call(
        lambda *refs: finish_kernel(dp_count, slots, table_rows, staged, *refs),
        4,
        (shape((1, D_NEW), F32), rows, rows, rows),
        [SMEM_SPEC] * 2 + [VMEM_SPEC] * (1 + len(moved)),
        [pltpu.VMEM((dp_count * slots, LANES), F32)] * 2
        + [pltpu.VMEM((dp_count * table_rows, LANES), F32)],
        new_bounds,
        offset,
        resident(places),
        *moved,
    )
    return (projected, gain_grad.reshape(D_NEW), first_next, second_next, adam_step)


def solution(mesh):
    placed = (
        P(("dp", "rep"), None),
        P(("dp", "rep"), None),
        P(),
        P(),
        P(),
        P(),
        P("dp", None),
        P("dp", None),
        P("dp", None),
    )
    return jax.shard_map(
        on_device,
        mesh=mesh,
        in_specs=placed,
        out_specs=(P(("dp", "rep"), None), P(), P("dp", None), P("dp", None), P("dp", None)),
        check_vma=False,
    )
```

```python
import jax
import jax.numpy as jnp
from jax import lax
from jax.experimental import pallas as pl
from jax.experimental.pallas import tpu as pltpu
from jax.sharding import PartitionSpec as P

D_OLD = 6144
D_NEW = 8192
LANES = 128
BYTES_PER_US = 3_000_000
VMEM_LIMIT = 56 * 1024 * 1024
F32 = jnp.float32
BF16 = jnp.bfloat16

SMEM_SPEC = pl.BlockSpec(memory_space=pltpu.SMEM)
VMEM_SPEC = pl.BlockSpec(memory_space=pltpu.VMEM)


def dot(left, right, contract):
    return lax.dot_general(left, right, ((contract[:1], contract[1:]), ((), ())), preferred_element_type=F32)


def one_hot(rows, values):
    lanes = values.shape[1]
    match = lax.broadcasted_iota(jnp.int32, (rows, lanes), 0).astype(BF16) == values.astype(BF16)
    return jnp.where(match, jnp.ones((), BF16), jnp.zeros((), BF16))


def split(value):
    high = value.astype(BF16)
    return high, (value - high.astype(F32)).astype(BF16)


def normed_tile(tile, hidden, inv_rms, gain):
    stream = hidden[:, tile * LANES : (tile + 1) * LANES].astype(F32)
    return ((stream * inv_rms) * gain[tile : tile + 1, :]).astype(BF16)


def lower_half(rows):
    return lax.broadcasted_iota(jnp.int32, (rows, LANES), 1) < LANES // 2


def token_kernel(rels, rep_count, cap, ob, src, gain, hidden_hbm, cot, live_gain, inv_out, *rest):
    *blocks, hist, hidden, own_grads, other_grads, sem = rest
    owns, others = blocks[: len(blocks) // 2], blocks[len(blocks) // 2 :]
    copy = pltpu.make_async_copy(hidden_hbm, hidden, sem)
    copy.start()
    me = lax.axis_index("dp")
    rep = lax.axis_index("rep")
    tiles = D_OLD // LANES
    tokens = hidden.shape[0]
    step = 1024
    total = jnp.zeros((tiles, LANES), F32)
    for at in range(0, D_NEW, step):
        units = src[:, at : at + step]
        total = total + dot(one_hot(tiles, units >> 7), one_hot(LANES, units & 127), (1, 1))
    hist[...] = total
    live_gain[...] = jnp.where(total > 0.5, gain[...], 0.0)
    copy.wait()
    squares = jnp.zeros((tokens, LANES), F32)
    for tile in range(tiles):
        stream = hidden[:, tile * LANES : (tile + 1) * LANES].astype(F32)
        squares = squares + stream * stream * hist[tile : tile + 1, :]
    inv_rms = lax.rsqrt(jnp.sum(squares, axis=1, keepdims=True) / D_NEW + 1e-05)
    inv_out[...] = jnp.broadcast_to(inv_rms, (tokens, LANES))
    staged = len(rels) > 1
    columns = cot[...]
    if staged:
        lower = lower_half(tokens)
        columns = columns.astype(F32)
        turned = pltpu.roll(columns, LANES // 2, 1)
        left, right = jnp.where(lower, columns, turned), jnp.where(lower, turned, columns)
        sides = [jnp.where(rep == 0, left, right), jnp.where(rep == 0, right, left)]
        columns = jnp.concatenate(sides, axis=1).astype(BF16)
    for tile in range(tiles):
        at = tile * LANES
        result = dot(normed_tile(tile, hidden, inv_rms, live_gain), columns, (0, 0))
        own_grads[at : at + LANES, :] = result[:, :LANES]
        if staged:
            other_grads[at : at + LANES, :] = result[:, LANES:]
    own_grads[D_OLD:, :] = jnp.zeros((cap, LANES), F32)
    other_grads[D_OLD:, :] = jnp.zeros((cap, LANES), F32)
    dp_count = len(rels[0])
    half = dp_count // len(owns)
    part = cap // rep_count
    for at in range(dp_count):
        if staged:
            first = ob[holder_at(rels, rep, me, at)]
            owns[at // half][at % half] = packed_rows(own_grads, first, part)
            first = ob[holder_at(rels, 1 - rep, me, at)]
            others[at // half][0, at % half] = packed_rows(other_grads, first, part).astype(BF16)
        else:
            first = ob[at]
            owns[0][at] = own_grads[pl.ds(first + rep * part, part), :]
            for away in range(1, rep_count):
                mate = (rep + away) % rep_count
                others[0][away - 1, at] = own_grads[pl.ds(first + mate * part, part), :].astype(BF16)


def packed_rows(grads, first, part):
    return jnp.where(lower_half(part), grads[pl.ds(first, part), :], grads[pl.ds(first + part, part), :])


def holder_at(rels, rep, me, at):
    return me ^ jnp.where(rep == 0, rels[0][at], rels[1][at])


def fill_normed(x, hidden, inv_rms, gain):
    for tile in range(D_OLD // LANES):
        x[:, tile * LANES : (tile + 1) * LANES] = normed_tile(tile, hidden, inv_rms[...], gain)


def project_kernel(dp_count, orders, cap, ob, hidden, inv_rms, gain, *rest):
    *pieces, out, dense, x, blocks, sems = rest
    me = lax.axis_index("dp")
    rep = lax.axis_index("rep")
    part = cap // 2
    half = dp_count // 2
    copies = []
    for at, piece in enumerate(pieces):
        side = rep if at < 2 else 1 - rep
        place = blocks.at[side, pl.ds((at % 2) * half, half)]
        copies.append(pltpu.make_async_copy(piece, place, sems.at[at]))
    for copy in copies:
        copy.start()
    fill_normed(x, hidden, inv_rms, gain)
    for copy in copies:
        copy.wait()
    for p in range(dp_count):
        away = me ^ p
        for side, order in enumerate(orders):
            at = sum(((away >> bit) & 1) << s for s, bit in enumerate(order))
            dense[pl.ds(ob[p] + side * part, part), :] = blocks[side, at].astype(F32)
    out[...] = dot(x[...], dense[0:D_OLD, :].astype(BF16), (1, 0)).astype(BF16)


def project_gathered_kernel(dp_count, cap, ob, hidden, inv_rms, gain, weights, out, dense, x):
    fill_normed(x, hidden, inv_rms, gain)
    for p in range(dp_count):
        dense[pl.ds(ob[p], cap), :] = weights[p * cap : (p + 1) * cap, :].astype(F32)
    out[...] = dot(x[...], dense[0:D_OLD, :].astype(BF16), (1, 0)).astype(BF16)


def offset_of(src, ob, nb, q, dp_count):
    first = src[nb[q]]
    holder = jnp.int32(0)
    for p in range(1, dp_count):
        holder = holder + (ob[p] <= first).astype(jnp.int32)
    return holder


def index_kernel(dp_count, cap, slots, table_rows, ob, nb, src, gain, units, chosen, keep, own_gain, places, tables, offset, rows, gains):
    me = lax.axis_index("dp")
    mine = ob[me]
    groups = cap // LANES
    offset[0] = offset_of(src, ob, nb, me, dp_count)
    rows[...] = jnp.full(rows.shape, -1, jnp.int32)
    for q in range(dp_count):
        start = nb[q] + ((me - offset_of(src, ob, nb, q, dp_count)) & (dp_count - 1))
        end = nb[q + 1]
        for k in range(slots):
            unit = start + dp_count * k
            row = jnp.where(unit < end, src[jnp.minimum(unit, D_NEW - 1)] - mine, -1)
            rows[q * slots + k : q * slots + k + 1, :] = jnp.full((1, LANES), row, jnp.int32)
    lanes = lax.broadcasted_iota(jnp.int32, rows.shape, 1)
    for g in range(groups):
        chosen[:, g * LANES : (g + 1) * LANES] = jnp.where(rows[...] == lanes + g * LANES, 1.0, 0.0).astype(BF16)
    gains[0 : gain.shape[0], :] = gain[...]
    gains[gain.shape[0] :, :] = jnp.ones((gains.shape[0] - gain.shape[0], LANES), F32)
    gain_rows = gains[pl.ds(mine >> 7, groups + 1), :]
    shift = mine & 127
    rolled = pltpu.roll(gain_rows, (LANES - shift) & 127, 1)
    lane_row = lax.broadcasted_iota(jnp.int32, (groups, LANES), 1)
    inverse = 1.0 / jnp.where(lane_row < LANES - shift, rolled[:groups], rolled[1:])
    for g in range(groups):
        own_gain[:, g * LANES : (g + 1) * LANES] = inverse[g : g + 1]
    same = dot(chosen[...], chosen[...], (1, 1))
    earlier = lax.broadcasted_iota(jnp.int32, same.shape, 0) < lax.broadcasted_iota(jnp.int32, same.shape, 1)
    repeated = jnp.max(jnp.where(earlier, same, 0.0), axis=0, keepdims=True)
    keep[...] = jnp.where(repeated < 0.5, 1.0, 0.0)
    step = 1024
    for first in range(0, D_NEW, step):
        source = units[:, first : first + step]
        position = first + lax.broadcasted_iota(jnp.int32, (1, step), 1)
        holder = jnp.zeros((1, step), jnp.int32)
        dest = jnp.zeros((1, step), jnp.int32)
        begin = jnp.zeros((1, step), jnp.int32)
        for p in range(1, dp_count):
            holder = holder + jnp.where(source >= ob[p], 1, 0)
            past = position >= nb[p]
            dest = jnp.where(past, p, dest)
            begin = jnp.where(past, nb[p], begin)
        rank = (position - begin) >> (dp_count.bit_length() - 1)
        place = holder * (table_rows * LANES) + dest * slots + rank
        places[:, first : first + step] = place & 127
        spread = one_hot(dp_count * table_rows, place >> 7)
        tables[:, first : first + step] = jnp.concatenate([spread, spread], axis=0)


def pack_kernel(dp_count, slots, table_rows, staged, chosen, keep, own_gain, *rest):
    *reduced, weight_in, first_in, second_in, out = rest
    pairs = dp_count * slots
    rows = weight_in.shape[0]
    weight, first, second = weight_in[...].astype(F32), first_in[...], second_in[...]
    if staged:
        turn = LANES // 2
        lower = lower_half(rows)
        grad = reduced[0][0] + reduced[1][0].astype(F32)
        grad = jnp.concatenate([grad, pltpu.roll(grad, turn, 1)], axis=0)
        left = lax.axis_index("rep") == 0
        weight, first, second = [
            jnp.where(left, value, pltpu.roll(value, turn, 1)) for value in (weight, first, second)
        ]
        product = jnp.where(lower, weight * grad, 0.0)
    else:
        grad = reduced[0][...]
        product = weight * grad
    high, low = split(product)
    ones = jnp.ones((8, LANES), BF16)
    column = (dot(ones, high, (1, 1)) + dot(ones, low, (1, 1))) * own_gain[...]
    picked = dot(jnp.concatenate(split(column), axis=0), chosen[...], (1, 1))
    table = []
    for part in (picked[0:1], picked[8:9]):
        part = part * keep[...]
        table += [part[:, r * LANES : (r + 1) * LANES] for r in range(table_rows)]
    updated = [0.9 * first + 0.1 * grad, 0.95 * second + 0.05 * grad * grad]
    if staged:
        updated = [jnp.where(lower, updated[0], pltpu.roll(updated[1], turn, 1))]
    filled = len(updated) * slots
    spare = out.shape[1] - filled - 2 * table_rows
    table = jnp.concatenate(table + [jnp.zeros((spare, LANES), F32)], axis=0).astype(BF16)
    picked = chosen[0:pairs]
    for at, value in enumerate(updated):
        moved = dot(picked, value.astype(BF16), (1, 0)).astype(BF16).reshape(dp_count, slots, LANES)
        out[:, at * slots : (at + 1) * slots, :] = moved
    for q in range(dp_count):
        out[q, filled:, :] = table


def finish_kernel(dp_count, slots, table_rows, staged, nb, offset_in, places, tables, *rest):
    arrived, rest = (rest[:2], rest[2:]) if staged else (rest[:1], rest[1:])
    gain_grad, first, second, adam, ones, twos, table = rest
    me = lax.axis_index("dp")
    offset = offset_in[0]
    groups = 1 if staged else 2
    pages = [(moved, 0) for moved in arrived] if staged else [(arrived[0], 0), (arrived[0], slots)]
    for i in range(dp_count):
        p = (i + offset) & (dp_count - 1)
        strided = pl.ds(i, slots, stride=dp_count)
        for (moved, at), rows in zip(pages, (ones, twos)):
            rows[strided, :] = moved[p, at : at + slots, :].astype(F32)
    cap = first.shape[0]
    live = lax.broadcasted_iota(jnp.int32, (cap, LANES), 0) < nb[me + 1] - nb[me]
    one, two = ones[0:cap, :], twos[0:cap, :]
    if staged:
        left = lax.axis_index("rep") == 0
        lower = lower_half(cap)
        one, two = jnp.where(left, one, two), jnp.where(left, two, one)
        turn = LANES // 2
        one, two = (
            jnp.where(lower, one, pltpu.roll(two, turn, 1)),
            jnp.where(lower, pltpu.roll(one, turn, 1), two),
        )
    first_next = jnp.where(live, one, 0.0)
    second_next = jnp.where(live, two, 0.0)
    first[...] = first_next
    second[...] = second_next
    adam[...] = first_next / (jnp.sqrt(second_next) + 1e-08)
    at = groups * slots
    for p in range(dp_count):
        here = p * table_rows
        terms = [
            moved[p, at + r : at + r + table_rows, :].astype(F32) for moved in arrived for r in (0, table_rows)
        ]
        table[here : here + table_rows, :] = sum(terms[1:], terms[0])
    high, low = split(table[...])
    values = jnp.concatenate([high.astype(F32), low.astype(F32)], axis=0).T.astype(BF16)
    step = 1024
    for start in range(0, D_NEW, step):
        spread = dot(values, tables[:, start : start + step], (1, 0))
        mask = lax.broadcasted_iota(jnp.int32, (LANES, step), 0) == places[:, start : start + step]
        value = jnp.where(mask, spread, 0.0)
        gain_grad[:, start : start + step] = jnp.sum(value, axis=0, keepdims=True)


def resident(value):
    return pltpu.with_memory_space_constraint(value, pltpu.VMEM)


def call(kernel, micros, out_shape, specs, scratch, *args):
    scalars = jax.ShapeDtypeStruct((1,), jnp.int32)
    out_specs = jax.tree.map(lambda out: SMEM_SPEC if out == scalars else VMEM_SPEC, out_shape)
    return pl.pallas_call(
        kernel,
        out_shape=out_shape,
        in_specs=specs,
        out_specs=out_specs,
        scratch_shapes=scratch,
        cost_estimate=pl.CostEstimate(flops=0, transcendentals=0, bytes_accessed=micros * BYTES_PER_US),
        compiler_params=pltpu.CompilerParams(vmem_limit_bytes=VMEM_LIMIT),
    )(*args)


def on_device(
    hidden_old,
    cotangent,
    gain_old,
    old_bounds,
    new_bounds,
    source_map,
    weight_old,
    moment_first,
    moment_second,
):
    dp_count = lax.axis_size("dp")
    rep_count = lax.axis_size("rep")
    cap = weight_old.shape[0]
    mean = D_NEW // dp_count
    new_cap = mean + mean // 4
    slots = (new_cap + dp_count - 1) // dp_count
    table_rows = (dp_count * slots + LANES - 1) // LANES
    tokens = hidden_old.shape[0]
    part = cap // rep_count
    shape = jax.ShapeDtypeStruct

    units = source_map.reshape(1, D_NEW)
    gain = gain_old.reshape(D_OLD // LANES, LANES)
    staged = rep_count == 2 and dp_count >= 4
    bits = dp_count.bit_length() - 1
    line = list(range(bits - 1))
    halving = [line + [bits - 1], line[::-1] + [bits - 1]]
    doubling = [[bits - 1] + line, [bits - 1] + line[::-1]]
    if staged:
        rels = [
            [sum(((at >> (bits - 1 - s)) & 1) << bit for s, bit in enumerate(order)) for at in range(dp_count)]
            for order in halving
        ]
        parts = 2
    else:
        rels = [list(range(dp_count))]
        parts = 1

    def across(value, orders, stage):
        pairs = [
            (dp * rep_count + rep, (dp ^ (1 << orders[rep][stage])) * rep_count + rep)
            for dp in range(dp_count)
            for rep in range(rep_count)
        ]
        return lax.ppermute(value, ("dp", "rep"), pairs)

    swap = [(0, 1), (1, 0)]
    any_spec = pl.BlockSpec(memory_space=pl.ANY)
    if staged:
        gathered = lax.dynamic_slice_in_dim(weight_old, lax.axis_index("rep") * part, part)[None]
        sent = across(gathered, doubling, 0)
    else:
        weights = lax.all_gather(weight_old, "dp", axis=0, tiled=True)

    tiles = D_OLD // LANES
    live_gain, inv_rms, *blocks = call(
        lambda *refs: token_kernel(rels, rep_count, cap, *refs),
        8,
        (
            shape((tiles, LANES), F32),
            shape((tokens, LANES), F32),
            *[pltpu.VMEM((dp_count // parts, part, LANES), F32)] * parts,
            *[pltpu.VMEM((rep_count - 1, dp_count // parts, part, LANES), BF16)] * parts,
        ),
        [SMEM_SPEC] + [VMEM_SPEC] * 2 + [any_spec] + [VMEM_SPEC],
        [
            pltpu.VMEM((tiles, LANES), F32),
            pltpu.VMEM((tokens, D_OLD), BF16),
            pltpu.VMEM((D_OLD + cap, LANES), F32),
            pltpu.VMEM((D_OLD + cap, LANES), F32),
            pltpu.SemaphoreType.DMA(()),
        ],
        old_bounds,
        units,
        gain,
        hidden_old,
        cotangent,
    )
    owns, others = blocks[:parts], blocks[parts:]
    def indices(units):
        return call(
            lambda *refs: index_kernel(dp_count, cap, slots, table_rows, *refs),
            5,
            (
                pltpu.VMEM((table_rows * LANES, cap), BF16),
                pltpu.VMEM((1, table_rows * LANES), F32),
                pltpu.VMEM((1, cap), F32),
                pltpu.VMEM((1, D_NEW), jnp.int32),
                pltpu.VMEM((2 * dp_count * table_rows, D_NEW), BF16),
                shape((1,), jnp.int32),
            ),
            [SMEM_SPEC] * 3 + [VMEM_SPEC] * 2,
            [pltpu.VMEM((table_rows * LANES, LANES), jnp.int32), pltpu.VMEM((D_OLD // LANES + 8, LANES), F32)],
            old_bounds,
            new_bounds,
            source_map,
            gain,
            units,
        )

    project_shape = shape((tokens, LANES), BF16)
    dense = [pltpu.VMEM((D_OLD + cap, LANES), F32), pltpu.VMEM((tokens, D_OLD), BF16)]
    if staged:
        half = dp_count // 2
        send, sent = lax.optimization_barrier((others[1][0], sent))
        gathered = jnp.concatenate([gathered, sent])
        sent = across(gathered, doubling, 1)
        pair, gathered = lax.optimization_barrier((lax.ppermute(send, "rep", swap), gathered))
        high = (owns[1] + pair.astype(F32)).astype(BF16)
        low = owns[0] + lax.ppermute(others[0][0], "rep", swap).astype(F32)
        for stage in range(bits - 1):
            came = across(high, halving, stage)
            if stage < bits - 2:
                gathered = jnp.concatenate([gathered, sent])
                sent = across(gathered, doubling, stage + 2)
                came, sent = lax.optimization_barrier((came, sent))
            if stage == 1:
                came, chosen = lax.optimization_barrier((came, chosen))
            came = came.astype(F32)
            half = half // 2
            low, high = low[:half] + came[:half], (low[half:] + came[half:]).astype(BF16)
            if stage == 0:
                high, late_units = lax.optimization_barrier((high, units))
                chosen, keep, own_gain, places, tables, offset = indices(late_units)
        came = across(high, halving, bits - 1)
        pieces = [gathered, sent]
        pieces += [lax.ppermute(piece, "rep", swap) for piece in pieces]
        came, *pieces = lax.optimization_barrier((came, *pieces))
        reduced = [resident(low), resident(came)]
        projected = call(
            lambda *refs: project_kernel(dp_count, doubling, cap, *refs),
            6,
            project_shape,
            [SMEM_SPEC] + [VMEM_SPEC] * 3 + [any_spec] * 4,
            dense + [pltpu.VMEM((2, dp_count, part, LANES), BF16), pltpu.SemaphoreType.DMA((4,))],
            old_bounds,
            hidden_old,
            inv_rms,
            live_gain,
            *pieces,
        )
    else:
        chip = owns[0]
        for away in range(1, rep_count):
            ring = [(r, (r + away) % rep_count) for r in range(rep_count)]
            chip = chip + lax.ppermute(others[0][away - 1], "rep", ring).astype(F32)
        blocks = lax.all_to_all(chip.astype(BF16), "dp", split_axis=0, concat_axis=0)
        grad_part = jnp.sum(blocks.astype(F32), axis=0)
        reduced = [lax.all_gather(grad_part, "rep", axis=0, tiled=True)]
        chosen, keep, own_gain, places, tables, offset = indices(units)
        projected = call(
            lambda *refs: project_gathered_kernel(dp_count, cap, *refs),
            6,
            project_shape,
            [SMEM_SPEC] + [VMEM_SPEC] * 4,
            dense,
            old_bounds,
            hidden_old,
            inv_rms,
            live_gain,
            weights,
        )

    message = (1 if staged else 2) * slots + 2 * table_rows
    message = (message + 7) // 8 * 8
    packed = call(
        lambda *refs: pack_kernel(dp_count, slots, table_rows, staged, *refs),
        3,
        pltpu.VMEM((dp_count, message, LANES), BF16),
        [VMEM_SPEC] * (6 + len(reduced)),
        [],
        *[resident(value) for value in (chosen, keep, own_gain)],
        *reduced,
        *[resident(value) for value in (weight_old, moment_first, moment_second)],
    )
    moved = [lax.all_to_all(packed, "dp", split_axis=0, concat_axis=0)]
    if staged:
        arrived, projected = lax.optimization_barrier((moved[0], projected))
        moved = [arrived, lax.ppermute(arrived, "rep", swap)]
        moved = [resident(value) for value in moved]
    rows = shape((new_cap, LANES), F32)
    gain_grad, first_next, second_next, adam_step = call(
        lambda *refs: finish_kernel(dp_count, slots, table_rows, staged, *refs),
        4,
        (shape((1, D_NEW), F32), rows, rows, rows),
        [SMEM_SPEC] * 2 + [VMEM_SPEC] * (2 + len(moved)),
        [pltpu.VMEM((dp_count * slots, LANES), F32)] * 2
        + [pltpu.VMEM((dp_count * table_rows, LANES), F32)],
        new_bounds,
        offset,
        resident(places),
        resident(tables),
        *moved,
    )
    return (projected, gain_grad.reshape(D_NEW), first_next, second_next, adam_step)


def solution(mesh):
    placed = (
        P(("dp", "rep"), None),
        P(("dp", "rep"), None),
        P(),
        P(),
        P(),
        P(),
        P("dp", None),
        P("dp", None),
        P("dp", None),
    )
    return jax.shard_map(
        on_device,
        mesh=mesh,
        in_specs=placed,
        out_specs=(P(("dp", "rep"), None), P(), P("dp", None), P("dp", None), P("dp", None)),
        check_vma=False,
    )
```

```python
import jax
import jax.numpy as jnp
from jax import lax
from jax.experimental import pallas as pl
from jax.experimental.pallas import tpu as pltpu
from jax.sharding import PartitionSpec as P

D_OLD = 6144
D_NEW = 8192
LANES = 128
BYTES_PER_US = 3_000_000
VMEM_LIMIT = 56 * 1024 * 1024
F32 = jnp.float32
BF16 = jnp.bfloat16

SMEM_SPEC = pl.BlockSpec(memory_space=pltpu.SMEM)
VMEM_SPEC = pl.BlockSpec(memory_space=pltpu.VMEM)


def dot(left, right, contract):
    return lax.dot_general(left, right, ((contract[:1], contract[1:]), ((), ())), preferred_element_type=F32)


def one_hot(rows, values):
    lanes = values.shape[1]
    match = lax.broadcasted_iota(jnp.int32, (rows, lanes), 0).astype(BF16) == values.astype(BF16)
    return jnp.where(match, jnp.ones((), BF16), jnp.zeros((), BF16))


def split(value):
    high = value.astype(BF16)
    return high, (value - high.astype(F32)).astype(BF16)


def normed_tile(tile, hidden, inv_rms, gain):
    stream = hidden[:, tile * LANES : (tile + 1) * LANES].astype(F32)
    return ((stream * inv_rms) * gain[tile : tile + 1, :]).astype(BF16)


def lower_half(rows):
    return lax.broadcasted_iota(jnp.int32, (rows, LANES), 1) < LANES // 2


def token_kernel(rels, rep_count, cap, ob, src, gain, hidden_hbm, cot, live_gain, inv_out, *rest):
    *blocks, hist, hidden, own_grads, other_grads, sem = rest
    owns, others = blocks[: len(blocks) // 2], blocks[len(blocks) // 2 :]
    copy = pltpu.make_async_copy(hidden_hbm, hidden, sem)
    copy.start()
    me = lax.axis_index("dp")
    rep = lax.axis_index("rep")
    tiles = D_OLD // LANES
    tokens = hidden.shape[0]
    step = 1024
    total = jnp.zeros((tiles, LANES), F32)
    for at in range(0, D_NEW, step):
        units = src[:, at : at + step]
        total = total + dot(one_hot(tiles, units >> 7), one_hot(LANES, units & 127), (1, 1))
    hist[...] = total
    live_gain[...] = jnp.where(total > 0.5, gain[...], 0.0)
    copy.wait()
    squares = jnp.zeros((tokens, LANES), F32)
    for tile in range(tiles):
        stream = hidden[:, tile * LANES : (tile + 1) * LANES].astype(F32)
        squares = squares + stream * stream * hist[tile : tile + 1, :]
    inv_rms = lax.rsqrt(jnp.sum(squares, axis=1, keepdims=True) / D_NEW + 1e-05)
    inv_out[...] = jnp.broadcast_to(inv_rms, (tokens, LANES))
    staged = len(rels) > 1
    columns = cot[...]
    if staged:
        lower = lower_half(tokens)
        columns = columns.astype(F32)
        turned = pltpu.roll(columns, LANES // 2, 1)
        left, right = jnp.where(lower, columns, turned), jnp.where(lower, turned, columns)
        sides = [jnp.where(rep == 0, left, right), jnp.where(rep == 0, right, left)]
        columns = jnp.concatenate(sides, axis=1).astype(BF16)
    for tile in range(tiles):
        at = tile * LANES
        result = dot(normed_tile(tile, hidden, inv_rms, live_gain), columns, (0, 0))
        own_grads[at : at + LANES, :] = result[:, :LANES]
        if staged:
            other_grads[at : at + LANES, :] = result[:, LANES:]
    own_grads[D_OLD:, :] = jnp.zeros((cap, LANES), F32)
    other_grads[D_OLD:, :] = jnp.zeros((cap, LANES), F32)
    dp_count = len(rels[0])
    half = dp_count // len(owns)
    part = cap // rep_count
    for at in range(dp_count):
        if staged:
            first = ob[holder_at(rels, rep, me, at)]
            owns[at // half][at % half] = packed_rows(own_grads, first, part)
            first = ob[holder_at(rels, 1 - rep, me, at)]
            others[at // half][0, at % half] = packed_rows(other_grads, first, part).astype(BF16)
        else:
            first = ob[at]
            owns[0][at] = own_grads[pl.ds(first + rep * part, part), :]
            for away in range(1, rep_count):
                mate = (rep + away) % rep_count
                others[0][away - 1, at] = own_grads[pl.ds(first + mate * part, part), :].astype(BF16)


def packed_rows(grads, first, part):
    return jnp.where(lower_half(part), grads[pl.ds(first, part), :], grads[pl.ds(first + part, part), :])


def holder_at(rels, rep, me, at):
    return me ^ jnp.where(rep == 0, rels[0][at], rels[1][at])


def fill_normed(x, hidden, inv_rms, gain):
    for tile in range(D_OLD // LANES):
        x[:, tile * LANES : (tile + 1) * LANES] = normed_tile(tile, hidden, inv_rms[...], gain)


def project_kernel(dp_count, orders, cap, ob, hidden, inv_rms, gain, *rest):
    *pieces, out, dense, x, blocks, sems = rest
    me = lax.axis_index("dp")
    rep = lax.axis_index("rep")
    part = cap // 2
    half = dp_count // 2
    copies = []
    for at, piece in enumerate(pieces):
        side = rep if at < 2 else 1 - rep
        place = blocks.at[side, pl.ds((at % 2) * half, half)]
        copies.append(pltpu.make_async_copy(piece, place, sems.at[at]))
    for copy in copies:
        copy.start()
    fill_normed(x, hidden, inv_rms, gain)
    for copy in copies:
        copy.wait()
    for p in range(dp_count):
        away = me ^ p
        for side, order in enumerate(orders):
            at = sum(((away >> bit) & 1) << s for s, bit in enumerate(order))
            dense[pl.ds(ob[p] + side * part, part), :] = blocks[side, at].astype(F32)
    out[...] = dot(x[...], dense[0:D_OLD, :].astype(BF16), (1, 0)).astype(BF16)


def project_gathered_kernel(dp_count, cap, ob, hidden, inv_rms, gain, weights, out, dense, x):
    fill_normed(x, hidden, inv_rms, gain)
    for p in range(dp_count):
        dense[pl.ds(ob[p], cap), :] = weights[p * cap : (p + 1) * cap, :].astype(F32)
    out[...] = dot(x[...], dense[0:D_OLD, :].astype(BF16), (1, 0)).astype(BF16)


def offset_of(src, ob, nb, q, dp_count):
    first = src[nb[q]]
    holder = jnp.int32(0)
    for p in range(1, dp_count):
        holder = holder + (ob[p] <= first).astype(jnp.int32)
    return holder


def index_kernel(dp_count, cap, slots, table_rows, ob, nb, src, gain, chosen, keep, own_gain, offset, rows, gains):
    me = lax.axis_index("dp")
    mine = ob[me]
    groups = cap // LANES
    offset[0] = offset_of(src, ob, nb, me, dp_count)
    rows[...] = jnp.full(rows.shape, -1, jnp.int32)
    for q in range(dp_count):
        start = nb[q] + ((me - offset_of(src, ob, nb, q, dp_count)) & (dp_count - 1))
        end = nb[q + 1]
        for k in range(slots):
            unit = start + dp_count * k
            row = jnp.where(unit < end, src[jnp.minimum(unit, D_NEW - 1)] - mine, -1)
            rows[q * slots + k : q * slots + k + 1, :] = jnp.full((1, LANES), row, jnp.int32)
    lanes = lax.broadcasted_iota(jnp.int32, rows.shape, 1)
    for g in range(groups):
        chosen[:, g * LANES : (g + 1) * LANES] = jnp.where(rows[...] == lanes + g * LANES, 1.0, 0.0).astype(BF16)
    gains[0 : gain.shape[0], :] = gain[...]
    gains[gain.shape[0] :, :] = jnp.ones((gains.shape[0] - gain.shape[0], LANES), F32)
    gain_rows = gains[pl.ds(mine >> 7, groups + 1), :]
    shift = mine & 127
    rolled = pltpu.roll(gain_rows, (LANES - shift) & 127, 1)
    lane_row = lax.broadcasted_iota(jnp.int32, (groups, LANES), 1)
    inverse = 1.0 / jnp.where(lane_row < LANES - shift, rolled[:groups], rolled[1:])
    for g in range(groups):
        own_gain[:, g * LANES : (g + 1) * LANES] = inverse[g : g + 1]
    same = dot(chosen[...], chosen[...], (1, 1))
    earlier = lax.broadcasted_iota(jnp.int32, same.shape, 0) < lax.broadcasted_iota(jnp.int32, same.shape, 1)
    repeated = jnp.max(jnp.where(earlier, same, 0.0), axis=0, keepdims=True)
    keep[...] = jnp.where(repeated < 0.5, 1.0, 0.0)


def place_kernel(dp_count, slots, table_rows, ob, nb, units, places, tables):
    step = 1024
    for first in range(0, D_NEW, step):
        source = units[:, first : first + step]
        position = first + lax.broadcasted_iota(jnp.int32, (1, step), 1)
        holder = jnp.zeros((1, step), jnp.int32)
        dest = jnp.zeros((1, step), jnp.int32)
        begin = jnp.zeros((1, step), jnp.int32)
        for p in range(1, dp_count):
            holder = holder + jnp.where(source >= ob[p], 1, 0)
            past = position >= nb[p]
            dest = jnp.where(past, p, dest)
            begin = jnp.where(past, nb[p], begin)
        rank = (position - begin) >> (dp_count.bit_length() - 1)
        place = holder * (table_rows * LANES) + dest * slots + rank
        places[:, first : first + step] = place & 127
        spread = one_hot(dp_count * table_rows, place >> 7)
        tables[:, first : first + step] = jnp.concatenate([spread, spread], axis=0)


def pack_kernel(dp_count, slots, table_rows, staged, chosen, keep, own_gain, *rest):
    *reduced, weight_in, first_in, second_in, out = rest
    pairs = dp_count * slots
    rows = weight_in.shape[0]
    weight, first, second = weight_in[...].astype(F32), first_in[...], second_in[...]
    if staged:
        turn = LANES // 2
        lower = lower_half(rows)
        grad = reduced[0][0] + reduced[1][0].astype(F32)
        grad = jnp.concatenate([grad, pltpu.roll(grad, turn, 1)], axis=0)
        left = lax.axis_index("rep") == 0
        weight, first, second = [
            jnp.where(left, value, pltpu.roll(value, turn, 1)) for value in (weight, first, second)
        ]
        product = jnp.where(lower, weight * grad, 0.0)
    else:
        grad = reduced[0][...]
        product = weight * grad
    high, low = split(product)
    ones = jnp.ones((8, LANES), BF16)
    column = (dot(ones, high, (1, 1)) + dot(ones, low, (1, 1))) * own_gain[...]
    picked = dot(jnp.concatenate(split(column), axis=0), chosen[...], (1, 1))
    table = []
    for part in (picked[0:1], picked[8:9]):
        part = part * keep[...]
        table += [part[:, r * LANES : (r + 1) * LANES] for r in range(table_rows)]
    updated = [0.9 * first + 0.1 * grad, 0.95 * second + 0.05 * grad * grad]
    if staged:
        updated = [jnp.where(lower, updated[0], pltpu.roll(updated[1], turn, 1))]
    filled = len(updated) * slots
    spare = out.shape[1] - filled - 2 * table_rows
    table = jnp.concatenate(table + [jnp.zeros((spare, LANES), F32)], axis=0).astype(BF16)
    picked = chosen[0:pairs]
    for at, value in enumerate(updated):
        moved = dot(picked, value.astype(BF16), (1, 0)).astype(BF16).reshape(dp_count, slots, LANES)
        out[:, at * slots : (at + 1) * slots, :] = moved
    for q in range(dp_count):
        out[q, filled:, :] = table


def finish_kernel(dp_count, slots, table_rows, staged, nb, offset_in, places, tables, *rest):
    arrived, rest = (rest[:2], rest[2:]) if staged else (rest[:1], rest[1:])
    gain_grad, first, second, adam, ones, twos, table = rest
    me = lax.axis_index("dp")
    offset = offset_in[0]
    groups = 1 if staged else 2
    pages = [(moved, 0) for moved in arrived] if staged else [(arrived[0], 0), (arrived[0], slots)]
    for i in range(dp_count):
        p = (i + offset) & (dp_count - 1)
        strided = pl.ds(i, slots, stride=dp_count)
        for (moved, at), rows in zip(pages, (ones, twos)):
            rows[strided, :] = moved[p, at : at + slots, :].astype(F32)
    cap = first.shape[0]
    live = lax.broadcasted_iota(jnp.int32, (cap, LANES), 0) < nb[me + 1] - nb[me]
    one, two = ones[0:cap, :], twos[0:cap, :]
    if staged:
        left = lax.axis_index("rep") == 0
        lower = lower_half(cap)
        one, two = jnp.where(left, one, two), jnp.where(left, two, one)
        turn = LANES // 2
        one, two = (
            jnp.where(lower, one, pltpu.roll(two, turn, 1)),
            jnp.where(lower, pltpu.roll(one, turn, 1), two),
        )
    first_next = jnp.where(live, one, 0.0)
    second_next = jnp.where(live, two, 0.0)
    first[...] = first_next
    second[...] = second_next
    adam[...] = first_next / (jnp.sqrt(second_next) + 1e-08)
    at = groups * slots
    for p in range(dp_count):
        here = p * table_rows
        terms = [
            moved[p, at + r : at + r + table_rows, :].astype(F32) for moved in arrived for r in (0, table_rows)
        ]
        table[here : here + table_rows, :] = sum(terms[1:], terms[0])
    high, low = split(table[...])
    values = jnp.concatenate([high.astype(F32), low.astype(F32)], axis=0).T.astype(BF16)
    step = 1024
    for start in range(0, D_NEW, step):
        spread = dot(values, tables[:, start : start + step], (1, 0))
        mask = lax.broadcasted_iota(jnp.int32, (LANES, step), 0) == places[:, start : start + step]
        value = jnp.where(mask, spread, 0.0)
        gain_grad[:, start : start + step] = jnp.sum(value, axis=0, keepdims=True)


def resident(value):
    return pltpu.with_memory_space_constraint(value, pltpu.VMEM)


def call(kernel, micros, out_shape, specs, scratch, *args):
    scalars = jax.ShapeDtypeStruct((1,), jnp.int32)
    out_specs = jax.tree.map(lambda out: SMEM_SPEC if out == scalars else VMEM_SPEC, out_shape)
    return pl.pallas_call(
        kernel,
        out_shape=out_shape,
        in_specs=specs,
        out_specs=out_specs,
        scratch_shapes=scratch,
        cost_estimate=pl.CostEstimate(flops=0, transcendentals=0, bytes_accessed=micros * BYTES_PER_US),
        compiler_params=pltpu.CompilerParams(vmem_limit_bytes=VMEM_LIMIT),
    )(*args)


def on_device(
    hidden_old,
    cotangent,
    gain_old,
    old_bounds,
    new_bounds,
    source_map,
    weight_old,
    moment_first,
    moment_second,
):
    dp_count = lax.axis_size("dp")
    rep_count = lax.axis_size("rep")
    cap = weight_old.shape[0]
    mean = D_NEW // dp_count
    new_cap = mean + mean // 4
    slots = (new_cap + dp_count - 1) // dp_count
    table_rows = (dp_count * slots + LANES - 1) // LANES
    tokens = hidden_old.shape[0]
    part = cap // rep_count
    shape = jax.ShapeDtypeStruct

    units = source_map.reshape(1, D_NEW)
    gain = gain_old.reshape(D_OLD // LANES, LANES)
    staged = rep_count == 2 and dp_count >= 4
    bits = dp_count.bit_length() - 1
    line = list(range(bits - 1))
    halving = [line + [bits - 1], line[-1:] + line[:-1] + [bits - 1]]
    doubling = [[bits - 1] + line, [bits - 1] + line[::-1]]
    if staged:
        rels = [
            [sum(((at >> (bits - 1 - s)) & 1) << bit for s, bit in enumerate(order)) for at in range(dp_count)]
            for order in halving
        ]
        parts = 2
    else:
        rels = [list(range(dp_count))]
        parts = 1

    def across(value, orders, stage):
        pairs = [
            (dp * rep_count + rep, (dp ^ (1 << orders[rep][stage])) * rep_count + rep)
            for dp in range(dp_count)
            for rep in range(rep_count)
        ]
        return lax.ppermute(value, ("dp", "rep"), pairs)

    swap = [(0, 1), (1, 0)]
    any_spec = pl.BlockSpec(memory_space=pl.ANY)
    if staged:
        gathered = lax.dynamic_slice_in_dim(weight_old, lax.axis_index("rep") * part, part)[None]
        sent = across(gathered, doubling, 0)
    else:
        weights = lax.all_gather(weight_old, "dp", axis=0, tiled=True)

    tiles = D_OLD // LANES
    live_gain, inv_rms, *blocks = call(
        lambda *refs: token_kernel(rels, rep_count, cap, *refs),
        8,
        (
            shape((tiles, LANES), F32),
            shape((tokens, LANES), F32),
            *[pltpu.VMEM((dp_count // parts, part, LANES), F32)] * parts,
            *[pltpu.VMEM((rep_count - 1, dp_count // parts, part, LANES), BF16)] * parts,
        ),
        [SMEM_SPEC] + [VMEM_SPEC] * 2 + [any_spec] + [VMEM_SPEC],
        [
            pltpu.VMEM((tiles, LANES), F32),
            pltpu.VMEM((tokens, D_OLD), BF16),
            pltpu.VMEM((D_OLD + cap, LANES), F32),
            pltpu.VMEM((D_OLD + cap, LANES), F32),
            pltpu.SemaphoreType.DMA(()),
        ],
        old_bounds,
        units,
        gain,
        hidden_old,
        cotangent,
    )
    owns, others = blocks[:parts], blocks[parts:]
    def indices(src):
        return call(
            lambda *refs: index_kernel(dp_count, cap, slots, table_rows, *refs),
            3,
            (
                pltpu.VMEM((table_rows * LANES, cap), BF16),
                pltpu.VMEM((1, table_rows * LANES), F32),
                pltpu.VMEM((1, cap), F32),
                shape((1,), jnp.int32),
            ),
            [SMEM_SPEC] * 3 + [VMEM_SPEC],
            [pltpu.VMEM((table_rows * LANES, LANES), jnp.int32), pltpu.VMEM((D_OLD // LANES + 8, LANES), F32)],
            old_bounds,
            new_bounds,
            src,
            gain,
        )

    project_shape = shape((tokens, LANES), BF16)
    dense = [pltpu.VMEM((D_OLD + cap, LANES), F32), pltpu.VMEM((tokens, D_OLD), BF16)]
    if staged:
        half = dp_count // 2
        send, sent = lax.optimization_barrier((others[1][0], sent))
        gathered = jnp.concatenate([gathered, sent])
        sent = across(gathered, doubling, 1)
        pair, gathered = lax.optimization_barrier((lax.ppermute(send, "rep", swap), gathered))
        high = (owns[1] + pair.astype(F32)).astype(BF16)
        low = owns[0] + lax.ppermute(others[0][0], "rep", swap).astype(F32)
        for stage in range(bits - 1):
            came = across(high, halving, stage)
            came, sent = lax.optimization_barrier((came, sent))
            if stage == 1:
                came, chosen = lax.optimization_barrier((came, chosen))
            if stage < bits - 2:
                gathered = jnp.concatenate([gathered, sent])
                sent = across(gathered, doubling, stage + 2)
                came, gathered = lax.optimization_barrier((came, gathered))
            if stage == 0:
                gathered, late_src = lax.optimization_barrier((gathered, source_map))
                chosen, keep, own_gain, offset = indices(late_src)
            came = came.astype(F32)
            half = half // 2
            low, high = low[:half] + came[:half], (low[half:] + came[half:]).astype(BF16)
        came = across(high, halving, bits - 1)
        pieces = [gathered, sent]
        pieces += [lax.ppermute(piece, "rep", swap) for piece in pieces]
        came, *pieces = lax.optimization_barrier((came, *pieces))
        reduced = [resident(low), resident(came)]
        projected = call(
            lambda *refs: project_kernel(dp_count, doubling, cap, *refs),
            6,
            project_shape,
            [SMEM_SPEC] + [VMEM_SPEC] * 3 + [any_spec] * 4,
            dense + [pltpu.VMEM((2, dp_count, part, LANES), BF16), pltpu.SemaphoreType.DMA((4,))],
            old_bounds,
            hidden_old,
            inv_rms,
            live_gain,
            *pieces,
        )
    else:
        chip = owns[0]
        for away in range(1, rep_count):
            ring = [(r, (r + away) % rep_count) for r in range(rep_count)]
            chip = chip + lax.ppermute(others[0][away - 1], "rep", ring).astype(F32)
        blocks = lax.all_to_all(chip.astype(BF16), "dp", split_axis=0, concat_axis=0)
        grad_part = jnp.sum(blocks.astype(F32), axis=0)
        reduced = [lax.all_gather(grad_part, "rep", axis=0, tiled=True)]
        chosen, keep, own_gain, offset = indices(source_map)
        projected = call(
            lambda *refs: project_gathered_kernel(dp_count, cap, *refs),
            6,
            project_shape,
            [SMEM_SPEC] + [VMEM_SPEC] * 4,
            dense,
            old_bounds,
            hidden_old,
            inv_rms,
            live_gain,
            weights,
        )

    message = (1 if staged else 2) * slots + 2 * table_rows
    message = (message + 7) // 8 * 8
    packed = call(
        lambda *refs: pack_kernel(dp_count, slots, table_rows, staged, *refs),
        3,
        pltpu.VMEM((dp_count, message, LANES), BF16),
        [VMEM_SPEC] * (6 + len(reduced)),
        [],
        *[resident(value) for value in (chosen, keep, own_gain)],
        *reduced,
        *[resident(value) for value in (weight_old, moment_first, moment_second)],
    )
    packed, late_units = lax.optimization_barrier((packed, units))
    places, tables = call(
        lambda *refs: place_kernel(dp_count, slots, table_rows, *refs),
        2,
        (pltpu.VMEM((1, D_NEW), jnp.int32), pltpu.VMEM((2 * dp_count * table_rows, D_NEW), BF16)),
        [SMEM_SPEC] * 2 + [VMEM_SPEC],
        [],
        old_bounds,
        new_bounds,
        late_units,
    )
    moved = [lax.all_to_all(packed, "dp", split_axis=0, concat_axis=0)]
    if staged:
        arrived, projected, places = lax.optimization_barrier((moved[0], projected, places))
        moved = [arrived, lax.ppermute(arrived, "rep", swap)]
        moved = [resident(value) for value in moved]
    rows = shape((new_cap, LANES), F32)
    gain_grad, first_next, second_next, adam_step = call(
        lambda *refs: finish_kernel(dp_count, slots, table_rows, staged, *refs),
        4,
        (shape((1, D_NEW), F32), rows, rows, rows),
        [SMEM_SPEC] * 2 + [VMEM_SPEC] * (2 + len(moved)),
        [pltpu.VMEM((dp_count * slots, LANES), F32)] * 2
        + [pltpu.VMEM((dp_count * table_rows, LANES), F32)],
        new_bounds,
        offset,
        resident(places),
        resident(tables),
        *moved,
    )
    return (projected, gain_grad.reshape(D_NEW), first_next, second_next, adam_step)


def solution(mesh):
    placed = (
        P(("dp", "rep"), None),
        P(("dp", "rep"), None),
        P(),
        P(),
        P(),
        P(),
        P("dp", None),
        P("dp", None),
        P("dp", None),
    )
    return jax.shard_map(
        on_device,
        mesh=mesh,
        in_specs=placed,
        out_specs=(P(("dp", "rep"), None), P(), P("dp", None), P("dp", None), P("dp", None)),
        check_vma=False,
    )
```

```python
import jax
import jax.numpy as jnp
from jax import lax
from jax.experimental import pallas as pl
from jax.experimental.pallas import tpu as pltpu
from jax.sharding import PartitionSpec as P

D_OLD = 6144
D_NEW = 8192
LANES = 128
BYTES_PER_US = 3_000_000
VMEM_LIMIT = 56 * 1024 * 1024
F32 = jnp.float32
BF16 = jnp.bfloat16

SMEM_SPEC = pl.BlockSpec(memory_space=pltpu.SMEM)
VMEM_SPEC = pl.BlockSpec(memory_space=pltpu.VMEM)


def dot(left, right, contract):
    return lax.dot_general(left, right, ((contract[:1], contract[1:]), ((), ())), preferred_element_type=F32)


def one_hot(rows, values):
    lanes = values.shape[1]
    match = lax.broadcasted_iota(jnp.int32, (rows, lanes), 0).astype(BF16) == values.astype(BF16)
    return jnp.where(match, jnp.ones((), BF16), jnp.zeros((), BF16))


def split(value):
    high = value.astype(BF16)
    return high, (value - high.astype(F32)).astype(BF16)


def normed_tile(tile, hidden, inv_rms, gain):
    stream = hidden[:, tile * LANES : (tile + 1) * LANES].astype(F32)
    return ((stream * inv_rms) * gain[tile : tile + 1, :]).astype(BF16)


def lower_half(rows):
    return lax.broadcasted_iota(jnp.int32, (rows, LANES), 1) < LANES // 2


def token_kernel(rels, rep_count, cap, ob, src, gain, hidden_hbm, cot, live_gain, inv_out, *rest):
    *blocks, hist, hidden, own_grads, other_grads, sem = rest
    owns, others = blocks[: len(blocks) // 2], blocks[len(blocks) // 2 :]
    pieces = sem.shape[0]
    width = D_OLD // pieces
    copies = []
    for piece in range(pieces):
        columns = pl.ds(piece * width, width)
        copies.append(pltpu.make_async_copy(hidden_hbm.at[:, columns], hidden.at[:, columns], sem.at[piece]))
    for copy in copies:
        copy.start()
    me = lax.axis_index("dp")
    rep = lax.axis_index("rep")
    tiles = D_OLD // LANES
    tokens = hidden.shape[0]
    step = 1024
    total = jnp.zeros((tiles, LANES), F32)
    for at in range(0, D_NEW, step):
        units = src[:, at : at + step]
        total = total + dot(one_hot(tiles, units >> 7), one_hot(LANES, units & 127), (1, 1))
    hist[...] = total
    live_gain[...] = jnp.where(total > 0.5, gain[...], 0.0)
    squares = jnp.zeros((tokens, LANES), F32)
    for tile in range(tiles):
        if tile * LANES % width == 0:
            copies[tile * LANES // width].wait()
        stream = hidden[:, tile * LANES : (tile + 1) * LANES].astype(F32)
        squares = squares + stream * stream * hist[tile : tile + 1, :]
    inv_rms = lax.rsqrt(jnp.sum(squares, axis=1, keepdims=True) / D_NEW + 1e-05)
    inv_out[...] = jnp.broadcast_to(inv_rms, (tokens, LANES))
    staged = len(rels) > 1
    columns = cot[...]
    if staged:
        lower = lower_half(tokens)
        columns = columns.astype(F32)
        turned = pltpu.roll(columns, LANES // 2, 1)
        left, right = jnp.where(lower, columns, turned), jnp.where(lower, turned, columns)
        sides = [jnp.where(rep == 0, left, right), jnp.where(rep == 0, right, left)]
        columns = jnp.concatenate(sides, axis=1).astype(BF16)
    for tile in range(tiles):
        at = tile * LANES
        result = dot(normed_tile(tile, hidden, inv_rms, live_gain), columns, (0, 0))
        own_grads[at : at + LANES, :] = result[:, :LANES]
        if staged:
            other_grads[at : at + LANES, :] = result[:, LANES:]
    own_grads[D_OLD:, :] = jnp.zeros((cap, LANES), F32)
    other_grads[D_OLD:, :] = jnp.zeros((cap, LANES), F32)
    dp_count = len(rels[0])
    half = dp_count // len(owns)
    part = cap // rep_count
    for at in range(dp_count):
        if staged:
            first = ob[holder_at(rels, rep, me, at)]
            owns[at // half][at % half] = packed_rows(own_grads, first, part)
            first = ob[holder_at(rels, 1 - rep, me, at)]
            others[at // half][0, at % half] = packed_rows(other_grads, first, part).astype(BF16)
        else:
            first = ob[at]
            owns[0][at] = own_grads[pl.ds(first + rep * part, part), :]
            for away in range(1, rep_count):
                mate = (rep + away) % rep_count
                others[0][away - 1, at] = own_grads[pl.ds(first + mate * part, part), :].astype(BF16)


def packed_rows(grads, first, part):
    return jnp.where(lower_half(part), grads[pl.ds(first, part), :], grads[pl.ds(first + part, part), :])


def holder_at(rels, rep, me, at):
    return me ^ jnp.where(rep == 0, rels[0][at], rels[1][at])


def fill_normed(x, hidden, inv_rms, gain):
    for tile in range(D_OLD // LANES):
        x[:, tile * LANES : (tile + 1) * LANES] = normed_tile(tile, hidden, inv_rms[...], gain)


def project_kernel(dp_count, orders, cap, ob, hidden, inv_rms, gain, *rest):
    *pieces, out, dense, x, blocks, sems = rest
    me = lax.axis_index("dp")
    rep = lax.axis_index("rep")
    part = cap // 2
    half = dp_count // 2
    copies = []
    for at, piece in enumerate(pieces):
        side = rep if at < 2 else 1 - rep
        place = blocks.at[side, pl.ds((at % 2) * half, half)]
        copies.append(pltpu.make_async_copy(piece, place, sems.at[at]))
    for copy in copies:
        copy.start()
    fill_normed(x, hidden, inv_rms, gain)
    for copy in copies:
        copy.wait()
    for p in range(dp_count):
        away = me ^ p
        for side, order in enumerate(orders):
            at = sum(((away >> bit) & 1) << s for s, bit in enumerate(order))
            dense[pl.ds(ob[p] + side * part, part), :] = blocks[side, at].astype(F32)
    out[...] = dot(x[...], dense[0:D_OLD, :].astype(BF16), (1, 0)).astype(BF16)


def project_gathered_kernel(dp_count, cap, ob, hidden, inv_rms, gain, weights, out, dense, x):
    fill_normed(x, hidden, inv_rms, gain)
    for p in range(dp_count):
        dense[pl.ds(ob[p], cap), :] = weights[p * cap : (p + 1) * cap, :].astype(F32)
    out[...] = dot(x[...], dense[0:D_OLD, :].astype(BF16), (1, 0)).astype(BF16)


def offset_of(src, ob, nb, q, dp_count):
    first = src[nb[q]]
    holder = jnp.int32(0)
    for p in range(1, dp_count):
        holder = holder + (ob[p] <= first).astype(jnp.int32)
    return holder


def index_kernel(dp_count, cap, slots, table_rows, ob, nb, src, gain, chosen, keep, own_gain, offset, rows, gains):
    me = lax.axis_index("dp")
    mine = ob[me]
    groups = cap // LANES
    offset[0] = offset_of(src, ob, nb, me, dp_count)
    rows[...] = jnp.full(rows.shape, -1, jnp.int32)
    for q in range(dp_count):
        start = nb[q] + ((me - offset_of(src, ob, nb, q, dp_count)) & (dp_count - 1))
        end = nb[q + 1]
        for k in range(slots):
            unit = start + dp_count * k
            row = jnp.where(unit < end, src[jnp.minimum(unit, D_NEW - 1)] - mine, -1)
            rows[q * slots + k : q * slots + k + 1, :] = jnp.full((1, LANES), row, jnp.int32)
    lanes = lax.broadcasted_iota(jnp.int32, rows.shape, 1)
    for g in range(groups):
        chosen[:, g * LANES : (g + 1) * LANES] = jnp.where(rows[...] == lanes + g * LANES, 1.0, 0.0).astype(BF16)
    gains[0 : gain.shape[0], :] = gain[...]
    gains[gain.shape[0] :, :] = jnp.ones((gains.shape[0] - gain.shape[0], LANES), F32)
    gain_rows = gains[pl.ds(mine >> 7, groups + 1), :]
    shift = mine & 127
    rolled = pltpu.roll(gain_rows, (LANES - shift) & 127, 1)
    lane_row = lax.broadcasted_iota(jnp.int32, (groups, LANES), 1)
    inverse = 1.0 / jnp.where(lane_row < LANES - shift, rolled[:groups], rolled[1:])
    for g in range(groups):
        own_gain[:, g * LANES : (g + 1) * LANES] = inverse[g : g + 1]
    same = dot(chosen[...], chosen[...], (1, 1))
    earlier = lax.broadcasted_iota(jnp.int32, same.shape, 0) < lax.broadcasted_iota(jnp.int32, same.shape, 1)
    repeated = jnp.max(jnp.where(earlier, same, 0.0), axis=0, keepdims=True)
    keep[...] = jnp.where(repeated < 0.5, 1.0, 0.0)


def place_kernel(dp_count, slots, table_rows, ob, nb, units, places, tables):
    step = 1024
    for first in range(0, D_NEW, step):
        source = units[:, first : first + step]
        position = first + lax.broadcasted_iota(jnp.int32, (1, step), 1)
        holder = jnp.zeros((1, step), jnp.int32)
        dest = jnp.zeros((1, step), jnp.int32)
        begin = jnp.zeros((1, step), jnp.int32)
        for p in range(1, dp_count):
            holder = holder + jnp.where(source >= ob[p], 1, 0)
            past = position >= nb[p]
            dest = jnp.where(past, p, dest)
            begin = jnp.where(past, nb[p], begin)
        rank = (position - begin) >> (dp_count.bit_length() - 1)
        place = holder * (table_rows * LANES) + dest * slots + rank
        places[:, first : first + step] = place & 127
        spread = one_hot(dp_count * table_rows, place >> 7)
        tables[:, first : first + step] = jnp.concatenate([spread, spread], axis=0)


def pack_kernel(dp_count, slots, table_rows, staged, chosen, keep, own_gain, *rest):
    *reduced, weight_in, first_in, second_in, out = rest
    pairs = dp_count * slots
    rows = weight_in.shape[0]
    weight, first, second = weight_in[...].astype(F32), first_in[...], second_in[...]
    if staged:
        turn = LANES // 2
        lower = lower_half(rows)
        grad = reduced[0][0] + reduced[1][0].astype(F32)
        grad = jnp.concatenate([grad, pltpu.roll(grad, turn, 1)], axis=0)
        left = lax.axis_index("rep") == 0
        weight, first, second = [
            jnp.where(left, value, pltpu.roll(value, turn, 1)) for value in (weight, first, second)
        ]
        product = jnp.where(lower, weight * grad, 0.0)
    else:
        grad = reduced[0][...]
        product = weight * grad
    high, low = split(product)
    ones = jnp.ones((8, LANES), BF16)
    column = (dot(ones, high, (1, 1)) + dot(ones, low, (1, 1))) * own_gain[...]
    picked = dot(jnp.concatenate(split(column), axis=0), chosen[...], (1, 1))
    table = []
    for part in (picked[0:1], picked[8:9]):
        part = part * keep[...]
        table += [part[:, r * LANES : (r + 1) * LANES] for r in range(table_rows)]
    updated = [0.9 * first + 0.1 * grad, 0.95 * second + 0.05 * grad * grad]
    if staged:
        updated = [jnp.where(lower, updated[0], pltpu.roll(updated[1], turn, 1))]
    filled = len(updated) * slots
    spare = out.shape[1] - filled - 2 * table_rows
    table = jnp.concatenate(table + [jnp.zeros((spare, LANES), F32)], axis=0).astype(BF16)
    picked = chosen[0:pairs]
    for at, value in enumerate(updated):
        moved = dot(picked, value.astype(BF16), (1, 0)).astype(BF16).reshape(dp_count, slots, LANES)
        out[:, at * slots : (at + 1) * slots, :] = moved
    for q in range(dp_count):
        out[q, filled:, :] = table


def finish_kernel(dp_count, slots, table_rows, staged, nb, offset_in, places, tables, *rest):
    arrived, rest = (rest[:2], rest[2:]) if staged else (rest[:1], rest[1:])
    gain_grad, first, second, adam, ones, twos, table = rest
    me = lax.axis_index("dp")
    offset = offset_in[0]
    groups = 1 if staged else 2
    pages = [(moved, 0) for moved in arrived] if staged else [(arrived[0], 0), (arrived[0], slots)]
    for i in range(dp_count):
        p = (i + offset) & (dp_count - 1)
        strided = pl.ds(i, slots, stride=dp_count)
        for (moved, at), rows in zip(pages, (ones, twos)):
            rows[strided, :] = moved[p, at : at + slots, :].astype(F32)
    cap = first.shape[0]
    live = lax.broadcasted_iota(jnp.int32, (cap, LANES), 0) < nb[me + 1] - nb[me]
    one, two = ones[0:cap, :], twos[0:cap, :]
    if staged:
        left = lax.axis_index("rep") == 0
        lower = lower_half(cap)
        one, two = jnp.where(left, one, two), jnp.where(left, two, one)
        turn = LANES // 2
        one, two = (
            jnp.where(lower, one, pltpu.roll(two, turn, 1)),
            jnp.where(lower, pltpu.roll(one, turn, 1), two),
        )
    first_next = jnp.where(live, one, 0.0)
    second_next = jnp.where(live, two, 0.0)
    first[...] = first_next
    second[...] = second_next
    adam[...] = first_next / (jnp.sqrt(second_next) + 1e-08)
    at = groups * slots
    for p in range(dp_count):
        here = p * table_rows
        terms = [
            moved[p, at + r : at + r + table_rows, :].astype(F32) for moved in arrived for r in (0, table_rows)
        ]
        table[here : here + table_rows, :] = sum(terms[1:], terms[0])
    high, low = split(table[...])
    values = jnp.concatenate([high.astype(F32), low.astype(F32)], axis=0).T.astype(BF16)
    step = 1024
    for start in range(0, D_NEW, step):
        spread = dot(values, tables[:, start : start + step], (1, 0))
        mask = lax.broadcasted_iota(jnp.int32, (LANES, step), 0) == places[:, start : start + step]
        value = jnp.where(mask, spread, 0.0)
        gain_grad[:, start : start + step] = jnp.sum(value, axis=0, keepdims=True)


def resident(value):
    return pltpu.with_memory_space_constraint(value, pltpu.VMEM)


def call(kernel, micros, out_shape, specs, scratch, *args):
    scalars = jax.ShapeDtypeStruct((1,), jnp.int32)
    out_specs = jax.tree.map(lambda out: SMEM_SPEC if out == scalars else VMEM_SPEC, out_shape)
    return pl.pallas_call(
        kernel,
        out_shape=out_shape,
        in_specs=specs,
        out_specs=out_specs,
        scratch_shapes=scratch,
        cost_estimate=pl.CostEstimate(flops=0, transcendentals=0, bytes_accessed=micros * BYTES_PER_US),
        compiler_params=pltpu.CompilerParams(vmem_limit_bytes=VMEM_LIMIT),
    )(*args)


def on_device(
    hidden_old,
    cotangent,
    gain_old,
    old_bounds,
    new_bounds,
    source_map,
    weight_old,
    moment_first,
    moment_second,
):
    dp_count = lax.axis_size("dp")
    rep_count = lax.axis_size("rep")
    cap = weight_old.shape[0]
    mean = D_NEW // dp_count
    new_cap = mean + mean // 4
    slots = (new_cap + dp_count - 1) // dp_count
    table_rows = (dp_count * slots + LANES - 1) // LANES
    tokens = hidden_old.shape[0]
    part = cap // rep_count
    shape = jax.ShapeDtypeStruct

    units = source_map.reshape(1, D_NEW)
    gain = gain_old.reshape(D_OLD // LANES, LANES)
    staged = rep_count == 2 and dp_count >= 4
    bits = dp_count.bit_length() - 1
    line = list(range(bits - 1))
    halving = [line + [bits - 1], line[::-1] + [bits - 1]]
    doubling = [[bits - 1] + line, [bits - 1] + line[::-1]]
    if staged:
        rels = [
            [sum(((at >> (bits - 1 - s)) & 1) << bit for s, bit in enumerate(order)) for at in range(dp_count)]
            for order in halving
        ]
        parts = 2
    else:
        rels = [list(range(dp_count))]
        parts = 1

    def across(value, orders, stage):
        pairs = [
            (dp * rep_count + rep, (dp ^ (1 << orders[rep][stage])) * rep_count + rep)
            for dp in range(dp_count)
            for rep in range(rep_count)
        ]
        return lax.ppermute(value, ("dp", "rep"), pairs)

    swap = [(0, 1), (1, 0)]
    any_spec = pl.BlockSpec(memory_space=pl.ANY)
    if staged:
        sent = across(weight_old, doubling, 0)
    else:
        weights = lax.all_gather(weight_old, "dp", axis=0, tiled=True)

    tiles = D_OLD // LANES
    live_gain, inv_rms, *blocks = call(
        lambda *refs: token_kernel(rels, rep_count, cap, *refs),
        8,
        (
            shape((tiles, LANES), F32),
            shape((tokens, LANES), F32),
            *[pltpu.VMEM((dp_count // parts, part, LANES), F32)] * parts,
            *[pltpu.VMEM((rep_count - 1, dp_count // parts, part, LANES), BF16)] * parts,
        ),
        [SMEM_SPEC] + [VMEM_SPEC] * 2 + [any_spec] + [VMEM_SPEC],
        [
            pltpu.VMEM((tiles, LANES), F32),
            pltpu.VMEM((tokens, D_OLD), BF16),
            pltpu.VMEM((D_OLD + cap, LANES), F32),
            pltpu.VMEM((D_OLD + cap, LANES), F32),
            pltpu.SemaphoreType.DMA((6,)),
        ],
        old_bounds,
        units,
        gain,
        hidden_old,
        cotangent,
    )
    owns, others = blocks[:parts], blocks[parts:]
    def indices(src):
        return call(
            lambda *refs: index_kernel(dp_count, cap, slots, table_rows, *refs),
            3,
            (
                pltpu.VMEM((table_rows * LANES, cap), BF16),
                pltpu.VMEM((1, table_rows * LANES), F32),
                pltpu.VMEM((1, cap), F32),
                shape((1,), jnp.int32),
            ),
            [SMEM_SPEC] * 3 + [VMEM_SPEC],
            [pltpu.VMEM((table_rows * LANES, LANES), jnp.int32), pltpu.VMEM((D_OLD // LANES + 8, LANES), F32)],
            old_bounds,
            new_bounds,
            src,
            gain,
        )

    project_shape = shape((tokens, LANES), BF16)
    dense = [pltpu.VMEM((D_OLD + cap, LANES), F32), pltpu.VMEM((tokens, D_OLD), BF16)]
    if staged:
        half = dp_count // 2
        send, sent = lax.optimization_barrier((others[1][0], sent))
        mine = lax.axis_index("rep") * part
        gathered = [lax.dynamic_slice_in_dim(block, mine, part)[None] for block in (weight_old, sent)]
        gathered = jnp.concatenate(gathered)
        sent = across(gathered, doubling, 1)
        pair, gathered = lax.optimization_barrier((lax.ppermute(send, "rep", swap), gathered))
        high = (owns[1] + pair.astype(F32)).astype(BF16)
        low = owns[0] + lax.ppermute(others[0][0], "rep", swap).astype(F32)
        for stage in range(bits - 1):
            came = across(high, halving, stage)
            if stage < bits - 2:
                gathered = jnp.concatenate([gathered, sent])
                sent = across(gathered, doubling, stage + 2)
                came, sent = lax.optimization_barrier((came, sent))
            if stage == 1:
                came, chosen = lax.optimization_barrier((came, chosen))
            came = came.astype(F32)
            half = half // 2
            low, high = low[:half] + came[:half], (low[half:] + came[half:]).astype(BF16)
            if stage == 0:
                high, late_src = lax.optimization_barrier((high, source_map))
                chosen, keep, own_gain, offset = indices(late_src)
        came = across(high, halving, bits - 1)
        pieces = [gathered, sent]
        pieces += [lax.ppermute(piece, "rep", swap) for piece in pieces]
        came, *pieces = lax.optimization_barrier((came, *pieces))
        reduced = [resident(low), resident(came)]
        projected = call(
            lambda *refs: project_kernel(dp_count, doubling, cap, *refs),
            6,
            project_shape,
            [SMEM_SPEC] + [VMEM_SPEC] * 3 + [any_spec] * 4,
            dense + [pltpu.VMEM((2, dp_count, part, LANES), BF16), pltpu.SemaphoreType.DMA((4,))],
            old_bounds,
            hidden_old,
            inv_rms,
            live_gain,
            *pieces,
        )
    else:
        chip = owns[0]
        for away in range(1, rep_count):
            ring = [(r, (r + away) % rep_count) for r in range(rep_count)]
            chip = chip + lax.ppermute(others[0][away - 1], "rep", ring).astype(F32)
        blocks = lax.all_to_all(chip.astype(BF16), "dp", split_axis=0, concat_axis=0)
        grad_part = jnp.sum(blocks.astype(F32), axis=0)
        reduced = [lax.all_gather(grad_part, "rep", axis=0, tiled=True)]
        chosen, keep, own_gain, offset = indices(source_map)
        projected = call(
            lambda *refs: project_gathered_kernel(dp_count, cap, *refs),
            6,
            project_shape,
            [SMEM_SPEC] + [VMEM_SPEC] * 4,
            dense,
            old_bounds,
            hidden_old,
            inv_rms,
            live_gain,
            weights,
        )

    message = (1 if staged else 2) * slots + 2 * table_rows
    message = (message + 7) // 8 * 8
    packed = call(
        lambda *refs: pack_kernel(dp_count, slots, table_rows, staged, *refs),
        3,
        pltpu.VMEM((dp_count, message, LANES), BF16),
        [VMEM_SPEC] * (6 + len(reduced)),
        [],
        *[resident(value) for value in (chosen, keep, own_gain)],
        *reduced,
        *[resident(value) for value in (weight_old, moment_first, moment_second)],
    )
    packed, late_units = lax.optimization_barrier((packed, units))
    places, tables = call(
        lambda *refs: place_kernel(dp_count, slots, table_rows, *refs),
        2,
        (pltpu.VMEM((1, D_NEW), jnp.int32), pltpu.VMEM((2 * dp_count * table_rows, D_NEW), BF16)),
        [SMEM_SPEC] * 2 + [VMEM_SPEC],
        [],
        old_bounds,
        new_bounds,
        late_units,
    )
    moved = [lax.all_to_all(packed, "dp", split_axis=0, concat_axis=0)]
    if staged:
        arrived, projected, places = lax.optimization_barrier((moved[0], projected, places))
        moved = [arrived, lax.ppermute(arrived, "rep", swap)]
        moved = [resident(value) for value in moved]
    rows = shape((new_cap, LANES), F32)
    gain_grad, first_next, second_next, adam_step = call(
        lambda *refs: finish_kernel(dp_count, slots, table_rows, staged, *refs),
        4,
        (shape((1, D_NEW), F32), rows, rows, rows),
        [SMEM_SPEC] * 2 + [VMEM_SPEC] * (2 + len(moved)),
        [pltpu.VMEM((dp_count * slots, LANES), F32)] * 2
        + [pltpu.VMEM((dp_count * table_rows, LANES), F32)],
        new_bounds,
        offset,
        resident(places),
        resident(tables),
        *moved,
    )
    return (projected, gain_grad.reshape(D_NEW), first_next, second_next, adam_step)


def solution(mesh):
    placed = (
        P(("dp", "rep"), None),
        P(("dp", "rep"), None),
        P(),
        P(),
        P(),
        P(),
        P("dp", None),
        P("dp", None),
        P("dp", None),
    )
    return jax.shard_map(
        on_device,
        mesh=mesh,
        in_specs=placed,
        out_specs=(P(("dp", "rep"), None), P(), P("dp", None), P("dp", None), P("dp", None)),
        check_vma=False,
    )
```

```python
import jax
import jax.numpy as jnp
from jax import lax
from jax.experimental import pallas as pl
from jax.experimental.pallas import tpu as pltpu
from jax.sharding import PartitionSpec as P

D_OLD = 6144
D_NEW = 8192
LANES = 128
BYTES_PER_US = 3_000_000
VMEM_LIMIT = 56 * 1024 * 1024
F32 = jnp.float32
BF16 = jnp.bfloat16

SMEM_SPEC = pl.BlockSpec(memory_space=pltpu.SMEM)
VMEM_SPEC = pl.BlockSpec(memory_space=pltpu.VMEM)


def dot(left, right, contract):
    return lax.dot_general(left, right, ((contract[:1], contract[1:]), ((), ())), preferred_element_type=F32)


def one_hot(rows, values):
    lanes = values.shape[1]
    match = lax.broadcasted_iota(jnp.int32, (rows, lanes), 0).astype(BF16) == values.astype(BF16)
    return jnp.where(match, jnp.ones((), BF16), jnp.zeros((), BF16))


def split(value):
    high = value.astype(BF16)
    return high, (value - high.astype(F32)).astype(BF16)


def normed_tile(tile, hidden, inv_rms, gain):
    stream = hidden[:, tile * LANES : (tile + 1) * LANES].astype(F32)
    return ((stream * inv_rms) * gain[tile : tile + 1, :]).astype(BF16)


def lower_half(rows):
    return lax.broadcasted_iota(jnp.int32, (rows, LANES), 1) < LANES // 2


def token_kernel(rels, rep_count, cap, ob, src, gain, hidden_hbm, cot, live_gain, inv_out, *rest):
    *blocks, hist, hidden, own_grads, other_grads, sem = rest
    owns, others = blocks[: len(blocks) // 2], blocks[len(blocks) // 2 :]
    pieces = sem.shape[0]
    width = D_OLD // pieces
    copies = []
    for piece in range(pieces):
        columns = pl.ds(piece * width, width)
        copies.append(pltpu.make_async_copy(hidden_hbm.at[:, columns], hidden.at[:, columns], sem.at[piece]))
    for copy in copies:
        copy.start()
    me = lax.axis_index("dp")
    rep = lax.axis_index("rep")
    tiles = D_OLD // LANES
    tokens = hidden.shape[0]
    step = 1024
    total = jnp.zeros((tiles, LANES), F32)
    for at in range(0, D_NEW, step):
        units = src[:, at : at + step]
        total = total + dot(one_hot(tiles, units >> 7), one_hot(LANES, units & 127), (1, 1))
    hist[...] = total
    live_gain[...] = jnp.where(total > 0.5, gain[...], 0.0)
    squares = jnp.zeros((tokens, LANES), F32)
    for tile in range(tiles):
        if tile * LANES % width == 0:
            copies[tile * LANES // width].wait()
        stream = hidden[:, tile * LANES : (tile + 1) * LANES].astype(F32)
        squares = squares + stream * stream * hist[tile : tile + 1, :]
    inv_rms = lax.rsqrt(jnp.sum(squares, axis=1, keepdims=True) / D_NEW + 1e-05)
    inv_out[...] = jnp.broadcast_to(inv_rms, (tokens, LANES))
    staged = len(rels) > 1
    columns = cot[...]
    if staged:
        lower = lower_half(tokens)
        columns = columns.astype(F32)
        turned = pltpu.roll(columns, LANES // 2, 1)
        left, right = jnp.where(lower, columns, turned), jnp.where(lower, turned, columns)
        sides = [jnp.where(rep == 0, left, right), jnp.where(rep == 0, right, left)]
        columns = jnp.concatenate(sides, axis=1).astype(BF16)
    for tile in range(tiles):
        at = tile * LANES
        result = dot(normed_tile(tile, hidden, inv_rms, live_gain), columns, (0, 0))
        own_grads[at : at + LANES, :] = result[:, :LANES]
        if staged:
            other_grads[at : at + LANES, :] = result[:, LANES:]
    own_grads[D_OLD:, :] = jnp.zeros((cap, LANES), F32)
    other_grads[D_OLD:, :] = jnp.zeros((cap, LANES), F32)
    dp_count = len(rels[0])
    half = dp_count // len(owns)
    part = cap // rep_count
    for at in range(dp_count):
        if staged:
            first = ob[holder_at(rels, rep, me, at)]
            owns[at // half][at % half] = packed_rows(own_grads, first, part)
            first = ob[holder_at(rels, 1 - rep, me, at)]
            others[at // half][0, at % half] = packed_rows(other_grads, first, part).astype(BF16)
        else:
            first = ob[at]
            owns[0][at] = own_grads[pl.ds(first + rep * part, part), :]
            for away in range(1, rep_count):
                mate = (rep + away) % rep_count
                others[0][away - 1, at] = own_grads[pl.ds(first + mate * part, part), :].astype(BF16)


def packed_rows(grads, first, part):
    return jnp.where(lower_half(part), grads[pl.ds(first, part), :], grads[pl.ds(first + part, part), :])


def holder_at(rels, rep, me, at):
    return me ^ jnp.where(rep == 0, rels[0][at], rels[1][at])


def fill_normed(x, hidden, inv_rms, gain):
    for tile in range(D_OLD // LANES):
        x[:, tile * LANES : (tile + 1) * LANES] = normed_tile(tile, hidden, inv_rms[...], gain)


def project_kernel(dp_count, orders, cap, ob, hidden, inv_rms, gain, *rest):
    *pieces, out, dense, x, blocks, sems = rest
    me = lax.axis_index("dp")
    rep = lax.axis_index("rep")
    part = cap // 2
    half = dp_count // 2
    copies = []
    for at, piece in enumerate(pieces):
        side = rep if at < 2 else 1 - rep
        place = blocks.at[side, pl.ds((at % 2) * half, half)]
        copies.append(pltpu.make_async_copy(piece, place, sems.at[at]))
    for copy in copies:
        copy.start()
    fill_normed(x, hidden, inv_rms, gain)
    for copy in copies:
        copy.wait()
    for p in range(dp_count):
        away = me ^ p
        for side, order in enumerate(orders):
            at = sum(((away >> bit) & 1) << s for s, bit in enumerate(order))
            dense[pl.ds(ob[p] + side * part, part), :] = blocks[side, at].astype(F32)
    out[...] = dot(x[...], dense[0:D_OLD, :].astype(BF16), (1, 0)).astype(BF16)


def project_gathered_kernel(dp_count, cap, ob, hidden, inv_rms, gain, weights, out, dense, x):
    fill_normed(x, hidden, inv_rms, gain)
    for p in range(dp_count):
        dense[pl.ds(ob[p], cap), :] = weights[p * cap : (p + 1) * cap, :].astype(F32)
    out[...] = dot(x[...], dense[0:D_OLD, :].astype(BF16), (1, 0)).astype(BF16)


def offset_of(src, ob, nb, q, dp_count):
    first = src[nb[q]]
    holder = jnp.int32(0)
    for p in range(1, dp_count):
        holder = holder + (ob[p] <= first).astype(jnp.int32)
    return holder


def index_kernel(dp_count, cap, slots, table_rows, ob, nb, src, gain, chosen, keep, own_gain, offset, rows, gains):
    me = lax.axis_index("dp")
    mine = ob[me]
    groups = cap // LANES
    offset[0] = offset_of(src, ob, nb, me, dp_count)
    rows[...] = jnp.full(rows.shape, -1, jnp.int32)
    for q in range(dp_count):
        start = nb[q] + ((me - offset_of(src, ob, nb, q, dp_count)) & (dp_count - 1))
        end = nb[q + 1]
        for k in range(slots):
            unit = start + dp_count * k
            row = jnp.where(unit < end, src[jnp.minimum(unit, D_NEW - 1)] - mine, -1)
            rows[q * slots + k : q * slots + k + 1, :] = jnp.full((1, LANES), row, jnp.int32)
    lanes = lax.broadcasted_iota(jnp.int32, rows.shape, 1)
    for g in range(groups):
        chosen[:, g * LANES : (g + 1) * LANES] = jnp.where(rows[...] == lanes + g * LANES, 1.0, 0.0).astype(BF16)
    gains[0 : gain.shape[0], :] = gain[...]
    gains[gain.shape[0] :, :] = jnp.ones((gains.shape[0] - gain.shape[0], LANES), F32)
    gain_rows = gains[pl.ds(mine >> 7, groups + 1), :]
    shift = mine & 127
    rolled = pltpu.roll(gain_rows, (LANES - shift) & 127, 1)
    lane_row = lax.broadcasted_iota(jnp.int32, (groups, LANES), 1)
    inverse = 1.0 / jnp.where(lane_row < LANES - shift, rolled[:groups], rolled[1:])
    for g in range(groups):
        own_gain[:, g * LANES : (g + 1) * LANES] = inverse[g : g + 1]
    same = dot(chosen[...], chosen[...], (1, 1))
    earlier = lax.broadcasted_iota(jnp.int32, same.shape, 0) < lax.broadcasted_iota(jnp.int32, same.shape, 1)
    repeated = jnp.max(jnp.where(earlier, same, 0.0), axis=0, keepdims=True)
    keep[...] = jnp.where(repeated < 0.5, 1.0, 0.0)


def place_kernel(dp_count, slots, table_rows, ob, nb, units, places, tables):
    step = 1024
    for first in range(0, D_NEW, step):
        source = units[:, first : first + step]
        position = first + lax.broadcasted_iota(jnp.int32, (1, step), 1)
        holder = jnp.zeros((1, step), jnp.int32)
        dest = jnp.zeros((1, step), jnp.int32)
        begin = jnp.zeros((1, step), jnp.int32)
        for p in range(1, dp_count):
            holder = holder + jnp.where(source >= ob[p], 1, 0)
            past = position >= nb[p]
            dest = jnp.where(past, p, dest)
            begin = jnp.where(past, nb[p], begin)
        rank = (position - begin) >> (dp_count.bit_length() - 1)
        place = holder * (table_rows * LANES) + dest * slots + rank
        places[:, first : first + step] = place & 127
        spread = one_hot(dp_count * table_rows, place >> 7)
        tables[:, first : first + step] = jnp.concatenate([spread, spread], axis=0)


def pack_kernel(dp_count, slots, table_rows, staged, chosen, keep, own_gain, *rest):
    *reduced, weight_in, first_in, second_in, out = rest
    pairs = dp_count * slots
    rows = weight_in.shape[0]
    weight, first, second = weight_in[...].astype(F32), first_in[...], second_in[...]
    if staged:
        turn = LANES // 2
        lower = lower_half(rows)
        grad = reduced[0][0] + reduced[1][0].astype(F32)
        grad = jnp.concatenate([grad, pltpu.roll(grad, turn, 1)], axis=0)
        left = lax.axis_index("rep") == 0
        weight, first, second = [
            jnp.where(left, value, pltpu.roll(value, turn, 1)) for value in (weight, first, second)
        ]
        product = jnp.where(lower, weight * grad, 0.0)
    else:
        grad = reduced[0][...]
        product = weight * grad
    high, low = split(product)
    ones = jnp.ones((8, LANES), BF16)
    column = (dot(ones, high, (1, 1)) + dot(ones, low, (1, 1))) * own_gain[...]
    picked = dot(jnp.concatenate(split(column), axis=0), chosen[...], (1, 1))
    table = []
    for part in (picked[0:1], picked[8:9]):
        part = part * keep[...]
        table += [part[:, r * LANES : (r + 1) * LANES] for r in range(table_rows)]
    updated = [0.9 * first + 0.1 * grad, 0.95 * second + 0.05 * grad * grad]
    if staged:
        updated = [jnp.where(lower, updated[0], pltpu.roll(updated[1], turn, 1))]
    filled = len(updated) * slots
    spare = out.shape[1] - filled - 2 * table_rows
    table = jnp.concatenate(table + [jnp.zeros((spare, LANES), F32)], axis=0).astype(BF16)
    picked = chosen[0:pairs]
    for at, value in enumerate(updated):
        moved = dot(picked, value.astype(BF16), (1, 0)).astype(BF16).reshape(dp_count, slots, LANES)
        out[:, at * slots : (at + 1) * slots, :] = moved
    for q in range(dp_count):
        out[q, filled:, :] = table


def finish_kernel(dp_count, slots, table_rows, staged, nb, offset_in, places, tables, *rest):
    arrived, rest = (rest[:2], rest[2:]) if staged else (rest[:1], rest[1:])
    gain_grad, first, second, adam, ones, twos, table = rest
    me = lax.axis_index("dp")
    offset = offset_in[0]
    groups = 1 if staged else 2
    pages = [(moved, 0) for moved in arrived] if staged else [(arrived[0], 0), (arrived[0], slots)]
    for i in range(dp_count):
        p = (i + offset) & (dp_count - 1)
        strided = pl.ds(i, slots, stride=dp_count)
        for (moved, at), rows in zip(pages, (ones, twos)):
            rows[strided, :] = moved[p, at : at + slots, :].astype(F32)
    cap = first.shape[0]
    live = lax.broadcasted_iota(jnp.int32, (cap, LANES), 0) < nb[me + 1] - nb[me]
    one, two = ones[0:cap, :], twos[0:cap, :]
    if staged:
        left = lax.axis_index("rep") == 0
        lower = lower_half(cap)
        one, two = jnp.where(left, one, two), jnp.where(left, two, one)
        turn = LANES // 2
        one, two = (
            jnp.where(lower, one, pltpu.roll(two, turn, 1)),
            jnp.where(lower, pltpu.roll(one, turn, 1), two),
        )
    first_next = jnp.where(live, one, 0.0)
    second_next = jnp.where(live, two, 0.0)
    first[...] = first_next
    second[...] = second_next
    adam[...] = first_next / (jnp.sqrt(second_next) + 1e-08)
    at = groups * slots
    for p in range(dp_count):
        here = p * table_rows
        terms = [
            moved[p, at + r : at + r + table_rows, :].astype(F32) for moved in arrived for r in (0, table_rows)
        ]
        table[here : here + table_rows, :] = sum(terms[1:], terms[0])
    high, low = split(table[...])
    values = jnp.concatenate([high.astype(F32), low.astype(F32)], axis=0).T.astype(BF16)
    step = 1024
    for start in range(0, D_NEW, step):
        spread = dot(values, tables[:, start : start + step], (1, 0))
        mask = lax.broadcasted_iota(jnp.int32, (LANES, step), 0) == places[:, start : start + step]
        value = jnp.where(mask, spread, 0.0)
        gain_grad[:, start : start + step] = jnp.sum(value, axis=0, keepdims=True)


def resident(value):
    return pltpu.with_memory_space_constraint(value, pltpu.VMEM)


def call(kernel, micros, out_shape, specs, scratch, *args):
    scalars = jax.ShapeDtypeStruct((1,), jnp.int32)
    out_specs = jax.tree.map(lambda out: SMEM_SPEC if out == scalars else VMEM_SPEC, out_shape)
    return pl.pallas_call(
        kernel,
        out_shape=out_shape,
        in_specs=specs,
        out_specs=out_specs,
        scratch_shapes=scratch,
        cost_estimate=pl.CostEstimate(flops=0, transcendentals=0, bytes_accessed=micros * BYTES_PER_US),
        compiler_params=pltpu.CompilerParams(vmem_limit_bytes=VMEM_LIMIT),
    )(*args)


def on_device(
    hidden_old,
    cotangent,
    gain_old,
    old_bounds,
    new_bounds,
    source_map,
    weight_old,
    moment_first,
    moment_second,
):
    dp_count = lax.axis_size("dp")
    rep_count = lax.axis_size("rep")
    cap = weight_old.shape[0]
    mean = D_NEW // dp_count
    new_cap = mean + mean // 4
    slots = (new_cap + dp_count - 1) // dp_count
    table_rows = (dp_count * slots + LANES - 1) // LANES
    tokens = hidden_old.shape[0]
    part = cap // rep_count
    shape = jax.ShapeDtypeStruct

    units = source_map.reshape(1, D_NEW)
    gain = gain_old.reshape(D_OLD // LANES, LANES)
    staged = rep_count == 2 and dp_count >= 8
    bits = dp_count.bit_length() - 1
    line = list(range(bits - 1))
    ends = [line[:1] + line[-1:], line[-1:] + line[:1]]
    halving = [pair + line[1:-1] + [bits - 1] for pair in ends]
    doubling = [[bits - 1] + line, [bits - 1] + line[::-1]]
    if staged:
        rels = [
            [sum(((at >> (bits - 1 - s)) & 1) << bit for s, bit in enumerate(order)) for at in range(dp_count)]
            for order in halving
        ]
        parts = 2
    else:
        rels = [list(range(dp_count))]
        parts = 1

    def across(value, orders, stage):
        pairs = [
            (dp * rep_count + rep, (dp ^ (1 << orders[rep][stage])) * rep_count + rep)
            for dp in range(dp_count)
            for rep in range(rep_count)
        ]
        return lax.ppermute(value, ("dp", "rep"), pairs)

    swap = [(0, 1), (1, 0)]
    any_spec = pl.BlockSpec(memory_space=pl.ANY)
    if staged:
        sent = across(weight_old, doubling, 0)
    else:
        weights = lax.all_gather(weight_old, "dp", axis=0, tiled=True)

    tiles = D_OLD // LANES
    live_gain, inv_rms, *blocks = call(
        lambda *refs: token_kernel(rels, rep_count, cap, *refs),
        8,
        (
            shape((tiles, LANES), F32),
            shape((tokens, LANES), F32),
            *[pltpu.VMEM((dp_count // parts, part, LANES), F32)] * parts,
            *[shape((rep_count - 1, dp_count // parts, part, LANES), BF16)] * parts,
        ),
        [SMEM_SPEC] + [VMEM_SPEC] * 2 + [any_spec] + [VMEM_SPEC],
        [
            pltpu.VMEM((tiles, LANES), F32),
            pltpu.VMEM((tokens, D_OLD), BF16),
            pltpu.VMEM((D_OLD + cap, LANES), F32),
            pltpu.VMEM((D_OLD + cap, LANES), F32),
            pltpu.SemaphoreType.DMA((6,)),
        ],
        old_bounds,
        units,
        gain,
        hidden_old,
        cotangent,
    )
    owns, others = blocks[:parts], blocks[parts:]
    def indices(src):
        return call(
            lambda *refs: index_kernel(dp_count, cap, slots, table_rows, *refs),
            0,
            (
                pltpu.VMEM((table_rows * LANES, cap), BF16),
                pltpu.VMEM((1, table_rows * LANES), F32),
                pltpu.VMEM((1, cap), F32),
                shape((1,), jnp.int32),
            ),
            [SMEM_SPEC] * 3 + [VMEM_SPEC],
            [pltpu.VMEM((table_rows * LANES, LANES), jnp.int32), pltpu.VMEM((D_OLD // LANES + 8, LANES), F32)],
            old_bounds,
            new_bounds,
            src,
            gain,
        )

    project_shape = shape((tokens, LANES), BF16)
    dense = [pltpu.VMEM((D_OLD + cap, LANES), F32), pltpu.VMEM((tokens, D_OLD), BF16)]
    if staged:
        half = dp_count // 2
        mine = lax.axis_index("rep") * part
        with jax.named_scope("weights_1"):
            send, sent = lax.optimization_barrier((others[1][0], sent))
            gathered = [lax.dynamic_slice_in_dim(block, mine, part)[None] for block in (weight_old, sent)]
            gathered = jnp.concatenate(gathered)
            sent = across(gathered, doubling, 1)
        with jax.named_scope("pair_exchange"):
            pair, gathered = lax.optimization_barrier((lax.ppermute(send, "rep", swap), gathered))
            high = (owns[1] + pair.astype(F32)).astype(BF16)
            low = owns[0] + lax.ppermute(others[0][0], "rep", swap).astype(F32)
        chosen, keep, own_gain, offset = indices(source_map)
        for stage in range(bits - 1):
            with jax.named_scope(f"gradient_{stage + 1}"):
                came = across(high, halving, stage)
            if stage < bits - 2:
                with jax.named_scope(f"weights_{stage + 2}"):
                    gathered = jnp.concatenate([gathered, sent])
                    sent = across(gathered, doubling, stage + 2)
            if stage != 1:
                came, sent = lax.optimization_barrier((came, sent))
            if stage == 1:
                came, chosen = lax.optimization_barrier((came, chosen))
            came = came.astype(F32)
            half = half // 2
            low, high = low[:half] + came[:half], (low[half:] + came[half:]).astype(BF16)
        with jax.named_scope("gradient_last"):
            came = across(high, halving, bits - 1)
        with jax.named_scope("weights_pair"):
            pieces = [gathered, sent]
            pieces += [lax.ppermute(piece, "rep", swap) for piece in pieces]
        came, *pieces = lax.optimization_barrier((came, *pieces))
        reduced = [resident(low), resident(came)]
        projected = call(
            lambda *refs: project_kernel(dp_count, doubling, cap, *refs),
            6,
            project_shape,
            [SMEM_SPEC] + [VMEM_SPEC] * 3 + [any_spec] * 4,
            dense + [pltpu.VMEM((2, dp_count, part, LANES), BF16), pltpu.SemaphoreType.DMA((4,))],
            old_bounds,
            hidden_old,
            inv_rms,
            live_gain,
            *pieces,
        )
    else:
        chip = owns[0]
        for away in range(1, rep_count):
            ring = [(r, (r + away) % rep_count) for r in range(rep_count)]
            chip = chip + lax.ppermute(others[0][away - 1], "rep", ring).astype(F32)
        blocks = lax.all_to_all(chip.astype(BF16), "dp", split_axis=0, concat_axis=0)
        grad_part = jnp.sum(blocks.astype(F32), axis=0)
        reduced = [lax.all_gather(grad_part, "rep", axis=0, tiled=True)]
        chosen, keep, own_gain, offset = indices(source_map)
        projected = call(
            lambda *refs: project_gathered_kernel(dp_count, cap, *refs),
            6,
            project_shape,
            [SMEM_SPEC] + [VMEM_SPEC] * 4,
            dense,
            old_bounds,
            hidden_old,
            inv_rms,
            live_gain,
            weights,
        )

    message = (1 if staged else 2) * slots + 2 * table_rows
    message = (message + 7) // 8 * 8
    packed = call(
        lambda *refs: pack_kernel(dp_count, slots, table_rows, staged, *refs),
        3,
        pltpu.VMEM((dp_count, message, LANES), BF16),
        [VMEM_SPEC] * (6 + len(reduced)),
        [],
        *[resident(value) for value in (chosen, keep, own_gain)],
        *reduced,
        *[resident(value) for value in (weight_old, moment_first, moment_second)],
    )
    packed, late_units = lax.optimization_barrier((packed, units))
    places, tables = call(
        lambda *refs: place_kernel(dp_count, slots, table_rows, *refs),
        2,
        (pltpu.VMEM((1, D_NEW), jnp.int32), pltpu.VMEM((2 * dp_count * table_rows, D_NEW), BF16)),
        [SMEM_SPEC] * 2 + [VMEM_SPEC],
        [],
        old_bounds,
        new_bounds,
        late_units,
    )
    moved = [lax.all_to_all(packed, "dp", split_axis=0, concat_axis=0)]
    if staged:
        arrived, projected, places = lax.optimization_barrier((moved[0], projected, places))
        moved = [arrived, lax.ppermute(arrived, "rep", swap)]
        moved = [resident(value) for value in moved]
    rows = shape((new_cap, LANES), F32)
    gain_grad, first_next, second_next, adam_step = call(
        lambda *refs: finish_kernel(dp_count, slots, table_rows, staged, *refs),
        4,
        (shape((1, D_NEW), F32), rows, rows, rows),
        [SMEM_SPEC] * 2 + [VMEM_SPEC] * (2 + len(moved)),
        [pltpu.VMEM((dp_count * slots, LANES), F32)] * 2
        + [pltpu.VMEM((dp_count * table_rows, LANES), F32)],
        new_bounds,
        offset,
        resident(places),
        resident(tables),
        *moved,
    )
    return (projected, gain_grad.reshape(D_NEW), first_next, second_next, adam_step)


def solution(mesh):
    placed = (
        P(("dp", "rep"), None),
        P(("dp", "rep"), None),
        P(),
        P(),
        P(),
        P(),
        P("dp", None),
        P("dp", None),
        P("dp", None),
    )
    return jax.shard_map(
        on_device,
        mesh=mesh,
        in_specs=placed,
        out_specs=(P(("dp", "rep"), None), P(), P("dp", None), P("dp", None), P("dp", None)),
        check_vma=False,
    )
```

```python
import jax
import jax.numpy as jnp
from jax import lax
from jax.experimental import pallas as pl
from jax.experimental.pallas import tpu as pltpu
from jax.sharding import PartitionSpec as P

D_OLD = 6144
D_NEW = 8192
LANES = 128
BYTES_PER_US = 3_000_000
VMEM_LIMIT = 56 * 1024 * 1024
F32 = jnp.float32
BF16 = jnp.bfloat16

SMEM_SPEC = pl.BlockSpec(memory_space=pltpu.SMEM)
VMEM_SPEC = pl.BlockSpec(memory_space=pltpu.VMEM)


def dot(left, right, contract):
    return lax.dot_general(left, right, ((contract[:1], contract[1:]), ((), ())), preferred_element_type=F32)


def one_hot(rows, values):
    lanes = values.shape[1]
    match = lax.broadcasted_iota(jnp.int32, (rows, lanes), 0).astype(BF16) == values.astype(BF16)
    return jnp.where(match, jnp.ones((), BF16), jnp.zeros((), BF16))


def split(value):
    high = value.astype(BF16)
    return high, (value - high.astype(F32)).astype(BF16)


def normed_tile(tile, hidden, inv_rms, gain):
    stream = hidden[:, tile * LANES : (tile + 1) * LANES].astype(F32)
    return ((stream * inv_rms) * gain[tile : tile + 1, :]).astype(BF16)


def lower_half(rows):
    return lax.broadcasted_iota(jnp.int32, (rows, LANES), 1) < LANES // 2


def token_kernel(rels, rep_count, cap, ob, src, gain, hidden_hbm, cot, live_gain, inv_out, *rest):
    *blocks, hist, hidden, own_grads, other_grads, sem = rest
    owns, others = blocks[: len(blocks) // 2], blocks[len(blocks) // 2 :]
    pieces = sem.shape[0]
    width = D_OLD // pieces
    copies = []
    for piece in range(pieces):
        columns = pl.ds(piece * width, width)
        copies.append(pltpu.make_async_copy(hidden_hbm.at[:, columns], hidden.at[:, columns], sem.at[piece]))
    for copy in copies:
        copy.start()
    me = lax.axis_index("dp")
    rep = lax.axis_index("rep")
    tiles = D_OLD // LANES
    tokens = hidden.shape[0]
    step = 1024
    total = jnp.zeros((tiles, LANES), F32)
    for at in range(0, D_NEW, step):
        units = src[:, at : at + step]
        total = total + dot(one_hot(tiles, units >> 7), one_hot(LANES, units & 127), (1, 1))
    hist[...] = total
    live_gain[...] = jnp.where(total > 0.5, gain[...], 0.0)
    squares = jnp.zeros((tokens, LANES), F32)
    for tile in range(tiles):
        if tile * LANES % width == 0:
            copies[tile * LANES // width].wait()
        stream = hidden[:, tile * LANES : (tile + 1) * LANES].astype(F32)
        squares = squares + stream * stream * hist[tile : tile + 1, :]
    inv_rms = lax.rsqrt(jnp.sum(squares, axis=1, keepdims=True) / D_NEW + 1e-05)
    inv_out[...] = jnp.broadcast_to(inv_rms, (tokens, LANES))
    staged = len(rels) > 1
    columns = cot[...]
    if staged:
        lower = lower_half(tokens)
        columns = columns.astype(F32)
        turned = pltpu.roll(columns, LANES // 2, 1)
        left, right = jnp.where(lower, columns, turned), jnp.where(lower, turned, columns)
        sides = [jnp.where(rep == 0, left, right), jnp.where(rep == 0, right, left)]
        columns = jnp.concatenate(sides, axis=1).astype(BF16)
    for tile in range(tiles):
        at = tile * LANES
        result = dot(normed_tile(tile, hidden, inv_rms, live_gain), columns, (0, 0))
        own_grads[at : at + LANES, :] = result[:, :LANES]
        if staged:
            other_grads[at : at + LANES, :] = result[:, LANES:]
    own_grads[D_OLD:, :] = jnp.zeros((cap, LANES), F32)
    other_grads[D_OLD:, :] = jnp.zeros((cap, LANES), F32)
    dp_count = len(rels[0])
    half = dp_count // len(owns)
    part = cap // rep_count
    for at in range(dp_count):
        if staged:
            first = ob[holder_at(rels, rep, me, at)]
            owns[at // half][at % half] = packed_rows(own_grads, first, part)
            first = ob[holder_at(rels, 1 - rep, me, at)]
            others[at // half][0, at % half] = packed_rows(other_grads, first, part).astype(BF16)
        else:
            first = ob[at]
            owns[0][at] = own_grads[pl.ds(first + rep * part, part), :]
            for away in range(1, rep_count):
                mate = (rep + away) % rep_count
                others[0][away - 1, at] = own_grads[pl.ds(first + mate * part, part), :].astype(BF16)


def packed_rows(grads, first, part):
    return jnp.where(lower_half(part), grads[pl.ds(first, part), :], grads[pl.ds(first + part, part), :])


def holder_at(rels, rep, me, at):
    return me ^ jnp.where(rep == 0, rels[0][at], rels[1][at])


def fill_normed(x, hidden, inv_rms, gain):
    for tile in range(D_OLD // LANES):
        x[:, tile * LANES : (tile + 1) * LANES] = normed_tile(tile, hidden, inv_rms[...], gain)


def project_kernel(dp_count, orders, cap, ob, hidden, inv_rms, gain, *rest):
    *pieces, out, dense, x, blocks, sems = rest
    me = lax.axis_index("dp")
    rep = lax.axis_index("rep")
    part = cap // 2
    half = dp_count // 2
    copies = []
    for at, piece in enumerate(pieces):
        side = rep if at < 2 else 1 - rep
        place = blocks.at[side, pl.ds((at % 2) * half, half)]
        copies.append(pltpu.make_async_copy(piece, place, sems.at[at]))
    for copy in copies:
        copy.start()
    fill_normed(x, hidden, inv_rms, gain)
    for copy in copies:
        copy.wait()
    for p in range(dp_count):
        away = me ^ p
        for side, order in enumerate(orders):
            at = sum(((away >> bit) & 1) << s for s, bit in enumerate(order))
            dense[pl.ds(ob[p] + side * part, part), :] = blocks[side, at].astype(F32)
    out[...] = dot(x[...], dense[0:D_OLD, :].astype(BF16), (1, 0)).astype(BF16)


def project_gathered_kernel(dp_count, cap, ob, hidden, inv_rms, gain, weights, out, dense, x):
    fill_normed(x, hidden, inv_rms, gain)
    for p in range(dp_count):
        dense[pl.ds(ob[p], cap), :] = weights[p * cap : (p + 1) * cap, :].astype(F32)
    out[...] = dot(x[...], dense[0:D_OLD, :].astype(BF16), (1, 0)).astype(BF16)


def offset_of(src, ob, nb, q, dp_count):
    first = src[nb[q]]
    holder = jnp.int32(0)
    for p in range(1, dp_count):
        holder = holder + (ob[p] <= first).astype(jnp.int32)
    return holder


def index_kernel(dp_count, cap, slots, table_rows, ob, nb, src, gain, chosen, keep, own_gain, offset, rows, gains):
    me = lax.axis_index("dp")
    mine = ob[me]
    groups = cap // LANES
    offset[0] = offset_of(src, ob, nb, me, dp_count)
    rows[...] = jnp.full(rows.shape, -1, jnp.int32)
    for q in range(dp_count):
        start = nb[q] + ((me - offset_of(src, ob, nb, q, dp_count)) & (dp_count - 1))
        end = nb[q + 1]
        for k in range(slots):
            unit = start + dp_count * k
            row = jnp.where(unit < end, src[jnp.minimum(unit, D_NEW - 1)] - mine, -1)
            rows[q * slots + k : q * slots + k + 1, :] = jnp.full((1, LANES), row, jnp.int32)
    lanes = lax.broadcasted_iota(jnp.int32, rows.shape, 1)
    for g in range(groups):
        chosen[:, g * LANES : (g + 1) * LANES] = jnp.where(rows[...] == lanes + g * LANES, 1.0, 0.0).astype(BF16)
    gains[0 : gain.shape[0], :] = gain[...]
    gains[gain.shape[0] :, :] = jnp.ones((gains.shape[0] - gain.shape[0], LANES), F32)
    gain_rows = gains[pl.ds(mine >> 7, groups + 1), :]
    shift = mine & 127
    rolled = pltpu.roll(gain_rows, (LANES - shift) & 127, 1)
    lane_row = lax.broadcasted_iota(jnp.int32, (groups, LANES), 1)
    inverse = 1.0 / jnp.where(lane_row < LANES - shift, rolled[:groups], rolled[1:])
    for g in range(groups):
        own_gain[:, g * LANES : (g + 1) * LANES] = inverse[g : g + 1]
    same = dot(chosen[...], chosen[...], (1, 1))
    earlier = lax.broadcasted_iota(jnp.int32, same.shape, 0) < lax.broadcasted_iota(jnp.int32, same.shape, 1)
    repeated = jnp.max(jnp.where(earlier, same, 0.0), axis=0, keepdims=True)
    keep[...] = jnp.where(repeated < 0.5, 1.0, 0.0)


def place_kernel(dp_count, slots, table_rows, ob, nb, units, places, tables):
    step = 1024
    for first in range(0, D_NEW, step):
        source = units[:, first : first + step]
        position = first + lax.broadcasted_iota(jnp.int32, (1, step), 1)
        holder = jnp.zeros((1, step), jnp.int32)
        dest = jnp.zeros((1, step), jnp.int32)
        begin = jnp.zeros((1, step), jnp.int32)
        for p in range(1, dp_count):
            holder = holder + jnp.where(source >= ob[p], 1, 0)
            past = position >= nb[p]
            dest = jnp.where(past, p, dest)
            begin = jnp.where(past, nb[p], begin)
        rank = (position - begin) >> (dp_count.bit_length() - 1)
        place = holder * (table_rows * LANES) + dest * slots + rank
        places[:, first : first + step] = place & 127
        spread = one_hot(dp_count * table_rows, place >> 7)
        tables[:, first : first + step] = jnp.concatenate([spread, spread], axis=0)


def pack_kernel(dp_count, slots, table_rows, staged, chosen, keep, own_gain, *rest):
    *reduced, weight_in, first_in, second_in, out = rest
    pairs = dp_count * slots
    rows = weight_in.shape[0]
    weight, first, second = weight_in[...].astype(F32), first_in[...], second_in[...]
    if staged:
        turn = LANES // 2
        lower = lower_half(rows)
        grad = reduced[0][0] + reduced[1][0].astype(F32)
        grad = jnp.concatenate([grad, pltpu.roll(grad, turn, 1)], axis=0)
        left = lax.axis_index("rep") == 0
        weight, first, second = [
            jnp.where(left, value, pltpu.roll(value, turn, 1)) for value in (weight, first, second)
        ]
        product = jnp.where(lower, weight * grad, 0.0)
    else:
        grad = reduced[0][...]
        product = weight * grad
    high, low = split(product)
    ones = jnp.ones((8, LANES), BF16)
    column = (dot(ones, high, (1, 1)) + dot(ones, low, (1, 1))) * own_gain[...]
    picked = dot(jnp.concatenate(split(column), axis=0), chosen[...], (1, 1))
    table = []
    for part in (picked[0:1], picked[8:9]):
        part = part * keep[...]
        table += [part[:, r * LANES : (r + 1) * LANES] for r in range(table_rows)]
    updated = [0.9 * first + 0.1 * grad, 0.95 * second + 0.05 * grad * grad]
    if staged:
        updated = [jnp.where(lower, updated[0], pltpu.roll(updated[1], turn, 1))]
    filled = len(updated) * slots
    spare = out.shape[1] - filled - 2 * table_rows
    table = jnp.concatenate(table + [jnp.zeros((spare, LANES), F32)], axis=0).astype(BF16)
    picked = chosen[0:pairs]
    for at, value in enumerate(updated):
        moved = dot(picked, value.astype(BF16), (1, 0)).astype(BF16).reshape(dp_count, slots, LANES)
        out[:, at * slots : (at + 1) * slots, :] = moved
    for q in range(dp_count):
        out[q, filled:, :] = table


def finish_kernel(dp_count, slots, table_rows, staged, nb, offset_in, places, tables, *rest):
    arrived, rest = (rest[:2], rest[2:]) if staged else (rest[:1], rest[1:])
    gain_grad, first, second, adam, ones, twos, steps, table, sems = rest
    me = lax.axis_index("dp")
    offset = offset_in[0]
    groups = 1 if staged else 2
    pages = [(moved, 0) for moved in arrived] if staged else [(arrived[0], 0), (arrived[0], slots)]
    for i in range(dp_count):
        p = (i + offset) & (dp_count - 1)
        strided = pl.ds(i, slots, stride=dp_count)
        for (moved, at), rows in zip(pages, (ones, twos)):
            rows[strided, :] = moved[p, at : at + slots, :].astype(F32)
    cap = first.shape[0]
    live = lax.broadcasted_iota(jnp.int32, (cap, LANES), 0) < nb[me + 1] - nb[me]
    one, two = ones[0:cap, :], twos[0:cap, :]
    if staged:
        left = lax.axis_index("rep") == 0
        lower = lower_half(cap)
        one, two = jnp.where(left, one, two), jnp.where(left, two, one)
        turn = LANES // 2
        one, two = (
            jnp.where(lower, one, pltpu.roll(two, turn, 1)),
            jnp.where(lower, pltpu.roll(one, turn, 1), two),
        )
    first_next = jnp.where(live, one, 0.0)
    second_next = jnp.where(live, two, 0.0)
    ones[0:cap, :] = first_next
    twos[0:cap, :] = second_next
    steps[0:cap, :] = first_next / (jnp.sqrt(second_next) + 1e-08)
    copies = [
        pltpu.make_async_copy(rows.at[pl.ds(0, cap), :], out, sems.at[at])
        for at, (rows, out) in enumerate(((ones, first), (twos, second), (steps, adam)))
    ]
    for copy in copies:
        copy.start()
    at = groups * slots
    for p in range(dp_count):
        here = p * table_rows
        terms = [
            moved[p, at + r : at + r + table_rows, :].astype(F32) for moved in arrived for r in (0, table_rows)
        ]
        table[here : here + table_rows, :] = sum(terms[1:], terms[0])
    high, low = split(table[...])
    values = jnp.concatenate([high.astype(F32), low.astype(F32)], axis=0).T.astype(BF16)
    step = 1024
    for start in range(0, D_NEW, step):
        spread = dot(values, tables[:, start : start + step], (1, 0))
        mask = lax.broadcasted_iota(jnp.int32, (LANES, step), 0) == places[:, start : start + step]
        value = jnp.where(mask, spread, 0.0)
        gain_grad[:, start : start + step] = jnp.sum(value, axis=0, keepdims=True)
    for copy in copies:
        copy.wait()


def resident(value):
    return pltpu.with_memory_space_constraint(value, pltpu.VMEM)


def call(kernel, micros, out_shape, specs, scratch, *args, direct=None):
    scalars = jax.ShapeDtypeStruct((1,), jnp.int32)
    any_spec = pl.BlockSpec(memory_space=pl.ANY)
    spec_of = lambda out: SMEM_SPEC if out == scalars else any_spec if out == direct else VMEM_SPEC
    out_specs = jax.tree.map(spec_of, out_shape)
    return pl.pallas_call(
        kernel,
        out_shape=out_shape,
        in_specs=specs,
        out_specs=out_specs,
        scratch_shapes=scratch,
        cost_estimate=pl.CostEstimate(flops=0, transcendentals=0, bytes_accessed=micros * BYTES_PER_US),
        compiler_params=pltpu.CompilerParams(vmem_limit_bytes=VMEM_LIMIT),
    )(*args)


def on_device(
    hidden_old,
    cotangent,
    gain_old,
    old_bounds,
    new_bounds,
    source_map,
    weight_old,
    moment_first,
    moment_second,
):
    dp_count = lax.axis_size("dp")
    rep_count = lax.axis_size("rep")
    cap = weight_old.shape[0]
    mean = D_NEW // dp_count
    new_cap = mean + mean // 4
    slots = (new_cap + dp_count - 1) // dp_count
    table_rows = (dp_count * slots + LANES - 1) // LANES
    tokens = hidden_old.shape[0]
    part = cap // rep_count
    shape = jax.ShapeDtypeStruct

    units = source_map.reshape(1, D_NEW)
    gain = gain_old.reshape(D_OLD // LANES, LANES)
    staged = rep_count == 2 and dp_count >= 8
    bits = dp_count.bit_length() - 1
    line = list(range(bits - 1))
    ends = [line[:1] + line[-1:], line[-1:] + line[:1]]
    halving = [pair + line[1:-1] + [bits - 1] for pair in ends]
    doubling = [[bits - 1] + line, [bits - 1] + line[::-1]]
    if staged:
        rels = [
            [sum(((at >> (bits - 1 - s)) & 1) << bit for s, bit in enumerate(order)) for at in range(dp_count)]
            for order in halving
        ]
        parts = 2
    else:
        rels = [list(range(dp_count))]
        parts = 1

    def across(value, orders, stage):
        pairs = [
            (dp * rep_count + rep, (dp ^ (1 << orders[rep][stage])) * rep_count + rep)
            for dp in range(dp_count)
            for rep in range(rep_count)
        ]
        return lax.ppermute(value, ("dp", "rep"), pairs)

    swap = [(0, 1), (1, 0)]
    any_spec = pl.BlockSpec(memory_space=pl.ANY)
    if staged:
        sent = across(weight_old, doubling, 0)
    else:
        weights = lax.all_gather(weight_old, "dp", axis=0, tiled=True)

    tiles = D_OLD // LANES
    live_gain, inv_rms, *blocks = call(
        lambda *refs: token_kernel(rels, rep_count, cap, *refs),
        8,
        (
            shape((tiles, LANES), F32),
            shape((tokens, LANES), F32),
            *[pltpu.VMEM((dp_count // parts, part, LANES), F32)] * parts,
            *[shape((rep_count - 1, dp_count // parts, part, LANES), BF16)] * parts,
        ),
        [SMEM_SPEC] + [VMEM_SPEC] * 2 + [any_spec] + [VMEM_SPEC],
        [
            pltpu.VMEM((tiles, LANES), F32),
            pltpu.VMEM((tokens, D_OLD), BF16),
            pltpu.VMEM((D_OLD + cap, LANES), F32),
            pltpu.VMEM((D_OLD + cap, LANES), F32),
            pltpu.SemaphoreType.DMA((6,)),
        ],
        old_bounds,
        units,
        gain,
        hidden_old,
        cotangent,
    )
    owns, others = blocks[:parts], blocks[parts:]
    def indices(src):
        return call(
            lambda *refs: index_kernel(dp_count, cap, slots, table_rows, *refs),
            0,
            (
                pltpu.VMEM((table_rows * LANES, cap), BF16),
                pltpu.VMEM((1, table_rows * LANES), F32),
                pltpu.VMEM((1, cap), F32),
                shape((1,), jnp.int32),
            ),
            [SMEM_SPEC] * 3 + [VMEM_SPEC],
            [pltpu.VMEM((table_rows * LANES, LANES), jnp.int32), pltpu.VMEM((D_OLD // LANES + 8, LANES), F32)],
            old_bounds,
            new_bounds,
            src,
            gain,
        )

    project_shape = shape((tokens, LANES), BF16)
    dense = [pltpu.VMEM((D_OLD + cap, LANES), F32), pltpu.VMEM((tokens, D_OLD), BF16)]
    if staged:
        half = dp_count // 2
        mine = lax.axis_index("rep") * part
        with jax.named_scope("weights_1"):
            send, sent = lax.optimization_barrier((others[1][0], sent))
            gathered = [lax.dynamic_slice_in_dim(block, mine, part)[None] for block in (weight_old, sent)]
            gathered = jnp.concatenate(gathered)
            sent = across(gathered, doubling, 1)
        with jax.named_scope("pair_exchange"):
            pair, gathered = lax.optimization_barrier((lax.ppermute(send, "rep", swap), gathered))
            high = (owns[1] + pair.astype(F32)).astype(BF16)
            low = owns[0] + lax.ppermute(others[0][0], "rep", swap).astype(F32)
        chosen, keep, own_gain, offset = indices(source_map)
        for stage in range(bits - 1):
            with jax.named_scope(f"gradient_{stage + 1}"):
                came = across(high, halving, stage)
            if stage < bits - 2:
                with jax.named_scope(f"weights_{stage + 2}"):
                    gathered = jnp.concatenate([gathered, sent])
                    sent = across(gathered, doubling, stage + 2)
            if stage != 1:
                came, sent = lax.optimization_barrier((came, sent))
            if stage == 1:
                came, chosen = lax.optimization_barrier((came, chosen))
            came = came.astype(F32)
            half = half // 2
            low, high = low[:half] + came[:half], (low[half:] + came[half:]).astype(BF16)
        with jax.named_scope("gradient_last"):
            came = across(high, halving, bits - 1)
        with jax.named_scope("weights_pair"):
            pieces = [gathered, sent]
            pieces += [lax.ppermute(piece, "rep", swap) for piece in pieces]
        came, *pieces[:3] = lax.optimization_barrier((came, *pieces[:3]))
        reduced = [resident(low), resident(came)]
        projected = call(
            lambda *refs: project_kernel(dp_count, doubling, cap, *refs),
            6,
            project_shape,
            [SMEM_SPEC] + [VMEM_SPEC] * 3 + [any_spec] * 4,
            dense + [pltpu.VMEM((2, dp_count, part, LANES), BF16), pltpu.SemaphoreType.DMA((4,))],
            old_bounds,
            hidden_old,
            inv_rms,
            live_gain,
            *pieces,
        )
    else:
        chip = owns[0]
        for away in range(1, rep_count):
            ring = [(r, (r + away) % rep_count) for r in range(rep_count)]
            chip = chip + lax.ppermute(others[0][away - 1], "rep", ring).astype(F32)
        blocks = lax.all_to_all(chip.astype(BF16), "dp", split_axis=0, concat_axis=0)
        grad_part = jnp.sum(blocks.astype(F32), axis=0)
        reduced = [lax.all_gather(grad_part, "rep", axis=0, tiled=True)]
        chosen, keep, own_gain, offset = indices(source_map)
        projected = call(
            lambda *refs: project_gathered_kernel(dp_count, cap, *refs),
            6,
            project_shape,
            [SMEM_SPEC] + [VMEM_SPEC] * 4,
            dense,
            old_bounds,
            hidden_old,
            inv_rms,
            live_gain,
            weights,
        )

    message = (1 if staged else 2) * slots + 2 * table_rows
    message = (message + 7) // 8 * 8
    packed = call(
        lambda *refs: pack_kernel(dp_count, slots, table_rows, staged, *refs),
        3,
        pltpu.VMEM((dp_count, message, LANES), BF16),
        [VMEM_SPEC] * (6 + len(reduced)),
        [],
        *[resident(value) for value in (chosen, keep, own_gain)],
        *reduced,
        *[resident(value) for value in (weight_old, moment_first, moment_second)],
    )
    packed, late_units = lax.optimization_barrier((packed, units))
    places, tables = call(
        lambda *refs: place_kernel(dp_count, slots, table_rows, *refs),
        2,
        (pltpu.VMEM((1, D_NEW), jnp.int32), pltpu.VMEM((2 * dp_count * table_rows, D_NEW), BF16)),
        [SMEM_SPEC] * 2 + [VMEM_SPEC],
        [],
        old_bounds,
        new_bounds,
        late_units,
    )
    moved = [lax.all_to_all(packed, "dp", split_axis=0, concat_axis=0)]
    if staged:
        arrived, projected, places = lax.optimization_barrier((moved[0], projected, places))
        moved = [arrived, lax.ppermute(arrived, "rep", swap)]
        moved = [resident(value) for value in moved]
    rows = shape((new_cap, LANES), F32)
    gain_grad, first_next, second_next, adam_step = call(
        lambda *refs: finish_kernel(dp_count, slots, table_rows, staged, *refs),
        4,
        (shape((1, D_NEW), F32), rows, rows, rows),
        [SMEM_SPEC] * 2 + [VMEM_SPEC] * (2 + len(moved)),
        [pltpu.VMEM((dp_count * slots, LANES), F32)] * 3
        + [pltpu.VMEM((dp_count * table_rows, LANES), F32), pltpu.SemaphoreType.DMA((3,))],
        new_bounds,
        offset,
        resident(places),
        resident(tables),
        *moved,
        direct=rows,
    )
    return (projected, gain_grad.reshape(D_NEW), first_next, second_next, adam_step)


def solution(mesh):
    placed = (
        P(("dp", "rep"), None),
        P(("dp", "rep"), None),
        P(),
        P(),
        P(),
        P(),
        P("dp", None),
        P("dp", None),
        P("dp", None),
    )
    return jax.shard_map(
        on_device,
        mesh=mesh,
        in_specs=placed,
        out_specs=(P(("dp", "rep"), None), P(), P("dp", None), P("dp", None), P("dp", None)),
        check_vma=False,
    )
```

```python
import jax
import jax.numpy as jnp
from jax import lax
from jax.experimental import pallas as pl
from jax.experimental.pallas import tpu as pltpu
from jax.sharding import PartitionSpec as P

D_OLD = 6144
D_NEW = 8192
LANES = 128
BYTES_PER_US = 3_000_000
VMEM_LIMIT = 56 * 1024 * 1024
F32 = jnp.float32
BF16 = jnp.bfloat16

SMEM_SPEC = pl.BlockSpec(memory_space=pltpu.SMEM)
VMEM_SPEC = pl.BlockSpec(memory_space=pltpu.VMEM)


def dot(left, right, contract):
    return lax.dot_general(left, right, ((contract[:1], contract[1:]), ((), ())), preferred_element_type=F32)


def one_hot(rows, values):
    lanes = values.shape[1]
    match = lax.broadcasted_iota(jnp.int32, (rows, lanes), 0).astype(BF16) == values.astype(BF16)
    return jnp.where(match, jnp.ones((), BF16), jnp.zeros((), BF16))


def split(value):
    high = value.astype(BF16)
    return high, (value - high.astype(F32)).astype(BF16)


def normed_tile(tile, hidden, inv_rms, gain):
    stream = hidden[:, tile * LANES : (tile + 1) * LANES].astype(F32)
    return ((stream * inv_rms) * gain[tile : tile + 1, :]).astype(BF16)


def lower_half(rows):
    return lax.broadcasted_iota(jnp.int32, (rows, LANES), 1) < LANES // 2


def token_kernel(rels, rep_count, cap, ob, src, gain, hidden_hbm, cot, live_gain, inv_out, *rest):
    *blocks, hist, hidden, own_grads, other_grads, sem = rest
    owns, others = blocks[: len(blocks) // 2], blocks[len(blocks) // 2 :]
    pieces = sem.shape[0]
    width = D_OLD // pieces
    copies = []
    for piece in range(pieces):
        columns = pl.ds(piece * width, width)
        copies.append(pltpu.make_async_copy(hidden_hbm.at[:, columns], hidden.at[:, columns], sem.at[piece]))
    for copy in copies:
        copy.start()
    me = lax.axis_index("dp")
    rep = lax.axis_index("rep")
    tiles = D_OLD // LANES
    tokens = hidden.shape[0]
    step = 1024
    total = jnp.zeros((tiles, LANES), F32)
    for at in range(0, D_NEW, step):
        units = src[:, at : at + step]
        total = total + dot(one_hot(tiles, units >> 7), one_hot(LANES, units & 127), (1, 1))
    hist[...] = total
    live_gain[...] = jnp.where(total > 0.5, gain[...], 0.0)
    squares = jnp.zeros((tokens, LANES), F32)
    for tile in range(tiles):
        if tile * LANES % width == 0:
            copies[tile * LANES // width].wait()
        stream = hidden[:, tile * LANES : (tile + 1) * LANES].astype(F32)
        squares = squares + stream * stream * hist[tile : tile + 1, :]
    inv_rms = lax.rsqrt(jnp.sum(squares, axis=1, keepdims=True) / D_NEW + 1e-05)
    inv_out[...] = jnp.broadcast_to(inv_rms, (tokens, LANES))
    staged = len(rels) > 1
    columns = cot[...]
    if staged:
        lower = lower_half(tokens)
        columns = columns.astype(F32)
        turned = pltpu.roll(columns, LANES // 2, 1)
        left, right = jnp.where(lower, columns, turned), jnp.where(lower, turned, columns)
        sides = [jnp.where(rep == 0, left, right), jnp.where(rep == 0, right, left)]
        columns = jnp.concatenate(sides, axis=1).astype(BF16)
    for tile in range(tiles):
        at = tile * LANES
        result = dot(normed_tile(tile, hidden, inv_rms, live_gain), columns, (0, 0))
        own_grads[at : at + LANES, :] = result[:, :LANES]
        if staged:
            other_grads[at : at + LANES, :] = result[:, LANES:]
    own_grads[D_OLD:, :] = jnp.zeros((cap, LANES), F32)
    other_grads[D_OLD:, :] = jnp.zeros((cap, LANES), F32)
    dp_count = len(rels[0])
    half = dp_count // len(owns)
    part = cap // rep_count
    for at in range(dp_count):
        if staged:
            first = ob[holder_at(rels, rep, me, at)]
            owns[at // half][at % half] = packed_rows(own_grads, first, part)
            first = ob[holder_at(rels, 1 - rep, me, at)]
            others[at // half][0, at % half] = packed_rows(other_grads, first, part).astype(BF16)
        else:
            first = ob[at]
            owns[0][at] = own_grads[pl.ds(first + rep * part, part), :]
            for away in range(1, rep_count):
                mate = (rep + away) % rep_count
                others[0][away - 1, at] = own_grads[pl.ds(first + mate * part, part), :].astype(BF16)


def packed_rows(grads, first, part):
    return jnp.where(lower_half(part), grads[pl.ds(first, part), :], grads[pl.ds(first + part, part), :])


def holder_at(rels, rep, me, at):
    return me ^ jnp.where(rep == 0, rels[0][at], rels[1][at])


def fill_normed(x, hidden, inv_rms, gain):
    for tile in range(D_OLD // LANES):
        x[:, tile * LANES : (tile + 1) * LANES] = normed_tile(tile, hidden, inv_rms[...], gain)


def project_kernel(dp_count, orders, cap, ob, hidden, inv_rms, gain, *rest):
    *pieces, out, dense, x, blocks, sems = rest
    me = lax.axis_index("dp")
    rep = lax.axis_index("rep")
    part = cap // 2
    half = dp_count // 2
    copies = []
    for at, piece in enumerate(pieces):
        side = rep if at < 2 else 1 - rep
        place = blocks.at[side, pl.ds((at % 2) * half, half)]
        copies.append(pltpu.make_async_copy(piece, place, sems.at[at]))
    for copy in copies:
        copy.start()
    fill_normed(x, hidden, inv_rms, gain)
    for copy in copies:
        copy.wait()
    for p in range(dp_count):
        away = me ^ p
        for side, order in enumerate(orders):
            at = sum(((away >> bit) & 1) << s for s, bit in enumerate(order))
            dense[pl.ds(ob[p] + side * part, part), :] = blocks[side, at].astype(F32)
    out[...] = dot(x[...], dense[0:D_OLD, :].astype(BF16), (1, 0)).astype(BF16)


def project_gathered_kernel(dp_count, cap, ob, hidden, inv_rms, gain, weights, out, dense, x):
    fill_normed(x, hidden, inv_rms, gain)
    for p in range(dp_count):
        dense[pl.ds(ob[p], cap), :] = weights[p * cap : (p + 1) * cap, :].astype(F32)
    out[...] = dot(x[...], dense[0:D_OLD, :].astype(BF16), (1, 0)).astype(BF16)


def offset_of(src, ob, nb, q, dp_count):
    first = src[nb[q]]
    holder = jnp.int32(0)
    for p in range(1, dp_count):
        holder = holder + (ob[p] <= first).astype(jnp.int32)
    return holder


def index_kernel(dp_count, cap, slots, table_rows, ob, nb, src, gain, chosen, keep, own_gain, offset, rows, gains):
    me = lax.axis_index("dp")
    mine = ob[me]
    groups = cap // LANES
    offset[0] = offset_of(src, ob, nb, me, dp_count)
    rows[...] = jnp.full(rows.shape, -1, jnp.int32)
    for q in range(dp_count):
        start = nb[q] + ((me - offset_of(src, ob, nb, q, dp_count)) & (dp_count - 1))
        end = nb[q + 1]
        for k in range(slots):
            unit = start + dp_count * k
            row = jnp.where(unit < end, src[jnp.minimum(unit, D_NEW - 1)] - mine, -1)
            rows[q * slots + k : q * slots + k + 1, :] = jnp.full((1, LANES), row, jnp.int32)
    lanes = lax.broadcasted_iota(jnp.int32, rows.shape, 1)
    for g in range(groups):
        chosen[:, g * LANES : (g + 1) * LANES] = jnp.where(rows[...] == lanes + g * LANES, 1.0, 0.0).astype(BF16)
    gains[0 : gain.shape[0], :] = gain[...]
    gains[gain.shape[0] :, :] = jnp.ones((gains.shape[0] - gain.shape[0], LANES), F32)
    gain_rows = gains[pl.ds(mine >> 7, groups + 1), :]
    shift = mine & 127
    rolled = pltpu.roll(gain_rows, (LANES - shift) & 127, 1)
    lane_row = lax.broadcasted_iota(jnp.int32, (groups, LANES), 1)
    inverse = 1.0 / jnp.where(lane_row < LANES - shift, rolled[:groups], rolled[1:])
    for g in range(groups):
        own_gain[:, g * LANES : (g + 1) * LANES] = inverse[g : g + 1]
    same = dot(chosen[...], chosen[...], (1, 1))
    earlier = lax.broadcasted_iota(jnp.int32, same.shape, 0) < lax.broadcasted_iota(jnp.int32, same.shape, 1)
    repeated = jnp.max(jnp.where(earlier, same, 0.0), axis=0, keepdims=True)
    keep[...] = jnp.where(repeated < 0.5, 1.0, 0.0)


def place_kernel(dp_count, slots, table_rows, ob, nb, units, places, tables):
    step = 1024
    for first in range(0, D_NEW, step):
        source = units[:, first : first + step]
        position = first + lax.broadcasted_iota(jnp.int32, (1, step), 1)
        holder = jnp.zeros((1, step), jnp.int32)
        dest = jnp.zeros((1, step), jnp.int32)
        begin = jnp.zeros((1, step), jnp.int32)
        for p in range(1, dp_count):
            holder = holder + jnp.where(source >= ob[p], 1, 0)
            past = position >= nb[p]
            dest = jnp.where(past, p, dest)
            begin = jnp.where(past, nb[p], begin)
        rank = (position - begin) >> (dp_count.bit_length() - 1)
        place = holder * (table_rows * LANES) + dest * slots + rank
        places[:, first : first + step] = place & 127
        spread = one_hot(dp_count * table_rows, place >> 7)
        tables[:, first : first + step] = jnp.concatenate([spread, spread], axis=0)


def pack_kernel(dp_count, slots, table_rows, staged, chosen, keep, own_gain, *rest):
    *reduced, weight_in, first_in, second_in, out = rest
    pairs = dp_count * slots
    rows = weight_in.shape[0]
    weight, first, second = weight_in[...].astype(F32), first_in[...], second_in[...]
    if staged:
        turn = LANES // 2
        lower = lower_half(rows)
        grad = reduced[0][0] + reduced[1][0].astype(F32)
        grad = jnp.concatenate([grad, pltpu.roll(grad, turn, 1)], axis=0)
        left = lax.axis_index("rep") == 0
        weight, first, second = [
            jnp.where(left, value, pltpu.roll(value, turn, 1)) for value in (weight, first, second)
        ]
        product = jnp.where(lower, weight * grad, 0.0)
    else:
        grad = reduced[0][...]
        product = weight * grad
    high, low = split(product)
    ones = jnp.ones((8, LANES), BF16)
    column = (dot(ones, high, (1, 1)) + dot(ones, low, (1, 1))) * own_gain[...]
    picked = dot(jnp.concatenate(split(column), axis=0), chosen[...], (1, 1))
    table = []
    for part in (picked[0:1], picked[8:9]):
        part = part * keep[...]
        table += [part[:, r * LANES : (r + 1) * LANES] for r in range(table_rows)]
    updated = [0.9 * first + 0.1 * grad, 0.95 * second + 0.05 * grad * grad]
    if staged:
        updated = [jnp.where(lower, updated[0], pltpu.roll(updated[1], turn, 1))]
    filled = len(updated) * slots
    spare = out.shape[1] - filled - 2 * table_rows
    table = jnp.concatenate(table + [jnp.zeros((spare, LANES), F32)], axis=0).astype(BF16)
    picked = chosen[0:pairs]
    for at, value in enumerate(updated):
        moved = dot(picked, value.astype(BF16), (1, 0)).astype(BF16).reshape(dp_count, slots, LANES)
        out[:, at * slots : (at + 1) * slots, :] = moved
    for q in range(dp_count):
        out[q, filled:, :] = table


def finish_kernel(dp_count, slots, table_rows, staged, nb, offset_in, places, tables, *rest):
    arrived, rest = (rest[:2], rest[2:]) if staged else (rest[:1], rest[1:])
    gain_grad, first, second, adam, ones, twos, table = rest
    me = lax.axis_index("dp")
    offset = offset_in[0]
    groups = 1 if staged else 2
    pages = [(moved, 0) for moved in arrived] if staged else [(arrived[0], 0), (arrived[0], slots)]
    for i in range(dp_count):
        p = (i + offset) & (dp_count - 1)
        strided = pl.ds(i, slots, stride=dp_count)
        for (moved, at), rows in zip(pages, (ones, twos)):
            rows[strided, :] = moved[p, at : at + slots, :].astype(F32)
    cap = first.shape[0]
    live = lax.broadcasted_iota(jnp.int32, (cap, LANES), 0) < nb[me + 1] - nb[me]
    one, two = ones[0:cap, :], twos[0:cap, :]
    if staged:
        left = lax.axis_index("rep") == 0
        lower = lower_half(cap)
        one, two = jnp.where(left, one, two), jnp.where(left, two, one)
        turn = LANES // 2
        one, two = (
            jnp.where(lower, one, pltpu.roll(two, turn, 1)),
            jnp.where(lower, pltpu.roll(one, turn, 1), two),
        )
    first_next = jnp.where(live, one, 0.0)
    second_next = jnp.where(live, two, 0.0)
    first[...] = first_next
    second[...] = second_next
    adam[...] = first_next / (jnp.sqrt(second_next) + 1e-08)
    at = groups * slots
    for p in range(dp_count):
        here = p * table_rows
        terms = [
            moved[p, at + r : at + r + table_rows, :].astype(F32) for moved in arrived for r in (0, table_rows)
        ]
        table[here : here + table_rows, :] = sum(terms[1:], terms[0])
    high, low = split(table[...])
    values = jnp.concatenate([high.astype(F32), low.astype(F32)], axis=0).T.astype(BF16)
    step = 1024
    for start in range(0, D_NEW, step):
        spread = dot(values, tables[:, start : start + step], (1, 0))
        mask = lax.broadcasted_iota(jnp.int32, (LANES, step), 0) == places[:, start : start + step]
        value = jnp.where(mask, spread, 0.0)
        gain_grad[:, start : start + step] = jnp.sum(value, axis=0, keepdims=True)


def resident(value):
    return pltpu.with_memory_space_constraint(value, pltpu.VMEM)


def call(kernel, micros, out_shape, specs, scratch, *args):
    scalars = jax.ShapeDtypeStruct((1,), jnp.int32)
    out_specs = jax.tree.map(lambda out: SMEM_SPEC if out == scalars else VMEM_SPEC, out_shape)
    return pl.pallas_call(
        kernel,
        out_shape=out_shape,
        in_specs=specs,
        out_specs=out_specs,
        scratch_shapes=scratch,
        cost_estimate=pl.CostEstimate(flops=0, transcendentals=0, bytes_accessed=micros * BYTES_PER_US),
        compiler_params=pltpu.CompilerParams(vmem_limit_bytes=VMEM_LIMIT),
    )(*args)


def on_device(
    hidden_old,
    cotangent,
    gain_old,
    old_bounds,
    new_bounds,
    source_map,
    weight_old,
    moment_first,
    moment_second,
):
    dp_count = lax.axis_size("dp")
    rep_count = lax.axis_size("rep")
    cap = weight_old.shape[0]
    mean = D_NEW // dp_count
    new_cap = mean + mean // 4
    slots = (new_cap + dp_count - 1) // dp_count
    table_rows = (dp_count * slots + LANES - 1) // LANES
    tokens = hidden_old.shape[0]
    part = cap // rep_count
    shape = jax.ShapeDtypeStruct

    units = source_map.reshape(1, D_NEW)
    gain = gain_old.reshape(D_OLD // LANES, LANES)
    staged = rep_count == 2 and dp_count >= 8
    bits = dp_count.bit_length() - 1
    line = list(range(bits - 1))
    ends = [line[:1] + line[-1:], line[-1:] + line[:1]]
    halving = [pair + line[1:-1] + [bits - 1] for pair in ends]
    doubling = [[bits - 1] + line, [bits - 1] + line[::-1]]
    if staged:
        rels = [
            [sum(((at >> (bits - 1 - s)) & 1) << bit for s, bit in enumerate(order)) for at in range(dp_count)]
            for order in halving
        ]
        parts = 2
    else:
        rels = [list(range(dp_count))]
        parts = 1

    def across(value, orders, stage):
        pairs = [
            (dp * rep_count + rep, (dp ^ (1 << orders[rep][stage])) * rep_count + rep)
            for dp in range(dp_count)
            for rep in range(rep_count)
        ]
        return lax.ppermute(value, ("dp", "rep"), pairs)

    swap = [(0, 1), (1, 0)]
    any_spec = pl.BlockSpec(memory_space=pl.ANY)
    if staged:
        sent = across(weight_old, doubling, 0)
    else:
        weights = lax.all_gather(weight_old, "dp", axis=0, tiled=True)

    tiles = D_OLD // LANES
    live_gain, inv_rms, *blocks = call(
        lambda *refs: token_kernel(rels, rep_count, cap, *refs),
        8,
        (
            shape((tiles, LANES), F32),
            shape((tokens, LANES), F32),
            *[pltpu.VMEM((dp_count // parts, part, LANES), F32)] * parts,
            *[shape((rep_count - 1, dp_count // parts, part, LANES), BF16)] * parts,
        ),
        [SMEM_SPEC] + [VMEM_SPEC] * 2 + [any_spec] + [VMEM_SPEC],
        [
            pltpu.VMEM((tiles, LANES), F32),
            pltpu.VMEM((tokens, D_OLD), BF16),
            pltpu.VMEM((D_OLD + cap, LANES), F32),
            pltpu.VMEM((D_OLD + cap, LANES), F32),
            pltpu.SemaphoreType.DMA((6,)),
        ],
        old_bounds,
        units,
        gain,
        hidden_old,
        cotangent,
    )
    owns, others = blocks[:parts], blocks[parts:]
    def indices(src):
        return call(
            lambda *refs: index_kernel(dp_count, cap, slots, table_rows, *refs),
            0,
            (
                pltpu.VMEM((table_rows * LANES, cap), BF16),
                pltpu.VMEM((1, table_rows * LANES), F32),
                pltpu.VMEM((1, cap), F32),
                shape((1,), jnp.int32),
            ),
            [SMEM_SPEC] * 3 + [VMEM_SPEC],
            [pltpu.VMEM((table_rows * LANES, LANES), jnp.int32), pltpu.VMEM((D_OLD // LANES + 8, LANES), F32)],
            old_bounds,
            new_bounds,
            src,
            gain,
        )

    project_shape = shape((tokens, LANES), BF16)
    dense = [pltpu.VMEM((D_OLD + cap, LANES), F32), pltpu.VMEM((tokens, D_OLD), BF16)]
    if staged:
        half = dp_count // 2
        mine = lax.axis_index("rep") * part
        with jax.named_scope("weights_1"):
            send, sent = lax.optimization_barrier((others[1][0], sent))
            gathered = [lax.dynamic_slice_in_dim(block, mine, part)[None] for block in (weight_old, sent)]
            gathered = jnp.concatenate(gathered)
            sent = across(gathered, doubling, 1)
        with jax.named_scope("pair_exchange"):
            pair, gathered = lax.optimization_barrier((lax.ppermute(send, "rep", swap), gathered))
            high = (owns[1] + pair.astype(F32)).astype(BF16)
            low = owns[0] + lax.ppermute(others[0][0], "rep", swap).astype(F32)
        for stage in range(bits - 1):
            with jax.named_scope(f"gradient_{stage + 1}"):
                came = across(high, halving, stage)
            if stage < bits - 2:
                with jax.named_scope(f"weights_{stage + 2}"):
                    gathered = jnp.concatenate([gathered, sent])
                    sent = across(gathered, doubling, stage + 2)
            if stage == 0:
                gathered, late_src = lax.optimization_barrier((gathered, source_map))
                chosen, keep, own_gain, offset = indices(late_src)
            if stage != 1:
                came, sent = lax.optimization_barrier((came, sent))
            if stage == 0:
                came, chosen = lax.optimization_barrier((came, chosen))
            came = came.astype(F32)
            half = half // 2
            low, high = low[:half] + came[:half], (low[half:] + came[half:]).astype(BF16)
        with jax.named_scope("gradient_last"):
            came = across(high, halving, bits - 1)
        with jax.named_scope("weights_pair"):
            pieces = [gathered, sent]
            pieces += [lax.ppermute(piece, "rep", swap) for piece in pieces]
        came, *pieces[:3] = lax.optimization_barrier((came, *pieces[:3]))
        reduced = [resident(low), resident(came)]
        projected = call(
            lambda *refs: project_kernel(dp_count, doubling, cap, *refs),
            6,
            project_shape,
            [SMEM_SPEC] + [VMEM_SPEC] * 3 + [any_spec] * 4,
            dense + [pltpu.VMEM((2, dp_count, part, LANES), BF16), pltpu.SemaphoreType.DMA((4,))],
            old_bounds,
            hidden_old,
            inv_rms,
            live_gain,
            *pieces,
        )
    else:
        chip = owns[0]
        for away in range(1, rep_count):
            ring = [(r, (r + away) % rep_count) for r in range(rep_count)]
            chip = chip + lax.ppermute(others[0][away - 1], "rep", ring).astype(F32)
        blocks = lax.all_to_all(chip.astype(BF16), "dp", split_axis=0, concat_axis=0)
        grad_part = jnp.sum(blocks.astype(F32), axis=0)
        reduced = [lax.all_gather(grad_part, "rep", axis=0, tiled=True)]
        chosen, keep, own_gain, offset = indices(source_map)
        projected = call(
            lambda *refs: project_gathered_kernel(dp_count, cap, *refs),
            6,
            project_shape,
            [SMEM_SPEC] + [VMEM_SPEC] * 4,
            dense,
            old_bounds,
            hidden_old,
            inv_rms,
            live_gain,
            weights,
        )

    message = (1 if staged else 2) * slots + 2 * table_rows
    message = (message + 7) // 8 * 8
    packed = call(
        lambda *refs: pack_kernel(dp_count, slots, table_rows, staged, *refs),
        3,
        pltpu.VMEM((dp_count, message, LANES), BF16),
        [VMEM_SPEC] * (6 + len(reduced)),
        [],
        *[resident(value) for value in (chosen, keep, own_gain)],
        *reduced,
        *[resident(value) for value in (weight_old, moment_first, moment_second)],
    )
    packed, late_units = lax.optimization_barrier((packed, units))
    places, tables = call(
        lambda *refs: place_kernel(dp_count, slots, table_rows, *refs),
        2,
        (pltpu.VMEM((1, D_NEW), jnp.int32), pltpu.VMEM((2 * dp_count * table_rows, D_NEW), BF16)),
        [SMEM_SPEC] * 2 + [VMEM_SPEC],
        [],
        old_bounds,
        new_bounds,
        late_units,
    )
    moved = [lax.all_to_all(packed, "dp", split_axis=0, concat_axis=0)]
    if staged:
        arrived, projected, places = lax.optimization_barrier((moved[0], projected, places))
        moved = [arrived, lax.ppermute(arrived, "rep", swap)]
        moved = [resident(value) for value in moved]
    rows = shape((new_cap, LANES), F32)
    gain_grad, first_next, second_next, adam_step = call(
        lambda *refs: finish_kernel(dp_count, slots, table_rows, staged, *refs),
        4,
        (shape((1, D_NEW), F32), rows, rows, rows),
        [SMEM_SPEC] * 2 + [VMEM_SPEC] * (2 + len(moved)),
        [pltpu.VMEM((dp_count * slots, LANES), F32)] * 2
        + [pltpu.VMEM((dp_count * table_rows, LANES), F32)],
        new_bounds,
        offset,
        resident(places),
        resident(tables),
        *moved,
    )
    return (projected, gain_grad.reshape(D_NEW), first_next, second_next, adam_step)


def solution(mesh):
    placed = (
        P(("dp", "rep"), None),
        P(("dp", "rep"), None),
        P(),
        P(),
        P(),
        P(),
        P("dp", None),
        P("dp", None),
        P("dp", None),
    )
    return jax.shard_map(
        on_device,
        mesh=mesh,
        in_specs=placed,
        out_specs=(P(("dp", "rep"), None), P(), P("dp", None), P("dp", None), P("dp", None)),
        check_vma=False,
    )
```

```python
import jax
import jax.numpy as jnp
from jax import lax
from jax.experimental import pallas as pl
from jax.experimental.pallas import tpu as pltpu
from jax.sharding import PartitionSpec as P

D_OLD = 6144
D_NEW = 8192
LANES = 128
BYTES_PER_US = 3_000_000
VMEM_LIMIT = 56 * 1024 * 1024
F32 = jnp.float32
BF16 = jnp.bfloat16

SMEM_SPEC = pl.BlockSpec(memory_space=pltpu.SMEM)
VMEM_SPEC = pl.BlockSpec(memory_space=pltpu.VMEM)


def dot(left, right, contract):
    return lax.dot_general(left, right, ((contract[:1], contract[1:]), ((), ())), preferred_element_type=F32)


def one_hot(rows, values):
    lanes = values.shape[1]
    match = lax.broadcasted_iota(jnp.int32, (rows, lanes), 0).astype(BF16) == values.astype(BF16)
    return jnp.where(match, jnp.ones((), BF16), jnp.zeros((), BF16))


def split(value):
    high = value.astype(BF16)
    return high, (value - high.astype(F32)).astype(BF16)


def normed_tile(tile, hidden, inv_rms, gain):
    stream = hidden[:, tile * LANES : (tile + 1) * LANES].astype(F32)
    return ((stream * inv_rms) * gain[tile : tile + 1, :]).astype(BF16)


def lower_half(rows):
    return lax.broadcasted_iota(jnp.int32, (rows, LANES), 1) < LANES // 2


def token_kernel(rels, rep_count, cap, ob, src, gain, hidden_hbm, cot, live_gain, inv_out, *rest):
    *blocks, hist, hidden, own_grads, other_grads, sem = rest
    owns, others = blocks[: len(blocks) // 2], blocks[len(blocks) // 2 :]
    pieces = sem.shape[0]
    width = D_OLD // pieces
    copies = []
    for piece in range(pieces):
        columns = pl.ds(piece * width, width)
        copies.append(pltpu.make_async_copy(hidden_hbm.at[:, columns], hidden.at[:, columns], sem.at[piece]))
    for copy in copies:
        copy.start()
    me = lax.axis_index("dp")
    rep = lax.axis_index("rep")
    tiles = D_OLD // LANES
    tokens = hidden.shape[0]
    step = 1024
    total = jnp.zeros((tiles, LANES), F32)
    for at in range(0, D_NEW, step):
        units = src[:, at : at + step]
        total = total + dot(one_hot(tiles, units >> 7), one_hot(LANES, units & 127), (1, 1))
    hist[...] = total
    live_gain[...] = jnp.where(total > 0.5, gain[...], 0.0)
    squares = jnp.zeros((tokens, LANES), F32)
    for tile in range(tiles):
        if tile * LANES % width == 0:
            copies[tile * LANES // width].wait()
        stream = hidden[:, tile * LANES : (tile + 1) * LANES].astype(F32)
        squares = squares + stream * stream * hist[tile : tile + 1, :]
    inv_rms = lax.rsqrt(jnp.sum(squares, axis=1, keepdims=True) / D_NEW + 1e-05)
    inv_out[...] = jnp.broadcast_to(inv_rms, (tokens, LANES))
    staged = len(rels) > 1
    columns = cot[...]
    if staged:
        lower = lower_half(tokens)
        columns = columns.astype(F32)
        turned = pltpu.roll(columns, LANES // 2, 1)
        left, right = jnp.where(lower, columns, turned), jnp.where(lower, turned, columns)
        sides = [jnp.where(rep == 0, left, right), jnp.where(rep == 0, right, left)]
        columns = jnp.concatenate(sides, axis=1).astype(BF16)
    for tile in range(tiles):
        at = tile * LANES
        result = dot(normed_tile(tile, hidden, inv_rms, live_gain), columns, (0, 0))
        own_grads[at : at + LANES, :] = result[:, :LANES]
        if staged:
            other_grads[at : at + LANES, :] = result[:, LANES:]
    own_grads[D_OLD:, :] = jnp.zeros((cap, LANES), F32)
    other_grads[D_OLD:, :] = jnp.zeros((cap, LANES), F32)
    dp_count = len(rels[0])
    half = dp_count // len(owns)
    part = cap // rep_count
    for at in range(dp_count):
        if staged:
            first = ob[holder_at(rels, rep, me, at)]
            owns[at // half][at % half] = packed_rows(own_grads, first, part)
            first = ob[holder_at(rels, 1 - rep, me, at)]
            others[at // half][0, at % half] = packed_rows(other_grads, first, part).astype(BF16)
        else:
            first = ob[at]
            owns[0][at] = own_grads[pl.ds(first + rep * part, part), :]
            for away in range(1, rep_count):
                mate = (rep + away) % rep_count
                others[0][away - 1, at] = own_grads[pl.ds(first + mate * part, part), :].astype(BF16)


def packed_rows(grads, first, part):
    return jnp.where(lower_half(part), grads[pl.ds(first, part), :], grads[pl.ds(first + part, part), :])


def holder_at(rels, rep, me, at):
    return me ^ jnp.where(rep == 0, rels[0][at], rels[1][at])


def fill_normed(x, hidden, inv_rms, gain):
    for tile in range(D_OLD // LANES):
        x[:, tile * LANES : (tile + 1) * LANES] = normed_tile(tile, hidden, inv_rms[...], gain)


def project_kernel(dp_count, orders, cap, ob, hidden, inv_rms, gain, *rest):
    *pieces, out, dense, x, blocks, sems = rest
    me = lax.axis_index("dp")
    rep = lax.axis_index("rep")
    part = cap // 2
    half = dp_count // 2
    copies = []
    for at, piece in enumerate(pieces):
        side = rep if at < 2 else 1 - rep
        place = blocks.at[side, pl.ds((at % 2) * half, half)]
        copies.append(pltpu.make_async_copy(piece, place, sems.at[at]))
    for copy in copies:
        copy.start()
    fill_normed(x, hidden, inv_rms, gain)
    for copy in copies:
        copy.wait()
    for p in range(dp_count):
        away = me ^ p
        for side, order in enumerate(orders):
            at = sum(((away >> bit) & 1) << s for s, bit in enumerate(order))
            dense[pl.ds(ob[p] + side * part, part), :] = blocks[side, at].astype(F32)
    out[...] = dot(x[...], dense[0:D_OLD, :].astype(BF16), (1, 0)).astype(BF16)


def project_gathered_kernel(dp_count, cap, ob, hidden, inv_rms, gain, weights, out, dense, x):
    fill_normed(x, hidden, inv_rms, gain)
    for p in range(dp_count):
        dense[pl.ds(ob[p], cap), :] = weights[p * cap : (p + 1) * cap, :].astype(F32)
    out[...] = dot(x[...], dense[0:D_OLD, :].astype(BF16), (1, 0)).astype(BF16)


def offset_of(src, ob, nb, q, dp_count):
    first = src[nb[q]]
    holder = jnp.int32(0)
    for p in range(1, dp_count):
        holder = holder + (ob[p] <= first).astype(jnp.int32)
    return holder


def index_kernel(dp_count, cap, slots, table_rows, ob, nb, src, gain, chosen, keep, own_gain, offset, rows, gains):
    me = lax.axis_index("dp")
    mine = ob[me]
    groups = cap // LANES
    offset[0] = offset_of(src, ob, nb, me, dp_count)
    rows[...] = jnp.full(rows.shape, -1, jnp.int32)
    for q in range(dp_count):
        start = nb[q] + ((me - offset_of(src, ob, nb, q, dp_count)) & (dp_count - 1))
        end = nb[q + 1]
        for k in range(slots):
            unit = start + dp_count * k
            row = jnp.where(unit < end, src[jnp.minimum(unit, D_NEW - 1)] - mine, -1)
            rows[q * slots + k : q * slots + k + 1, :] = jnp.full((1, LANES), row, jnp.int32)
    lanes = lax.broadcasted_iota(jnp.int32, rows.shape, 1)
    for g in range(groups):
        chosen[:, g * LANES : (g + 1) * LANES] = jnp.where(rows[...] == lanes + g * LANES, 1.0, 0.0).astype(BF16)
    gains[0 : gain.shape[0], :] = gain[...]
    gains[gain.shape[0] :, :] = jnp.ones((gains.shape[0] - gain.shape[0], LANES), F32)
    gain_rows = gains[pl.ds(mine >> 7, groups + 1), :]
    shift = mine & 127
    rolled = pltpu.roll(gain_rows, (LANES - shift) & 127, 1)
    lane_row = lax.broadcasted_iota(jnp.int32, (groups, LANES), 1)
    inverse = 1.0 / jnp.where(lane_row < LANES - shift, rolled[:groups], rolled[1:])
    for g in range(groups):
        own_gain[:, g * LANES : (g + 1) * LANES] = inverse[g : g + 1]
    same = dot(chosen[...], chosen[...], (1, 1))
    earlier = lax.broadcasted_iota(jnp.int32, same.shape, 0) < lax.broadcasted_iota(jnp.int32, same.shape, 1)
    repeated = jnp.max(jnp.where(earlier, same, 0.0), axis=0, keepdims=True)
    keep[...] = jnp.where(repeated < 0.5, 1.0, 0.0)


def place_kernel(dp_count, slots, table_rows, ob, nb, units, places, tables):
    step = 1024
    for first in range(0, D_NEW, step):
        source = units[:, first : first + step]
        position = first + lax.broadcasted_iota(jnp.int32, (1, step), 1)
        holder = jnp.zeros((1, step), jnp.int32)
        dest = jnp.zeros((1, step), jnp.int32)
        begin = jnp.zeros((1, step), jnp.int32)
        for p in range(1, dp_count):
            holder = holder + jnp.where(source >= ob[p], 1, 0)
            past = position >= nb[p]
            dest = jnp.where(past, p, dest)
            begin = jnp.where(past, nb[p], begin)
        rank = (position - begin) >> (dp_count.bit_length() - 1)
        place = holder * (table_rows * LANES) + dest * slots + rank
        places[:, first : first + step] = place & 127
        spread = one_hot(dp_count * table_rows, place >> 7)
        tables[:, first : first + step] = jnp.concatenate([spread, spread], axis=0)


def pack_kernel(dp_count, slots, table_rows, staged, chosen, keep, own_gain, *rest):
    *reduced, weight_in, first_in, second_in, out = rest
    pairs = dp_count * slots
    rows = weight_in.shape[0]
    weight, first, second = weight_in[...].astype(F32), first_in[...], second_in[...]
    if staged:
        turn = LANES // 2
        lower = lower_half(rows)
        grad = reduced[0][0] + reduced[1][0].astype(F32)
        grad = jnp.concatenate([grad, pltpu.roll(grad, turn, 1)], axis=0)
        left = lax.axis_index("rep") == 0
        weight, first, second = [
            jnp.where(left, value, pltpu.roll(value, turn, 1)) for value in (weight, first, second)
        ]
        product = jnp.where(lower, weight * grad, 0.0)
    else:
        grad = reduced[0][...]
        product = weight * grad
    high, low = split(product)
    ones = jnp.ones((8, LANES), BF16)
    column = (dot(ones, high, (1, 1)) + dot(ones, low, (1, 1))) * own_gain[...]
    picked = dot(jnp.concatenate(split(column), axis=0), chosen[...], (1, 1))
    table = []
    for part in (picked[0:1], picked[8:9]):
        part = part * keep[...]
        table += [part[:, r * LANES : (r + 1) * LANES] for r in range(table_rows)]
    updated = [0.9 * first + 0.1 * grad, 0.95 * second + 0.05 * grad * grad]
    if staged:
        updated = [jnp.where(lower, updated[0], pltpu.roll(updated[1], turn, 1))]
    filled = len(updated) * slots
    spare = out.shape[1] - filled - 2 * table_rows
    table = jnp.concatenate(table + [jnp.zeros((spare, LANES), F32)], axis=0).astype(BF16)
    picked = chosen[0:pairs]
    for at, value in enumerate(updated):
        moved = dot(picked, value.astype(BF16), (1, 0)).astype(BF16).reshape(dp_count, slots, LANES)
        out[:, at * slots : (at + 1) * slots, :] = moved
    for q in range(dp_count):
        out[q, filled:, :] = table


def finish_kernel(dp_count, slots, table_rows, staged, nb, offset_in, places, tables, *rest):
    arrived, rest = (rest[:2], rest[2:]) if staged else (rest[:1], rest[1:])
    gain_grad, first, second, adam, ones, twos, table = rest
    me = lax.axis_index("dp")
    offset = offset_in[0]
    groups = 1 if staged else 2
    pages = [(moved, 0) for moved in arrived] if staged else [(arrived[0], 0), (arrived[0], slots)]
    for i in range(dp_count):
        p = (i + offset) & (dp_count - 1)
        strided = pl.ds(i, slots, stride=dp_count)
        for (moved, at), rows in zip(pages, (ones, twos)):
            rows[strided, :] = moved[p, at : at + slots, :].astype(F32)
    cap = first.shape[0]
    live = lax.broadcasted_iota(jnp.int32, (cap, LANES), 0) < nb[me + 1] - nb[me]
    one, two = ones[0:cap, :], twos[0:cap, :]
    if staged:
        left = lax.axis_index("rep") == 0
        lower = lower_half(cap)
        one, two = jnp.where(left, one, two), jnp.where(left, two, one)
        turn = LANES // 2
        one, two = (
            jnp.where(lower, one, pltpu.roll(two, turn, 1)),
            jnp.where(lower, pltpu.roll(one, turn, 1), two),
        )
    first_next = jnp.where(live, one, 0.0)
    second_next = jnp.where(live, two, 0.0)
    first[...] = first_next
    second[...] = second_next
    adam[...] = first_next / (jnp.sqrt(second_next) + 1e-08)
    at = groups * slots
    for p in range(dp_count):
        here = p * table_rows
        terms = [
            moved[p, at + r : at + r + table_rows, :].astype(F32) for moved in arrived for r in (0, table_rows)
        ]
        table[here : here + table_rows, :] = sum(terms[1:], terms[0])
    high, low = split(table[...])
    values = jnp.concatenate([high.astype(F32), low.astype(F32)], axis=0).T.astype(BF16)
    step = 1024
    for start in range(0, D_NEW, step):
        spread = dot(values, tables[:, start : start + step], (1, 0))
        mask = lax.broadcasted_iota(jnp.int32, (LANES, step), 0) == places[:, start : start + step]
        value = jnp.where(mask, spread, 0.0)
        gain_grad[:, start : start + step] = jnp.sum(value, axis=0, keepdims=True)


def resident(value):
    return pltpu.with_memory_space_constraint(value, pltpu.VMEM)


def call(kernel, micros, out_shape, specs, scratch, *args):
    scalars = jax.ShapeDtypeStruct((1,), jnp.int32)
    out_specs = jax.tree.map(lambda out: SMEM_SPEC if out == scalars else VMEM_SPEC, out_shape)
    return pl.pallas_call(
        kernel,
        out_shape=out_shape,
        in_specs=specs,
        out_specs=out_specs,
        scratch_shapes=scratch,
        cost_estimate=pl.CostEstimate(flops=0, transcendentals=0, bytes_accessed=micros * BYTES_PER_US),
        compiler_params=pltpu.CompilerParams(vmem_limit_bytes=VMEM_LIMIT),
    )(*args)


def on_device(
    hidden_old,
    cotangent,
    gain_old,
    old_bounds,
    new_bounds,
    source_map,
    weight_old,
    moment_first,
    moment_second,
):
    dp_count = lax.axis_size("dp")
    rep_count = lax.axis_size("rep")
    cap = weight_old.shape[0]
    mean = D_NEW // dp_count
    new_cap = mean + mean // 4
    slots = (new_cap + dp_count - 1) // dp_count
    table_rows = (dp_count * slots + LANES - 1) // LANES
    tokens = hidden_old.shape[0]
    part = cap // rep_count
    shape = jax.ShapeDtypeStruct

    units = source_map.reshape(1, D_NEW)
    gain = gain_old.reshape(D_OLD // LANES, LANES)
    staged = rep_count == 2 and dp_count >= 8
    bits = dp_count.bit_length() - 1
    line = list(range(bits - 1))
    ends = [line[:1] + line[-1:], line[-1:] + line[:1]]
    halving = [pair + line[1:-1] + [bits - 1] for pair in ends]
    doubling = [[bits - 1] + line, [bits - 1] + line[::-1]]
    if staged:
        rels = [
            [sum(((at >> (bits - 1 - s)) & 1) << bit for s, bit in enumerate(order)) for at in range(dp_count)]
            for order in halving
        ]
        parts = 2
    else:
        rels = [list(range(dp_count))]
        parts = 1

    def across(value, orders, stage):
        pairs = [
            (dp * rep_count + rep, (dp ^ (1 << orders[rep][stage])) * rep_count + rep)
            for dp in range(dp_count)
            for rep in range(rep_count)
        ]
        return lax.ppermute(value, ("dp", "rep"), pairs)

    swap = [(0, 1), (1, 0)]
    any_spec = pl.BlockSpec(memory_space=pl.ANY)
    if staged:
        sent = across(weight_old, doubling, 0)
    else:
        weights = lax.all_gather(weight_old, "dp", axis=0, tiled=True)

    tiles = D_OLD // LANES
    live_gain, inv_rms, *blocks = call(
        lambda *refs: token_kernel(rels, rep_count, cap, *refs),
        8,
        (
            shape((tiles, LANES), F32),
            shape((tokens, LANES), F32),
            *[pltpu.VMEM((dp_count // parts, part, LANES), F32)] * parts,
            *[shape((rep_count - 1, dp_count // parts, part, LANES), BF16)] * parts,
        ),
        [SMEM_SPEC] + [VMEM_SPEC] * 2 + [any_spec] + [VMEM_SPEC],
        [
            pltpu.VMEM((tiles, LANES), F32),
            pltpu.VMEM((tokens, D_OLD), BF16),
            pltpu.VMEM((D_OLD + cap, LANES), F32),
            pltpu.VMEM((D_OLD + cap, LANES), F32),
            pltpu.SemaphoreType.DMA((6,)),
        ],
        old_bounds,
        units,
        gain,
        hidden_old,
        cotangent,
    )
    owns, others = blocks[:parts], blocks[parts:]
    def indices(src):
        return call(
            lambda *refs: index_kernel(dp_count, cap, slots, table_rows, *refs),
            0,
            (
                pltpu.VMEM((table_rows * LANES, cap), BF16),
                pltpu.VMEM((1, table_rows * LANES), F32),
                pltpu.VMEM((1, cap), F32),
                shape((1,), jnp.int32),
            ),
            [SMEM_SPEC] * 3 + [VMEM_SPEC],
            [pltpu.VMEM((table_rows * LANES, LANES), jnp.int32), pltpu.VMEM((D_OLD // LANES + 8, LANES), F32)],
            old_bounds,
            new_bounds,
            src,
            gain,
        )

    project_shape = shape((tokens, LANES), BF16)
    dense = [pltpu.VMEM((D_OLD + cap, LANES), F32), pltpu.VMEM((tokens, D_OLD), BF16)]
    if staged:
        half = dp_count // 2
        mine = lax.axis_index("rep") * part
        with jax.named_scope("weights_1"):
            send, sent = lax.optimization_barrier((others[1][0], sent))
            gathered = [lax.dynamic_slice_in_dim(block, mine, part)[None] for block in (weight_old, sent)]
            gathered = jnp.concatenate(gathered)
            sent = across(gathered, doubling, 1)
        with jax.named_scope("pair_exchange"):
            pair, gathered = lax.optimization_barrier((lax.ppermute(send, "rep", swap), gathered))
            high = (owns[1] + pair.astype(F32)).astype(BF16)
            low = owns[0] + lax.ppermute(others[0][0], "rep", swap).astype(F32)
        for stage in range(bits - 1):
            with jax.named_scope(f"gradient_{stage + 1}"):
                came = across(high, halving, stage)
            if stage < bits - 2:
                with jax.named_scope(f"weights_{stage + 2}"):
                    gathered = jnp.concatenate([gathered, sent])
                    sent = across(gathered, doubling, stage + 2)
            if stage == 0:
                gathered, late_src = lax.optimization_barrier((gathered, source_map))
                chosen, keep, own_gain, offset = indices(late_src)
            if stage == 0:
                came, sent = lax.optimization_barrier((came, sent))
            if stage == 0:
                came, chosen = lax.optimization_barrier((came, chosen))
            came = came.astype(F32)
            half = half // 2
            low, high = low[:half] + came[:half], (low[half:] + came[half:]).astype(BF16)
        with jax.named_scope("gradient_last"):
            came = across(high, halving, bits - 1)
        with jax.named_scope("weights_pair"):
            from_mate = lax.ppermute(gathered, "rep", swap)
        came, gathered, from_mate = lax.optimization_barrier((came, gathered, from_mate))
        reduced = [resident(low), resident(came)]
    else:
        chip = owns[0]
        for away in range(1, rep_count):
            ring = [(r, (r + away) % rep_count) for r in range(rep_count)]
            chip = chip + lax.ppermute(others[0][away - 1], "rep", ring).astype(F32)
        blocks = lax.all_to_all(chip.astype(BF16), "dp", split_axis=0, concat_axis=0)
        grad_part = jnp.sum(blocks.astype(F32), axis=0)
        reduced = [lax.all_gather(grad_part, "rep", axis=0, tiled=True)]
        chosen, keep, own_gain, offset = indices(source_map)
        projected = call(
            lambda *refs: project_gathered_kernel(dp_count, cap, *refs),
            6,
            project_shape,
            [SMEM_SPEC] + [VMEM_SPEC] * 4,
            dense,
            old_bounds,
            hidden_old,
            inv_rms,
            live_gain,
            weights,
        )

    message = (1 if staged else 2) * slots + 2 * table_rows
    message = (message + 7) // 8 * 8
    packed = call(
        lambda *refs: pack_kernel(dp_count, slots, table_rows, staged, *refs),
        3,
        pltpu.VMEM((dp_count, message, LANES), BF16),
        [VMEM_SPEC] * (6 + len(reduced)),
        [],
        *[resident(value) for value in (chosen, keep, own_gain)],
        *reduced,
        *[resident(value) for value in (weight_old, moment_first, moment_second)],
    )
    if staged:
        packed, late = lax.optimization_barrier((packed, sent))
        projected = call(
            lambda *refs: project_kernel(dp_count, doubling, cap, *refs),
            6,
            project_shape,
            [SMEM_SPEC] + [VMEM_SPEC] * 3 + [any_spec] * 4,
            dense + [pltpu.VMEM((2, dp_count, part, LANES), BF16), pltpu.SemaphoreType.DMA((4,))],
            old_bounds,
            hidden_old,
            inv_rms,
            live_gain,
            gathered,
            late,
            from_mate,
            lax.ppermute(late, "rep", swap),
        )
    packed, late_units = lax.optimization_barrier((packed, units))
    places, tables = call(
        lambda *refs: place_kernel(dp_count, slots, table_rows, *refs),
        2,
        (pltpu.VMEM((1, D_NEW), jnp.int32), pltpu.VMEM((2 * dp_count * table_rows, D_NEW), BF16)),
        [SMEM_SPEC] * 2 + [VMEM_SPEC],
        [],
        old_bounds,
        new_bounds,
        late_units,
    )
    moved = [lax.all_to_all(packed, "dp", split_axis=0, concat_axis=0)]
    if staged:
        arrived, projected, places = lax.optimization_barrier((moved[0], projected, places))
        moved = [arrived, lax.ppermute(arrived, "rep", swap)]
        moved = [resident(value) for value in moved]
    rows = shape((new_cap, LANES), F32)
    gain_grad, first_next, second_next, adam_step = call(
        lambda *refs: finish_kernel(dp_count, slots, table_rows, staged, *refs),
        4,
        (shape((1, D_NEW), F32), rows, rows, rows),
        [SMEM_SPEC] * 2 + [VMEM_SPEC] * (2 + len(moved)),
        [pltpu.VMEM((dp_count * slots, LANES), F32)] * 2
        + [pltpu.VMEM((dp_count * table_rows, LANES), F32)],
        new_bounds,
        offset,
        resident(places),
        resident(tables),
        *moved,
    )
    return (projected, gain_grad.reshape(D_NEW), first_next, second_next, adam_step)


def solution(mesh):
    placed = (
        P(("dp", "rep"), None),
        P(("dp", "rep"), None),
        P(),
        P(),
        P(),
        P(),
        P("dp", None),
        P("dp", None),
        P("dp", None),
    )
    return jax.shard_map(
        on_device,
        mesh=mesh,
        in_specs=placed,
        out_specs=(P(("dp", "rep"), None), P(), P("dp", None), P("dp", None), P("dp", None)),
        check_vma=False,
    )
```
